32 devices in a mesh: bx: 8 (over z, x), by: 4 (over y, core).
Axes of the slice: x: 2, y: 2, z: 4, core: 2. Of those that a mesh axis runs over, the one named last changes fastest.
Arguments:
- thermal_anomaly: float32 [8, 256, 1024], P(None, 'bx', 'by'), may hold values from -6 to 6
- saltiness_anomaly: float32 [8, 256, 1024], P(None, 'bx', 'by'), may hold values from -6 to 6
- speed_across_first_face: float32 [8, 256, 1024], P(None, 'bx', 'by'), may hold values from -4 to 4
- speed_across_second_face: float32 [8, 256, 1024], P(None, 'bx', 'by'), may hold values from -4 to 4
- isoline_incline_first: float32 [8, 256, 1024], P(None, 'bx', 'by'), may hold values from -0.6 to 0.6
- isoline_incline_second: float32 [8, 256, 1024], P(None, 'bx', 'by'), may hold values from -0.6 to 0.6
- top_boundary_source: float32 [2, 256, 1024], P(None, 'bx', 'by'), may hold values from -6 to 6
- wet_layer_number: int32 [256, 1024], P('bx', 'by'), may hold values from 0 to 8, as said below
- operator_main_entry: float32 [256, 1024], P(('bx', 'by')), may hold values from 0.05 to 1
Outputs:
- temperature_new: float32 [8, 256, 1024], P(None, 'bx', 'by')
- salinity_new: float32 [8, 256, 1024], P(None, 'bx', 'by')
- surface_pressure: float32 [256, 1024], P(('bx', 'by'))
The draws below stay inside these ranges and needn't reach their ends.
Inputs may be any that keep to these rules, and one draw needn't show every extreme that they name: wet_layer_number is 0 on every column of a land block (aligned blocks of 64 x 64 columns); other columns hold any count.
All inputs are finite; a program needn't handle non-finite values.
Results may differ from the reference program's by a relative error of at most 0.0003.
Values sent between devices are 32-bit elements; how exact they have to be, the bound alone decides.
No kernel may reach another device: no remote copies, remote signals or barrier semaphores. Data moves between devices by JAX's collectives and lax.ppermute only.
A program may use at most 64 MiB of HBM per device.

```python
import math
import jax
import jax.numpy as jnp
from jax import lax

VERTICAL_LAYERS = 8
BS = 64
ITERS = 3
MESH_WIDTH_FIRST = 256
MESH_WIDTH_SECOND = 1024


def draw_wet_layer_number(key, part):
    block_key = jax.random.fold_in(key, 11)
    depth_key = jax.random.fold_in(key, 23)
    blocks = jax.random.randint(block_key, (MESH_WIDTH_FIRST // BS, MESH_WIDTH_SECOND // BS), 0, 4)
    block_wet = (blocks > 0).astype(jnp.int32)
    cell_wet = jnp.repeat(jnp.repeat(block_wet, BS, axis=0), BS, axis=1)
    depth = jax.random.randint(depth_key, (MESH_WIDTH_FIRST, MESH_WIDTH_SECOND), 0, VERTICAL_LAYERS + 1)
    return (depth * cell_wet).astype(jnp.int32)


def shard_levels(rng, shape, split, low, high):
    factor_of, own = 1.0, jax.random.fold_in(rng, 6)
    for dim, parts in split:
        draws = jnp.exp(jax.random.uniform(jax.random.fold_in(own, dim), (parts,), jnp.float32, low / len(split), high / len(split)))
        factor_of = factor_of * jnp.repeat(draws, shape[dim] // parts).reshape([-1 if axis == dim else 1 for axis in range(len(shape))])
    return factor_of


def scatter_about(rng, dims, spread, limit, split=(), held_as=jnp.bfloat16):
    values = jax.random.normal(rng, dims, jnp.float32) * spread
    if len(split) > 0:
        values = shard_levels(rng, dims, split, -0.22, 0.18) * values
    return jnp.clip(values, min=-limit, max=limit).astype(held_as)


def setup_inputs(seed: int = 0) -> dict:
    seeds = jax.random.split(jax.random.key(seed), 10)
    return {
        "thermal_anomaly": scatter_about(seeds[0], (VERTICAL_LAYERS, MESH_WIDTH_FIRST, MESH_WIDTH_SECOND), 1.0, 6.0, ((1, 8), (2, 4)), jnp.float32),
        "saltiness_anomaly": scatter_about(seeds[1], (VERTICAL_LAYERS, MESH_WIDTH_FIRST, MESH_WIDTH_SECOND), 1.0, 6.0, ((1, 8), (2, 4)), jnp.float32),
        "speed_across_first_face": scatter_about(seeds[2], (VERTICAL_LAYERS, MESH_WIDTH_FIRST, MESH_WIDTH_SECOND), 0.3, 4.0, ((1, 8), (2, 4)), jnp.float32),
        "speed_across_second_face": scatter_about(seeds[3], (VERTICAL_LAYERS, MESH_WIDTH_FIRST, MESH_WIDTH_SECOND), 0.3, 4.0, ((1, 8), (2, 4)), jnp.float32),
        "isoline_incline_first": jnp.clip(jax.random.uniform(seeds[4], (VERTICAL_LAYERS, MESH_WIDTH_FIRST, MESH_WIDTH_SECOND), jnp.float32, -0.6, 0.6) * shard_levels(seeds[4], (VERTICAL_LAYERS, MESH_WIDTH_FIRST, MESH_WIDTH_SECOND), ((1, 8), (2, 4)), -0.4, 0.0), -0.6, 0.6),
        "isoline_incline_second": jnp.clip(jax.random.uniform(seeds[5], (VERTICAL_LAYERS, MESH_WIDTH_FIRST, MESH_WIDTH_SECOND), jnp.float32, -0.6, 0.6) * shard_levels(seeds[5], (VERTICAL_LAYERS, MESH_WIDTH_FIRST, MESH_WIDTH_SECOND), ((1, 8), (2, 4)), -0.4, 0.0), -0.6, 0.6),
        "top_boundary_source": scatter_about(seeds[6], (2, MESH_WIDTH_FIRST, MESH_WIDTH_SECOND), 0.5, 6.0, ((1, 8), (2, 4)), jnp.float32),
        "wet_layer_number": draw_wet_layer_number(jax.random.fold_in(seeds[9], 71), 0),
        "operator_main_entry": jnp.clip(jnp.exp(math.log(1.0) - 2.9957323 * jax.random.uniform(seeds[8], (MESH_WIDTH_FIRST, MESH_WIDTH_SECOND), jnp.float32) ** shard_levels(seeds[8], (MESH_WIDTH_FIRST, MESH_WIDTH_SECOND), ((0, 32),), -0.2, 0.2)), 0.05, 1.0),
    }


def tendency(cp, up, vp, sxp, syp, wetp):
    cp = cp * wetp
    mask_x = wetp[:, :-1, 1:-1] * wetp[:, 1:, 1:-1]
    left = cp[:, :, :-1, 1:-1]
    right = cp[:, :, 1:, 1:-1]
    cross_x = 0.25 * (cp[:, :, :-1, 2:] - cp[:, :, :-1, :-2] + (cp[:, :, 1:, 2:] - cp[:, :, 1:, :-2]))
    flux_x = mask_x * (up[:, :-1, 1:-1] * 0.5 * (left + right) - 0.15 * (right - left + sxp[:, :-1, 1:-1] * cross_x))
    mask_y = wetp[:, 1:-1, :-1] * wetp[:, 1:-1, 1:]
    lower = cp[:, :, 1:-1, :-1]
    upper = cp[:, :, 1:-1, 1:]
    cross_y = 0.25 * (cp[:, :, 2:, :-1] - cp[:, :, :-2, :-1] + (cp[:, :, 2:, 1:] - cp[:, :, :-2, 1:]))
    flux_y = mask_y * (vp[:, 1:-1, :-1] * 0.5 * (lower + upper) - 0.15 * (upper - lower + syp[:, 1:-1, :-1] * cross_y))
    wet_in = wetp[:, 1:-1, 1:-1]
    return wet_in * (-(flux_x[:, :, 1:] - flux_x[:, :, :-1]) - (flux_y[:, :, :, 1:] - flux_y[:, :, :, :-1]))

def column_step(carried_quantities, tend, wet, top_boundary_source):
    layer_tally = wet.shape[0]
    star = (carried_quantities + tend) * wet
    star = star.at[:, 0].add(top_boundary_source * wet[0])
    density = -0.2 * star[0] + 0.8 * star[1]
    strat = density[1:] - density[:-1]
    couple = (0.05 + 1.0 / (1.0 + 10.0 * jnp.maximum(strat, 0.0))) * wet[:-1] * wet[1:]
    zero_plane = jnp.zeros_like(wet[:1])
    above = jnp.concatenate([zero_plane, couple], 0)
    below = jnp.concatenate([couple, zero_plane], 0)
    diag = 1.0 + above + below
    primes = []
    rights = []
    for level in range(layer_tally):
        if level == 0:
            pivot = diag[0]
            rhs = star[:, 0]
        else:
            pivot = diag[level] - above[level] * primes[-1]
            rhs = star[:, level] + above[level] * rights[-1]
        primes.append(-below[level] / pivot * -1.0)
        rights.append(rhs / pivot)
    solved = [None] * layer_tally
    solved[layer_tally - 1] = rights[layer_tally - 1]
    for level in range(layer_tally - 2, -1, -1):
        solved[level] = rights[level] + primes[level] * solved[level + 1]
    fresh = jnp.stack(solved, 1) * wet
    density_new = -0.2 * fresh[0] + 0.8 * fresh[1]
    forcing = 4.0 / math.sqrt(layer_tally) * lax.optimization_barrier(jnp.sum(wet * density_new, 0))
    return (fresh, forcing)

def nine_point(padded, operator_main_entry):
    centre = padded[1:-1, 1:-1]
    edges = padded[:-2, 1:-1] + padded[2:, 1:-1] + padded[1:-1, :-2] + padded[1:-1, 2:]
    corners = padded[:-2, :-2] + padded[:-2, 2:] + padded[2:, :-2] + padded[2:, 2:]
    return (6.0 + operator_main_entry) * centre - edges - 0.5 * corners

def reference(thermal_anomaly, saltiness_anomaly, speed_across_first_face, speed_across_second_face, isoline_incline_first, isoline_incline_second, top_boundary_source, wet_layer_number, operator_main_entry):
    layer_tally = thermal_anomaly.shape[0]
    level_ids = jnp.arange(layer_tally, dtype=jnp.int32)[:, None, None]
    wet = (level_ids < wet_layer_number[None]).astype(jnp.float32)
    pad_three = ((0, 0), (1, 1), (1, 1))
    carried_quantities = jnp.stack([thermal_anomaly, saltiness_anomaly], 0)
    tracers_p = jnp.pad(carried_quantities, ((0, 0), (0, 0), (1, 1), (1, 1)))
    tend = tendency(tracers_p, jnp.pad(speed_across_first_face, pad_three), jnp.pad(speed_across_second_face, pad_three), jnp.pad(isoline_incline_first, pad_three), jnp.pad(isoline_incline_second, pad_three), jnp.pad(wet, pad_three))
    fresh, forcing = column_step(carried_quantities, tend, wet, top_boundary_source)
    solution = jnp.zeros_like(forcing)
    resid = forcing
    direction = forcing
    norm_now = jnp.sum(resid * resid)
    for step in range(ITERS):
        image = nine_point(jnp.pad(direction, 1), operator_main_entry)
        alpha = norm_now / jnp.sum(direction * image)
        solution = solution + alpha * direction
        resid = resid - alpha * image
        norm_next = jnp.sum(resid * resid)
        direction = resid + norm_next / norm_now * direction
        norm_now = norm_next
    return (fresh[0], fresh[1], solution)
```

```python
import math

import jax
import jax.numpy as jnp
from jax import lax
from jax.sharding import PartitionSpec as P

ITERS = 3
CENTRE = 4.5
SCALE = 4.5
DEEP = ITERS + 1


def with_halo(cells, sides):
    for axis, dim, width in sides:
        count = lax.axis_size(axis)
        ends = count - 1
        head = lax.slice_in_dim(cells, 0, width, axis=dim)
        tail = lax.slice_in_dim(cells, cells.shape[dim] - width, cells.shape[dim], axis=dim)
        cells = jnp.concatenate(
            [
                lax.ppermute(tail, axis, [(i, (i + 1) % count) for i in range(ends)]),
                cells,
                lax.ppermute(head, axis, [((i + 1) % count, i) for i in range(ends)]),
            ],
            axis=dim,
        )
    return cells


def tendency(cp, up, vp, sxp, syp, wetp):
    cp = cp * wetp
    mask_x = wetp[:, :-1, 1:-1] * wetp[:, 1:, 1:-1]
    left = cp[:, :, :-1, 1:-1]
    right = cp[:, :, 1:, 1:-1]
    cross_x = 0.25 * (
        cp[:, :, :-1, 2:] - cp[:, :, :-1, :-2] + (cp[:, :, 1:, 2:] - cp[:, :, 1:, :-2])
    )
    flux_x = mask_x * (
        up[:, :-1, 1:-1] * 0.5 * (left + right)
        - 0.15 * (right - left + sxp[:, :-1, 1:-1] * cross_x)
    )
    mask_y = wetp[:, 1:-1, :-1] * wetp[:, 1:-1, 1:]
    lower = cp[:, :, 1:-1, :-1]
    upper = cp[:, :, 1:-1, 1:]
    cross_y = 0.25 * (
        cp[:, :, 2:, :-1] - cp[:, :, :-2, :-1] + (cp[:, :, 2:, 1:] - cp[:, :, :-2, 1:])
    )
    flux_y = mask_y * (
        vp[:, 1:-1, :-1] * 0.5 * (lower + upper)
        - 0.15 * (upper - lower + syp[:, 1:-1, :-1] * cross_y)
    )
    wet_in = wetp[:, 1:-1, 1:-1]
    return wet_in * (
        -(flux_x[:, :, 1:] - flux_x[:, :, :-1]) - (flux_y[:, :, :, 1:] - flux_y[:, :, :, :-1])
    )


def column_step(carried_quantities, tend, wet, top_boundary_source):
    layer_tally = wet.shape[0]
    star = (carried_quantities + tend) * wet
    star = star.at[:, 0].add(top_boundary_source * wet[0])
    density = -0.2 * star[0] + 0.8 * star[1]
    strat = density[1:] - density[:-1]
    couple = (0.05 + 1.0 / (1.0 + 10.0 * jnp.maximum(strat, 0.0))) * wet[:-1] * wet[1:]
    zero_plane = jnp.zeros_like(wet[:1])
    above = jnp.concatenate([zero_plane, couple], 0)
    below = jnp.concatenate([couple, zero_plane], 0)
    diag = 1.0 + above + below
    primes = []
    rights = []
    for level in range(layer_tally):
        if level == 0:
            pivot = diag[0]
            rhs = star[:, 0]
        else:
            pivot = diag[level] - above[level] * primes[-1]
            rhs = star[:, level] + above[level] * rights[-1]
        primes.append(-below[level] / pivot * -1.0)
        rights.append(rhs / pivot)
    solved = [None] * layer_tally
    solved[layer_tally - 1] = rights[layer_tally - 1]
    for level in range(layer_tally - 2, -1, -1):
        solved[level] = rights[level] + primes[level] * solved[level + 1]
    fresh = jnp.stack(solved, 1) * wet
    density_new = -0.2 * fresh[0] + 0.8 * fresh[1]
    forcing = 4.0 / math.sqrt(layer_tally) * jnp.sum(wet * density_new, 0)
    return (fresh, forcing)


def shifted_operator(padded, main):
    centre = padded[1:-1, 1:-1]
    edges = padded[:-2, 1:-1] + padded[2:, 1:-1] + padded[1:-1, :-2] + padded[1:-1, 2:]
    corners = padded[:-2, :-2] + padded[:-2, 2:] + padded[2:, :-2] + padded[2:, 2:]
    return ((6.0 - CENTRE + main) * centre - edges - 0.5 * corners) * (1.0 / SCALE)


def coefficients(moments):
    def inner(a, b):
        return sum(x * y * moments[i + j] for i, x in enumerate(a) for j, y in enumerate(b))

    one = jnp.ones_like(moments[0])
    resid = [one]
    direction = [one]
    total = [jnp.zeros_like(one)] * ITERS
    norm_now = inner(resid, resid)
    for step in range(ITERS):
        image = [jnp.zeros_like(one)] * (len(direction) + 1)
        for i, x in enumerate(direction):
            image[i] = image[i] + CENTRE * x
            image[i + 1] = image[i + 1] + SCALE * x
        alpha = norm_now / inner(direction, image)
        for i, x in enumerate(direction):
            total[i] = total[i] + alpha * x
        if step + 1 < ITERS:
            resid = [r - alpha * q for r, q in zip(resid + [jnp.zeros_like(one)], image)]
            norm_next = inner(resid, resid)
            beta = norm_next / norm_now
            direction = [r + beta * p for r, p in zip(resid, direction + [jnp.zeros_like(one)])]
            norm_now = norm_next
    return total


def local(
    thermal_anomaly,
    saltiness_anomaly,
    speed_across_first_face,
    speed_across_second_face,
    isoline_incline_first,
    isoline_incline_second,
    top_boundary_source,
    wet_layer_number,
    operator_main_entry,
):
    layers, rows, columns = thermal_anomaly.shape
    across = lax.axis_size("by")
    along = lax.axis_size("bx")
    own_bx = lax.axis_index("bx")
    own_by = lax.axis_index("by")
    strip = rows // across
    planes = jnp.concatenate(
        [
            thermal_anomaly,
            saltiness_anomaly,
            speed_across_first_face,
            speed_across_second_face,
            isoline_incline_first,
            isoline_incline_second,
            top_boundary_source,
            wet_layer_number.astype(jnp.float32)[None],
        ],
        0,
    )
    padded = with_halo(planes, (("by", 2, 1), ("bx", 1, DEEP)))
    tracers_p = padded[: 2 * layers].reshape((2, layers) + padded.shape[1:])
    east_p = padded[2 * layers : 3 * layers]
    north_p = padded[3 * layers : 4 * layers]
    slope_ep = padded[4 * layers : 5 * layers]
    slope_np = padded[5 * layers : 6 * layers]
    source_p = padded[6 * layers : 6 * layers + 2]
    depth_p = padded[6 * layers + 2]
    level_ids = jnp.arange(layers, dtype=jnp.float32)[:, None, None]
    wet_p = (level_ids < depth_p[None]).astype(jnp.float32)
    tend = tendency(tracers_p, east_p, north_p, slope_ep, slope_np, wet_p)
    fresh, forcing = column_step(
        tracers_p[:, :, 1:-1, 1:-1], tend, wet_p[:, 1:-1, 1:-1], source_p[:, 1:-1, 1:-1]
    )
    fresh = fresh[:, :, ITERS:-ITERS]

    tall = strip + 2 * ITERS
    everyone = range(across)
    blocks = jnp.zeros((across, tall, columns), jnp.float32)
    for hop in everyone:
        peer = (own_by + hop) % across
        block = lax.dynamic_slice(forcing, (peer * strip, 0), (tall, columns))
        if hop:
            block = lax.ppermute(block, "by", [(i, (i + hop) % across) for i in everyone])
        origin = (own_by - hop) % across
        blocks = lax.dynamic_update_slice(blocks, block[None], (origin, 0, 0))
    field = jnp.concatenate([blocks[i] for i in everyone], 1)

    ends = across * along - 1
    names = ("bx", "by")
    wide = ITERS - 1
    main = jnp.concatenate(
        [
            lax.ppermute(operator_main_entry[-wide:], names, [(i, i + 1) for i in range(ends)]),
            operator_main_entry,
            lax.ppermute(operator_main_entry[:wide], names, [(i + 1, i) for i in range(ends)]),
        ],
        0,
    )
    first = (own_bx * across + own_by) * strip
    basis = [field[ITERS:-ITERS]]
    for step in range(ITERS):
        trim = step
        here = main[trim : main.shape[0] - trim]
        field = shifted_operator(jnp.pad(field, ((0, 0), (1, 1))), here)
        reach = wide - step
        line = first - reach + jnp.arange(field.shape[0])[:, None]
        field = jnp.where((line >= 0) & (line < along * across * strip), field, 0.0)
        basis.append(field[reach : field.shape[0] - reach])
    pairs = [(0, 0), (0, 1), (1, 1), (1, 2), (2, 2), (2, 3)]
    sums = jnp.stack([jnp.sum(basis[i] * basis[j]) for i, j in pairs])
    row = jnp.pad(sums, (0, 128 - len(pairs)))
    gathered = lax.all_to_all(
        jnp.broadcast_to(row[None, None], (ends + 1, 1, 128)), names, 0, 0, tiled=True
    )
    moments = jnp.sum(gathered, (0, 1))
    total = coefficients([moments[i] for i in range(len(pairs))])
    pressure = total[0] * basis[0] + total[1] * basis[1] + total[2] * basis[2]
    return (fresh[0], fresh[1], pressure)


def solution(mesh):
    tile = P(None, "bx", "by")
    rows = P(("bx", "by"), None)
    return jax.shard_map(
        local,
        mesh=mesh,
        in_specs=(tile,) * 7 + (P("bx", "by"), rows),
        out_specs=(tile, tile, rows),
        check_vma=False,
    )
```

```python
import functools
import math

import jax
import jax.numpy as jnp
from jax import lax
from jax.experimental import pallas as pl
from jax.experimental.pallas import tpu as pltpu
from jax.sharding import PartitionSpec as P

ITERS = 3
CENTRE = 4.5
SCALE = 4.5
DEEP = ITERS + 1
SUB = 8
LANE = 128
PAIRS = ((0, 0), (0, 1), (1, 1), (1, 2), (2, 2), (2, 3))


def iota(shape, dim):
    return lax.broadcasted_iota(jnp.int32, shape, dim)


def below(x):
    return pltpu.roll(x, x.shape[0] - 1, 0)


def above(x):
    return pltpu.roll(x, 1, 0)


def left_by(x, lanes):
    return pltpu.roll(x, x.shape[1] - lanes, 1)


def pack_edges(lo_t, lo_s, lo_d, hi_t, hi_s, hi_v, hi_y, hi_d, first_ref, even_ref, odd_ref):
    layers, rows, _ = lo_t.shape
    cells = 2 * layers
    lane = iota((rows, LANE), 1)

    def put(total, where, column):
        return jnp.where(where, column, total)

    first = jnp.zeros((rows, LANE), jnp.float32)
    last = jnp.zeros((rows, LANE), jnp.float32)
    edge = LANE - 1
    for k in range(layers):
        first = put(first, lane == k, lo_t[k][:, 0:1])
        first = put(first, lane == layers + k, lo_s[k][:, 0:1])
        last = put(last, lane == k, hi_t[k][:, edge:])
        last = put(last, lane == layers + k, hi_s[k][:, edge:])
        two = (lane == cells + k) | (lane == cells + layers + k)
        last = put(last, two, hi_v[k][:, edge:])
        two = (lane == 2 * cells + k) | (lane == 2 * cells + layers + k)
        last = put(last, two, hi_y[k][:, edge:])
    span = (lane >= 3 * cells) & (lane < 4 * cells)
    first = put(first, span, lo_d[:, 0:1].astype(jnp.float32))
    last = put(last, span, hi_d[:, edge:].astype(jnp.float32))
    first_ref[...] = first
    even = lax.axis_index("by") % 2 == 0
    even_ref[...] = jnp.where(even, last, first)
    odd_ref[...] = jnp.where(even, first, last)


def pack_rows(*refs):
    tops, bottoms, (even_ref, odd_ref) = refs[:8], refs[8:16], refs[16:]

    def flat(group):
        planes = []
        for ref in group[:7]:
            planes += [ref[k] for k in range(ref.shape[0])]
        planes.append(group[7][...].astype(jnp.float32))
        planes.append(planes[-1])
        return planes

    even = lax.axis_index("bx") % 2 == 0
    tops, bottoms = flat(tops), flat(bottoms)
    upper = iota(tops[0].shape, 0) < DEEP
    for q in range(len(tops) // 2):
        up = jnp.where(upper, tops[2 * q], pltpu.roll(tops[2 * q + 1], DEEP, 0))
        down = jnp.where(upper, pltpu.roll(bottoms[2 * q], DEEP, 0), bottoms[2 * q + 1])
        even_ref[q] = jnp.where(even, down, up)
        odd_ref[q] = jnp.where(even, up, down)


def join_edges(first_ref, from_even, from_odd, even_in, odd_in, edge_ref, even_ref, odd_ref):
    rows = first_ref.shape[0]
    half = LANE // 2
    even = lax.axis_index("by") % 2 == 0
    lane = iota((rows, LANE), 1)
    a, b = from_even[...], from_odd[...]
    left = jnp.where(even, b, a)
    right = jnp.where(even, a, b)
    left = jnp.where(lane < half, left, pltpu.roll(first_ref[...], half, 1))
    edge_ref[:, :LANE] = left
    edge_ref[:, LANE:] = right
    even = lax.axis_index("bx") % 2 == 0
    upper = iota((SUB, 2 * LANE), 0) < DEEP
    up = pltpu.roll(edge_ref[:SUB, :], DEEP, 0)
    down = edge_ref[rows - SUB :, :]
    even_ref[0] = jnp.where(upper, even_in[0], jnp.where(even, down, up))
    odd_ref[0] = jnp.where(upper, odd_in[0], jnp.where(even, up, down))


def tile_step(get, source, depth, edge, layers):
    rows, columns = depth.shape
    cells = 2 * layers
    lane = iota((rows, columns), 1)
    first, last = lane == 0, lane == columns - 1

    def after(x, fill):
        return jnp.where(last, fill, left_by(x, 1))

    def before(x, fill):
        return jnp.where(first, fill, pltpu.roll(x, 1, 1))

    level = (iota((rows, LANE), 1) % layers).astype(jnp.float32)
    left, right = edge[:, :LANE], edge[:, LANE:]
    wet_left = level < left_by(left, 3 * cells)
    wet_own = level < left_by(left, LANE // 2 + 3 * cells)
    wet_right = level < left_by(right, 3 * cells)
    cell_left = jnp.where(wet_left, left, 0.0)
    cell_own = jnp.where(wet_own, left_by(left, LANE // 2), 0.0)
    cell_right = jnp.where(wet_right, right, 0.0)
    slope_left = below(cell_left) - above(cell_left)
    slope_own = below(cell_own) - above(cell_own)
    slope_right = below(cell_right) - above(cell_right)
    flux_left = left_by(left, cells) * 0.5 * (cell_left + cell_own) - 0.15 * (
        cell_own - cell_left + left_by(left, 2 * cells) * 0.25 * (slope_left + slope_own)
    )
    flux_left = jnp.where(wet_left & wet_own, flux_left, 0.0)

    depth_right = right[:, 3 * cells : 3 * cells + 1]
    depth_east = jnp.minimum(depth, below(depth))
    depth_north = jnp.minimum(depth, after(depth, depth_right))
    stars = ([], [])
    for k in range(layers):
        wet = depth > k
        mask = depth_east > k
        half = 0.5 * get(2, k)
        e_here = jnp.where(mask, half + 0.15, 0.0)
        e_next = jnp.where(mask, half - 0.15, 0.0)
        e_cross = jnp.where(mask, 0.0375 * get(4, k), 0.0)
        mask = depth_north > k
        half = 0.5 * get(3, k)
        n_here = jnp.where(mask, half + 0.15, 0.0)
        n_next = jnp.where(mask, half - 0.15, 0.0)
        n_cross = jnp.where(mask, 0.0375 * get(5, k), 0.0)
        for t in range(2):
            one = slice(t * layers + k, t * layers + k + 1)
            cell = jnp.where(wet, get(t, k), 0.0)
            east, west = below(cell), above(cell)
            north = after(cell, cell_right[:, one])
            south = before(cell, cell_left[:, one])
            cross = north - south
            flux = e_here * cell + e_next * east - e_cross * (cross + below(cross))
            star = cell - (flux - above(flux))
            cross = east - west
            cross = cross + after(cross, slope_right[:, one])
            flux = n_here * cell + n_next * north - n_cross * cross
            star = star - (flux - before(flux, flux_left[:, one]))
            if k == 0:
                star = star + source[t]
            stars[t].append(jnp.where(wet, star, 0.0))
    primes, rights = [], ([], [])
    upper = None
    density = 0.8 * stars[1][0] - 0.2 * stars[0][0]
    for k in range(layers):
        if k + 1 < layers:
            deeper = 0.8 * stars[1][k + 1] - 0.2 * stars[0][k + 1]
            couple = 0.05 + 1.0 / (1.0 + 10.0 * jnp.maximum(deeper - density, 0.0))
            couple = jnp.where(depth > k + 1, couple, 0.0)
            density = deeper
        else:
            couple = None
        if k == 0:
            inverse = 1.0 / (1.0 + couple)
        elif couple is not None:
            inverse = 1.0 / (1.0 + upper + couple - upper * primes[-1])
        else:
            inverse = 1.0 / (1.0 + upper - upper * primes[-1])
        for t in range(2):
            value = stars[t][k]
            if k:
                value = value + upper * rights[t][-1]
            rights[t].append(value * inverse)
        if couple is not None:
            primes.append(couple * inverse)
        upper = couple
    fresh = ([None] * layers, [None] * layers)
    forcing = None
    solved = [rights[0][-1], rights[1][-1]]
    for k in range(layers - 1, -1, -1):
        wet = depth > k
        for t in range(2):
            if k < layers - 1:
                solved[t] = rights[t][k] + primes[k] * solved[t]
            fresh[t][k] = jnp.where(wet, solved[t], 0.0)
        part = 0.8 * fresh[1][k] - 0.2 * fresh[0][k]
        forcing = part if forcing is None else forcing + part
    return fresh[0], fresh[1], forcing * (4.0 / math.sqrt(layers))


def inner_tile(t, s, u, v, x, y, source, depth, edge, t_out, s_out, f_out):
    layers = t.shape[0]
    refs = (t, s, u, v, x, y)
    warm, salt, forcing = tile_step(
        lambda kind, k: refs[kind][k],
        [source[0], source[1]],
        depth[...].astype(jnp.float32),
        edge[...],
        layers,
    )
    for k in range(layers):
        t_out[k] = warm[k]
        s_out[k] = salt[k]
    f_out[...] = forcing


def rim_rows(across, even_out, odd_out, even_in, odd_in, t_old, s_old, f_old, *refs):
    t_new, s_new = refs[0], refs[1]
    sends, (field, blocks) = refs[2 : 2 + across], refs[2 + across :]
    layers = t_old.shape[0]
    rows = f_old.shape[0]
    strip = rows // across
    step = pl.program_id(0)
    top = step == 0
    even = lax.axis_index("bx") % 2 == 0
    use_odd = top == even
    shape = (SUB, f_old.shape[1])
    upper = iota(shape, 0) < DEEP
    planes = []
    for q in range(even_out.shape[0]):
        sent = jnp.where(use_odd, odd_out[q], even_out[q])
        came = jnp.where(use_odd, odd_in[q], even_in[q])
        low = jnp.where(top, came, sent)
        high = jnp.where(top, sent, came)
        planes.append(jnp.where(upper, low, pltpu.roll(high, DEEP, 0)))
        planes.append(jnp.where(upper, pltpu.roll(low, DEEP, 0), high))
    order = (0, 1, 2, 3, 4, 5)
    base = 6 * layers
    warm, salt, forcing = tile_step(
        lambda kind, k: planes[order[kind] * layers + k],
        [planes[base], planes[base + 1]],
        planes[base + 2],
        planes[base + 3],
        layers,
    )
    target = jnp.where(top, 0, SUB - 1)
    mine = iota(shape, 0) == target
    for k in range(layers):
        t_new[k] = jnp.where(mine, pltpu.roll(warm[k], DEEP, 0), t_old[k])
        s_new[k] = jnp.where(mine, pltpu.roll(salt[k], DEEP, 0), s_old[k])
    moved = pltpu.roll(forcing, DEEP, 0)

    @pl.when(top)
    def _():
        field[SUB : SUB + rows, :] = f_old[...]
        field[:SUB, :] = moved
        field[SUB : 2 * SUB, :] = jnp.where(mine, moved, f_old[:SUB, :])

    @pl.when(jnp.logical_not(top))
    def _():
        field[SUB + rows : 2 * SUB + rows, :] = moved
        field[rows : rows + SUB, :] = jnp.where(mine, moved, field[rows : rows + SUB, :])
        tall = blocks.shape[1]
        for peer in range(across):
            start = SUB - ITERS + peer * strip
            stop = min(start + tall, field.shape[0])
            blocks[peer, : stop - start, :] = field[start:stop, :]
        me = lax.axis_index("by")
        for hop in range(across):
            sends[hop][...] = blocks[hop_peer(me, hop, across)]


def hop_peer(me, hop, count):
    if count & (count - 1) == 0:
        return me ^ hop
    return (me + hop) % count


def hop_origin(me, hop, count):
    if count & (count - 1) == 0:
        return me ^ hop
    return (me + count - hop) % count


def powers(across, along, *refs):
    came = refs[:across]
    main_up, main_own, main_down = refs[across : across + 3]
    basis_ref, row_ref, field, main = refs[across + 3 :]
    strip, columns = main_own.shape
    width = columns // across
    tall = field.shape[0]
    me = lax.axis_index("by")
    for hop in range(across):
        origin = hop_origin(me, hop, across)
        field[:, pl.ds(pl.multiple_of(origin * width, LANE), width)] = came[hop][...]
    wide = ITERS - 1
    main[...] = jnp.zeros(main.shape, jnp.float32)
    main[ITERS - wide : ITERS, :] = main_up[...]
    main[ITERS : ITERS + strip, :] = main_own[...]
    main[ITERS + strip : ITERS + strip + wide, :] = main_down[...]
    shape = (tall, columns)
    lane = iota(shape, 1)
    line = (lax.axis_index("bx") * across + me) * strip - ITERS + iota(shape, 0)
    inside = (line >= 0) & (line < along * across * strip)
    first, last = lane == 0, lane == columns - 1
    centre = (main[...] + (6.0 - CENTRE)) * (1.0 / SCALE)
    centre = jnp.where(inside, centre, 0.0)
    share = jnp.where(inside, -1.0 / SCALE, 0.0)
    now = field[...]
    own = [now[ITERS : ITERS + strip]]
    for _ in range(ITERS):
        beside = below(now) + above(now)
        spread = now + 0.5 * beside
        east = jnp.where(last, 0.0, left_by(spread, 1))
        west = jnp.where(first, 0.0, pltpu.roll(spread, 1, 1))
        now = centre * now + share * (beside + east + west)
        own.append(now[ITERS : ITERS + strip])
    for k in range(ITERS):
        basis_ref[k] = own[k]
    place = iota((1, LANE), 1)
    row = jnp.zeros((1, LANE), jnp.float32)
    for k, (i, j) in enumerate(PAIRS):
        part = jnp.sum(own[i] * own[j], axis=0, keepdims=True)
        row = jnp.where(place == k, jnp.sum(part, axis=1, keepdims=True), row)
    row_ref[...] = jnp.broadcast_to(row[None], row_ref.shape)


def coefficients(moments):
    def inner(a, b):
        return sum(x * y * moments[i + j] for i, x in enumerate(a) for j, y in enumerate(b))

    zero = jnp.zeros_like(moments[0])
    resid = [zero + 1.0]
    direction = [zero + 1.0]
    total = [zero] * ITERS
    norm_now = inner(resid, resid)
    for step in range(ITERS):
        image = [zero] * (len(direction) + 1)
        for i, x in enumerate(direction):
            image[i] = image[i] + CENTRE * x
            image[i + 1] = image[i + 1] + SCALE * x
        alpha = norm_now / inner(direction, image)
        for i, x in enumerate(direction):
            total[i] = total[i] + alpha * x
        if step + 1 < ITERS:
            resid = [r - alpha * q for r, q in zip(resid + [zero], image)]
            norm_next = inner(resid, resid)
            beta = norm_next / norm_now
            direction = [r + beta * p for r, p in zip(resid, direction + [zero])]
            norm_now = norm_next
    return total


def combine(rows_ref, basis_ref, out_ref):
    moments = jnp.sum(rows_ref[...], axis=0)
    total = coefficients([moments[:, k : k + 1] for k in range(len(PAIRS))])
    out_ref[...] = total[0] * basis_ref[0] + total[1] * basis_ref[1] + total[2] * basis_ref[2]


def shape_of(*dims):
    return jax.ShapeDtypeStruct(dims, jnp.float32)


def whole(x):
    return pl.BlockSpec(x.shape, lambda *_: (0,) * len(x.shape))


def block(shape, *index):
    return pl.BlockSpec(shape, lambda *_: index)


def pairs(count, start):
    both = [(i, i + 1) for i in range(start, count - 1, 2)]
    return both + [(b, a) for a, b in both]


def local(t, s, u, v, x, y, source, depth, main):
    layers, rows, columns = t.shape
    across, along = lax.axis_size("by"), lax.axis_size("bx")
    strip = rows // across
    params = pltpu.CompilerParams(vmem_limit_bytes=48 << 20)

    call = functools.partial(pl.pallas_call, compiler_params=params)

    stack = (layers, rows, LANE)
    end = columns // LANE - 1
    pack = shape_of(rows, LANE)
    lo, hi = block(stack, 0, 0, 0), block(stack, 0, 0, end)
    lo_d, hi_d = block((rows, LANE), 0, 0), block((rows, LANE), 0, end)
    first, even, odd = call(
        pack_edges,
        grid=(1,),
        in_specs=[lo, lo, lo_d, hi, hi, hi, hi, hi_d],
        out_specs=[whole(pack)] * 3,
        out_shape=[pack] * 3,
    )(t, s, depth, t, s, v, y, depth)
    from_even = lax.ppermute(even, "by", pairs(across, 0))
    from_odd = lax.ppermute(odd, "by", pairs(across, 1))

    fields = (t, s, u, v, x, y, source)
    deep = [(f.shape[0], SUB, columns) for f in fields]
    foot = rows // SUB - 1
    count = (6 * layers + 4) // 2
    rim = shape_of(count, SUB, columns)
    even, odd = call(
        pack_rows,
        grid=(1,),
        in_specs=[block(d, 0, 0, 0) for d in deep]
        + [block((SUB, columns), 0, 0)]
        + [block(d, 0, foot, 0) for d in deep]
        + [block((SUB, columns), foot, 0)],
        out_specs=[whole(rim)] * 2,
        out_shape=[rim] * 2,
    )(*fields, depth, *fields, depth)

    plane = shape_of(rows, columns)
    tail = block((1, SUB, columns), count - 1, 0, 0)
    edge, even, odd = call(
        join_edges,
        grid=(1,),
        in_specs=[whole(pack)] * 3 + [tail] * 2,
        out_specs=[block((rows, 2 * LANE), 0, 0), tail, tail],
        out_shape=[shape_of(rows, 2 * LANE), rim, rim],
        input_output_aliases={3: 1, 4: 2},
    )(first, from_even, from_odd, even, odd)
    odd_in = lax.ppermute(odd, "bx", pairs(along, 1))
    even_in = lax.ppermute(even, "bx", pairs(along, 0))

    cube = shape_of(layers, rows, columns)
    args = (*fields, depth, edge)
    warm, salt, forcing = call(
        inner_tile,
        grid=(1,),
        in_specs=[whole(a) for a in args],
        out_specs=[whole(cube), whole(cube), whole(plane)],
        out_shape=[cube, cube, plane],
    )(*args)

    ends = across * along - 1
    names = ("bx", "by")
    wide = ITERS - 1
    main_up = lax.ppermute(main[-wide:], names, [(i, i + 1) for i in range(ends)])
    main_down = lax.ppermute(main[:wide], names, [(i + 1, i) for i in range(ends)])

    tall = -(-(strip + 2 * ITERS) // SUB) * SUB
    part = shape_of(tall, columns)
    touched = pl.BlockSpec((layers, SUB, columns), lambda i: (0, i * foot, 0))
    warm, salt, *sends = call(
        functools.partial(rim_rows, across),
        grid=(2,),
        in_specs=[whole(rim)] * 4 + [touched, touched, whole(plane)],
        out_specs=[touched, touched] + [whole(part)] * across,
        out_shape=[cube, cube] + [part] * across,
        input_output_aliases={4: 0, 5: 1},
        scratch_shapes=[
            pltpu.VMEM((rows + 2 * SUB, columns), jnp.float32),
            pltpu.VMEM((across, tall, columns), jnp.float32),
        ],
    )(even, odd, even_in, odd_in, warm, salt, forcing)

    came = [sends[0]]
    for hop in range(1, across):
        route = [(i, hop_peer(i, hop, across)) for i in range(across)]
        came.append(lax.ppermute(sends[hop], "by", route))

    basis_shape = shape_of(ITERS, strip, columns * across)
    row_shape = shape_of(ends + 1, 1, LANE)
    args = (*came, main_up, main, main_down)
    basis, row = call(
        functools.partial(powers, across, along),
        grid=(1,),
        in_specs=[whole(a) for a in args],
        out_specs=[whole(basis_shape), whole(row_shape)],
        out_shape=[basis_shape, row_shape],
        scratch_shapes=[pltpu.VMEM((tall, columns * across), jnp.float32)] * 2,
    )(*args)
    gathered = lax.all_to_all(row, names, 0, 0, tiled=True)
    result = shape_of(strip, columns * across)
    pressure = call(
        combine,
        grid=(1,),
        in_specs=[whole(gathered), whole(basis)],
        out_specs=whole(result),
        out_shape=result,
    )(gathered, basis)
    return warm, salt, pressure


def solution(mesh):
    tile = P(None, "bx", "by")
    rows = P(("bx", "by"), None)
    return jax.shard_map(
        local,
        mesh=mesh,
        in_specs=(tile,) * 7 + (P("bx", "by"), rows),
        out_specs=(tile, tile, rows),
        check_vma=False,
    )
```

```python
import functools
import math

import jax
import jax.numpy as jnp
from jax import lax
from jax.experimental import pallas as pl
from jax.experimental.pallas import tpu as pltpu
from jax.sharding import PartitionSpec as P

ITERS = 3
CENTRE = 4.5
SCALE = 4.5
DEEP = ITERS + 1
SUB = 8
LANE = 128
PAIRS = ((0, 0), (0, 1), (1, 1), (1, 2), (2, 2), (2, 3))


def iota(shape, dim):
    return lax.broadcasted_iota(jnp.int32, shape, dim)


def below(x):
    return pltpu.roll(x, x.shape[0] - 1, 0)


def above(x):
    return pltpu.roll(x, 1, 0)


def left_by(x, lanes):
    return pltpu.roll(x, x.shape[1] - lanes, 1)


def pack_edges(t, s, v, y, depth, main, first_ref, even_ref, odd_ref, cubes, planes, lines, sems):
    layers, rows, columns = t.shape
    cells = 2 * layers
    wide = ITERS - 1
    head, tail = pl.ds(0, LANE), pl.ds(columns - LANE, LANE)
    moves = [(t.at[:, :, tail], cubes.at[0]), (s.at[:, :, tail], cubes.at[1])]
    moves += [(v.at[:, :, tail], cubes.at[2]), (y.at[:, :, tail], cubes.at[3])]
    moves += [(t.at[:, :, head], cubes.at[4]), (s.at[:, :, head], cubes.at[5])]
    moves += [(depth.at[:, tail], planes.at[0]), (depth.at[:, head], planes.at[1]), (main, lines)]
    copies = [pltpu.make_async_copy(a, b, sems.at[i]) for i, (a, b) in enumerate(moves)]
    for copy in copies:
        copy.start()
    for copy in copies:
        copy.wait()
    lane = iota((rows, LANE), 1)
    first = jnp.zeros((rows, LANE), jnp.float32)
    last = jnp.zeros((rows, LANE), jnp.float32)
    edge = LANE - 1
    for k in range(layers):
        first = jnp.where(lane == k, cubes[4, k][:, 0:1], first)
        first = jnp.where(lane == layers + k, cubes[5, k][:, 0:1], first)
        last = jnp.where(lane == k, cubes[0, k][:, edge:], last)
        last = jnp.where(lane == layers + k, cubes[1, k][:, edge:], last)
        two = (lane == cells + k) | (lane == cells + layers + k)
        last = jnp.where(two, cubes[2, k][:, edge:], last)
        two = (lane == 2 * cells + k) | (lane == 2 * cells + layers + k)
        last = jnp.where(two, cubes[3, k][:, edge:], last)
    span = (lane >= 3 * cells) & (lane < 4 * cells)
    first = jnp.where(span, planes[1][:, 0:1].astype(jnp.float32), first)
    last = jnp.where(span, planes[0][:, edge:].astype(jnp.float32), last)
    first_ref[...] = first
    even = lax.axis_index("by") % 2 == 0
    even_ref[:rows, :] = jnp.where(even, last, first)
    odd_ref[:rows, :] = jnp.where(even, first, last)
    strip = lines.shape[0]
    parts = lines.shape[1] // LANE
    for r in range(wide):
        for j in range(parts):
            here = slice(j * LANE, (j + 1) * LANE)
            up = lines[r : r + 1, here]
            down = lines[strip - wide + r : strip - wide + r + 1, here]
            at = rows + r * parts + j
            even_ref[at : at + 1, :] = jnp.where(even, down, up)
            odd_ref[at : at + 1, :] = jnp.where(even, up, down)


def pack_rows(across, *refs):
    tops, bottoms, (main, even_ref, odd_ref) = refs[:8], refs[8:16], refs[16:]

    def flat(group):
        planes = []
        for ref in group[:7]:
            planes += [ref[k] for k in range(ref.shape[0])]
        planes.append(group[7][...].astype(jnp.float32))
        planes.append(planes[-1])
        return planes

    even = lax.axis_index("bx") % 2 == 0
    tops, bottoms = flat(tops), flat(bottoms)
    upper = iota(tops[0].shape, 0) < DEEP
    count = len(tops) // 2
    for q in range(count):
        up = jnp.where(upper, tops[2 * q], pltpu.roll(tops[2 * q + 1], DEEP, 0))
        down = jnp.where(upper, pltpu.roll(bottoms[2 * q], DEEP, 0), bottoms[2 * q + 1])
        even_ref[q] = jnp.where(even, down, up)
        odd_ref[q] = jnp.where(even, up, down)
    wide = ITERS - 1
    strip = main.shape[0]
    width = tops[0].shape[1]
    for r in range(wide):
        for j in range(across):
            here = slice(j * width, (j + 1) * width)
            up = main[r : r + 1, here]
            down = main[strip - wide + r : strip - wide + r + 1, here]
            q, at = divmod(r * across + j, SUB)
            even_ref[count + q, at : at + 1, :] = jnp.where(even, down, up)
            odd_ref[count + q, at : at + 1, :] = jnp.where(even, up, down)


def join_edges(first_ref, from_even, from_odd, even_in, odd_in, edge_ref, even_ref, odd_ref):
    rows = first_ref.shape[0]
    half = LANE // 2
    even = lax.axis_index("by") % 2 == 0
    lane = iota((rows, LANE), 1)
    a, b = from_even[:rows, :], from_odd[:rows, :]
    left = jnp.where(even, b, a)
    right = jnp.where(even, a, b)
    left = jnp.where(lane < half, left, pltpu.roll(first_ref[...], half, 1))
    edge_ref[:, :LANE] = left
    edge_ref[:, LANE:] = right
    even = lax.axis_index("bx") % 2 == 0
    upper = iota((SUB, 2 * LANE), 0) < DEEP
    up = pltpu.roll(edge_ref[:SUB, :], DEEP, 0)
    down = edge_ref[rows - SUB :, :]
    even_ref[0] = jnp.where(upper, even_in[0], jnp.where(even, down, up))
    odd_ref[0] = jnp.where(upper, odd_in[0], jnp.where(even, up, down))


def tile_step(get, source, depth, edge, layers):
    rows, columns = depth.shape
    cells = 2 * layers
    lane = iota((rows, columns), 1)
    first, last = lane == 0, lane == columns - 1

    def after(x, fill):
        return jnp.where(last, fill, left_by(x, 1))

    def before(x, fill):
        return jnp.where(first, fill, pltpu.roll(x, 1, 1))

    level = (iota((rows, LANE), 1) % layers).astype(jnp.float32)
    left, right = edge[:, :LANE], edge[:, LANE:]
    wet_left = level < left_by(left, 3 * cells)
    wet_own = level < left_by(left, LANE // 2 + 3 * cells)
    wet_right = level < left_by(right, 3 * cells)
    cell_left = jnp.where(wet_left, left, 0.0)
    cell_own = jnp.where(wet_own, left_by(left, LANE // 2), 0.0)
    cell_right = jnp.where(wet_right, right, 0.0)
    slope_left = below(cell_left) - above(cell_left)
    slope_own = below(cell_own) - above(cell_own)
    slope_right = below(cell_right) - above(cell_right)
    flux_left = left_by(left, cells) * 0.5 * (cell_left + cell_own) - 0.15 * (
        cell_own - cell_left + left_by(left, 2 * cells) * 0.25 * (slope_left + slope_own)
    )
    flux_left = jnp.where(wet_left & wet_own, flux_left, 0.0)

    depth_right = right[:, 3 * cells : 3 * cells + 1]
    depth_east = jnp.minimum(depth, below(depth))
    depth_north = jnp.minimum(depth, after(depth, depth_right))
    stars = ([], [])
    for k in range(layers):
        wet = depth > k
        mask = depth_east > k
        half = 0.5 * get(2, k)
        e_here = jnp.where(mask, half + 0.15, 0.0)
        e_next = jnp.where(mask, half - 0.15, 0.0)
        e_cross = jnp.where(mask, 0.0375 * get(4, k), 0.0)
        mask = depth_north > k
        half = 0.5 * get(3, k)
        n_here = jnp.where(mask, half + 0.15, 0.0)
        n_next = jnp.where(mask, half - 0.15, 0.0)
        n_cross = jnp.where(mask, 0.0375 * get(5, k), 0.0)
        for t in range(2):
            one = slice(t * layers + k, t * layers + k + 1)
            cell = jnp.where(wet, get(t, k), 0.0)
            east, west = below(cell), above(cell)
            north = after(cell, cell_right[:, one])
            south = before(cell, cell_left[:, one])
            cross = north - south
            flux = e_here * cell + e_next * east - e_cross * (cross + below(cross))
            star = cell - (flux - above(flux))
            cross = east - west
            cross = cross + after(cross, slope_right[:, one])
            flux = n_here * cell + n_next * north - n_cross * cross
            star = star - (flux - before(flux, flux_left[:, one]))
            if k == 0:
                star = star + source[t]
            stars[t].append(jnp.where(wet, star, 0.0))
    primes, rights = [], ([], [])
    upper = None
    density = 0.8 * stars[1][0] - 0.2 * stars[0][0]
    for k in range(layers):
        if k + 1 < layers:
            deeper = 0.8 * stars[1][k + 1] - 0.2 * stars[0][k + 1]
            couple = 0.05 + 1.0 / (1.0 + 10.0 * jnp.maximum(deeper - density, 0.0))
            couple = jnp.where(depth > k + 1, couple, 0.0)
            density = deeper
        else:
            couple = None
        if k == 0:
            inverse = 1.0 / (1.0 + couple)
        elif couple is not None:
            inverse = 1.0 / (1.0 + upper + couple - upper * primes[-1])
        else:
            inverse = 1.0 / (1.0 + upper - upper * primes[-1])
        for t in range(2):
            value = stars[t][k]
            if k:
                value = value + upper * rights[t][-1]
            rights[t].append(value * inverse)
        if couple is not None:
            primes.append(couple * inverse)
        upper = couple
    fresh = ([None] * layers, [None] * layers)
    forcing = None
    solved = [rights[0][-1], rights[1][-1]]
    for k in range(layers - 1, -1, -1):
        wet = depth > k
        for t in range(2):
            if k < layers - 1:
                solved[t] = rights[t][k] + primes[k] * solved[t]
            fresh[t][k] = jnp.where(wet, solved[t], 0.0)
        part = 0.8 * fresh[1][k] - 0.2 * fresh[0][k]
        forcing = part if forcing is None else forcing + part
    return fresh[0], fresh[1], forcing * (4.0 / math.sqrt(layers))


def inner_tile(t, s, u, v, x, y, source, depth, edge, t_out, s_out, f_out):
    layers = t.shape[0]
    refs = (t, s, u, v, x, y)
    warm, salt, forcing = tile_step(
        lambda kind, k: refs[kind][k],
        [source[0], source[1]],
        depth[...].astype(jnp.float32),
        edge[...],
        layers,
    )
    for k in range(layers):
        t_out[k] = warm[k]
        s_out[k] = salt[k]
    f_out[...] = forcing


def rim_rows(across, even_out, odd_out, even_in, odd_in, f_old, *refs):
    layers = refs[0].shape[0]
    t_fix, s_fix = refs[:2]
    sends, (field, blocks) = refs[2 : 2 + across], refs[2 + across :]
    rows = f_old.shape[0]
    strip = rows // across
    even = lax.axis_index("bx") % 2 == 0
    me = lax.axis_index("by")
    shape = (SUB, f_old.shape[1])
    upper = iota(shape, 0) < DEEP
    planes = []
    base = 6 * layers
    for q in range(base // 2 + 2):
        sent_even, sent_odd, came_even, came_odd = even_out[q], odd_out[q], even_in[q], odd_in[q]
        ups = [jnp.where(even, came_odd, came_even), jnp.where(even, sent_odd, sent_even)]
        downs = [jnp.where(even, sent_even, sent_odd), jnp.where(even, came_even, came_odd)]
        one = [jnp.where(upper, low, pltpu.roll(high, DEEP, 0)) for low, high in (ups, downs)]
        two = [jnp.where(upper, pltpu.roll(low, DEEP, 0), high) for low, high in (ups, downs)]
        planes += [jnp.concatenate(one, 0), jnp.concatenate(two, 0)]
    warm, salt, forcing = tile_step(
        lambda kind, k: planes[kind * layers + k],
        [planes[base], planes[base + 1]],
        planes[base + 2],
        planes[base + 3],
        layers,
    )
    for fix, fresh in ((t_fix, warm), (s_fix, salt)):
        for k in range(layers):
            fix[k, :SUB, :] = pltpu.roll(fresh[k][:SUB], DEEP, 0)
            fix[k, SUB:, :] = pltpu.roll(fresh[k][SUB:], DEEP, 0)
    top = pltpu.roll(forcing[:SUB], DEEP, 0)
    bottom = pltpu.roll(forcing[SUB:], DEEP, 0)
    line = iota(shape, 0)
    field[:SUB, :] = top
    field[SUB : SUB + rows, :] = f_old[...]
    field[SUB : 2 * SUB, :] = jnp.where(line == 0, top, f_old[:SUB, :])
    field[rows : rows + SUB, :] = jnp.where(line == SUB - 1, bottom, field[rows : rows + SUB, :])
    field[SUB + rows : 2 * SUB + rows, :] = bottom
    extra = even_out.shape[0] - base // 2 - 2
    tall = blocks.shape[1] - extra * SUB
    for peer in range(across):
        start = SUB - ITERS + peer * strip
        stop = min(start + tall, field.shape[0])
        blocks[peer, : stop - start, :] = field[start:stop, :]
    use_even = even == (me == 0)
    for q in range(extra):
        relay = jnp.where(use_even, even_in[base // 2 + 2 + q], odd_in[base // 2 + 2 + q])
        for peer in range(across):
            blocks[peer, tall + q * SUB : tall + (q + 1) * SUB, :] = relay
    for hop in range(across):
        sends[hop][...] = blocks[hop_peer(me, hop, across)]


def patch(fix_t, fix_s, t_old, s_old, t_new, s_new):
    target = jnp.where(pl.program_id(0) == 0, 0, SUB - 1)
    mine = iota(t_old.shape, 1) == target
    t_new[...] = jnp.where(mine, fix_t[...], t_old[...])
    s_new[...] = jnp.where(mine, fix_s[...], s_old[...])


def hop_peer(me, hop, count):
    if count & (count - 1) == 0:
        return me ^ hop
    return (me + hop) % count


def hop_origin(me, hop, count):
    if count & (count - 1) == 0:
        return me ^ hop
    return (me + count - hop) % count


def powers(across, along, *refs):
    came = refs[:across]
    from_even, from_odd, main_own = refs[across : across + 3]
    basis_ref, row_ref, field, main = refs[across + 3 :]
    strip, columns = main_own.shape
    width = columns // across
    tall = field.shape[0]
    me = lax.axis_index("by")
    for hop in range(across):
        origin = hop_origin(me, hop, across)
        field[:, pl.ds(pl.multiple_of(origin * width, LANE), width)] = came[hop][:tall, :]
    wide = ITERS - 1
    main[...] = jnp.zeros(main.shape, jnp.float32)
    main[ITERS : ITERS + strip, :] = main_own[...]
    over, under = ITERS - wide, ITERS + strip
    even = me % 2 == 0
    parts = columns // LANE
    begin = from_even.shape[0] - wide * parts
    for r in range(wide):
        for j in range(parts):
            here = slice(j * LANE, (j + 1) * LANE)
            at = begin + r * parts + j
            a, b = from_even[at : at + 1, :], from_odd[at : at + 1, :]
            main[over + r : over + r + 1, here] = jnp.where(even, b, a)
            main[under + r : under + r + 1, here] = jnp.where(even, a, b)

    def relayed(start, mine, sender):
        hop = [h for h in range(across) if hop_origin(mine, h, across) == sender][0]

        @pl.when(me == mine)
        def _():
            for r in range(wide):
                for j in range(across):
                    at = tall + r * across + j
                    here = slice(j * width, (j + 1) * width)
                    main[start + r : start + r + 1, here] = came[hop][at : at + 1, :]

    relayed(over, 0, across - 1)
    relayed(under, across - 1, 0)
    shape = (tall, columns)
    lane = iota(shape, 1)
    line = (lax.axis_index("bx") * across + me) * strip - ITERS + iota(shape, 0)
    inside = (line >= 0) & (line < along * across * strip)
    first, last = lane == 0, lane == columns - 1
    centre = (main[...] + (6.0 - CENTRE)) * (1.0 / SCALE)
    centre = jnp.where(inside, centre, 0.0)
    share = jnp.where(inside, -1.0 / SCALE, 0.0)
    now = field[...]
    own = [now[ITERS : ITERS + strip]]
    for _ in range(ITERS):
        beside = below(now) + above(now)
        spread = now + 0.5 * beside
        east = jnp.where(last, 0.0, left_by(spread, 1))
        west = jnp.where(first, 0.0, pltpu.roll(spread, 1, 1))
        now = centre * now + share * (beside + east + west)
        own.append(now[ITERS : ITERS + strip])
    for k in range(ITERS):
        basis_ref[k] = own[k]
    place = iota((1, LANE), 1)
    row = jnp.zeros((1, LANE), jnp.float32)
    for k, (i, j) in enumerate(PAIRS):
        part = jnp.sum(own[i] * own[j], axis=0, keepdims=True)
        row = jnp.where(place == k, jnp.sum(part, axis=1, keepdims=True), row)
    row_ref[...] = jnp.broadcast_to(row[None], row_ref.shape)


def coefficients(moments):
    def inner(a, b):
        return sum(x * y * moments[i + j] for i, x in enumerate(a) for j, y in enumerate(b))

    zero = jnp.zeros_like(moments[0])
    resid = [zero + 1.0]
    direction = [zero + 1.0]
    total = [zero] * ITERS
    norm_now = inner(resid, resid)
    for step in range(ITERS):
        image = [zero] * (len(direction) + 1)
        for i, x in enumerate(direction):
            image[i] = image[i] + CENTRE * x
            image[i + 1] = image[i + 1] + SCALE * x
        alpha = norm_now / inner(direction, image)
        for i, x in enumerate(direction):
            total[i] = total[i] + alpha * x
        if step + 1 < ITERS:
            resid = [r - alpha * q for r, q in zip(resid + [zero], image)]
            norm_next = inner(resid, resid)
            beta = norm_next / norm_now
            direction = [r + beta * p for r, p in zip(resid, direction + [zero])]
            norm_now = norm_next
    return total


def combine(rows_ref, basis_ref, out_ref):
    moments = jnp.sum(rows_ref[...], axis=0)
    total = coefficients([moments[:, k : k + 1] for k in range(len(PAIRS))])
    out_ref[...] = total[0] * basis_ref[0] + total[1] * basis_ref[1] + total[2] * basis_ref[2]


def shape_of(*dims):
    return jax.ShapeDtypeStruct(dims, jnp.float32)


def whole(x):
    return pl.BlockSpec(x.shape, lambda *_: (0,) * len(x.shape))


def block(shape, *index):
    return pl.BlockSpec(shape, lambda *_: index)


def pairs(count, start):
    both = [(i, i + 1) for i in range(start, count - 1, 2)]
    return both + [(b, a) for a, b in both]


def local(t, s, u, v, x, y, source, depth, main):
    layers, rows, columns = t.shape
    across, along = lax.axis_size("by"), lax.axis_size("bx")
    strip = rows // across
    params = pltpu.CompilerParams(vmem_limit_bytes=48 << 20)

    call = functools.partial(pl.pallas_call, compiler_params=params)

    hbm = pl.BlockSpec(memory_space=pltpu.HBM)
    wide = ITERS - 1
    pack = shape_of(rows, LANE)
    more = shape_of(rows + wide * (columns * across // LANE), LANE)
    first, even, odd = call(
        pack_edges,
        grid=(1,),
        in_specs=[hbm] * 6,
        out_specs=[whole(pack), whole(more), whole(more)],
        out_shape=[pack, more, more],
        scratch_shapes=[
            pltpu.VMEM((6, layers, rows, LANE), jnp.float32),
            pltpu.VMEM((2, rows, LANE), jnp.int32),
            pltpu.VMEM(main.shape, jnp.float32),
            pltpu.SemaphoreType.DMA((9,)),
        ],
    )(*(pltpu.with_memory_space_constraint(a, pltpu.HBM) for a in (t, s, v, y, depth, main)))
    from_even = lax.ppermute(even, "by", pairs(across, 0))
    from_odd = lax.ppermute(odd, "by", pairs(across, 1))

    fields = (t, s, u, v, x, y, source)
    deep = [(f.shape[0], SUB, columns) for f in fields]
    foot = rows // SUB - 1
    count = (6 * layers + 4) // 2
    extra = -(-wide * across // SUB)
    rim = shape_of(count + extra, SUB, columns)
    even, odd = call(
        functools.partial(pack_rows, across),
        grid=(1,),
        in_specs=[block(d, 0, 0, 0) for d in deep]
        + [block((SUB, columns), 0, 0)]
        + [block(d, 0, foot, 0) for d in deep]
        + [block((SUB, columns), foot, 0), whole(main)],
        out_specs=[whole(rim)] * 2,
        out_shape=[rim] * 2,
    )(*fields, depth, *fields, depth, main)

    plane = shape_of(rows, columns)
    tail = block((1, SUB, columns), count - 1, 0, 0)
    edge, even, odd = call(
        join_edges,
        grid=(1,),
        in_specs=[whole(pack), whole(more), whole(more), tail, tail],
        out_specs=[block((rows, 2 * LANE), 0, 0), tail, tail],
        out_shape=[shape_of(rows, 2 * LANE), rim, rim],
        input_output_aliases={3: 1, 4: 2},
    )(first, from_even, from_odd, even, odd)
    odd_in = lax.ppermute(odd, "bx", pairs(along, 1))
    even_in = lax.ppermute(even, "bx", pairs(along, 0))

    cube = shape_of(layers, rows, columns)
    args = (*fields, depth, edge)
    warm, salt, forcing = call(
        inner_tile,
        grid=(1,),
        in_specs=[whole(a) for a in args],
        out_specs=[whole(cube), whole(cube), whole(plane)],
        out_shape=[cube, cube, plane],
    )(*args)

    tall = -(-(strip + 2 * ITERS) // SUB) * SUB
    part = shape_of(tall + extra * SUB, columns)
    fix = shape_of(layers, 2 * SUB, columns)
    fix_t, fix_s, *sends = call(
        functools.partial(rim_rows, across),
        grid=(1,),
        in_specs=[whole(rim)] * 4 + [whole(plane)],
        out_specs=[whole(fix)] * 2 + [whole(part)] * across,
        out_shape=[fix] * 2 + [part] * across,
        scratch_shapes=[
            pltpu.VMEM((rows + 2 * SUB, columns), jnp.float32),
            pltpu.VMEM((across,) + part.shape, jnp.float32),
        ],
    )(even, odd, even_in, odd_in, forcing)

    came = [sends[0]]
    for hop in range(1, across):
        route = [(i, hop_peer(i, hop, across)) for i in range(across)]
        came.append(lax.ppermute(sends[hop], "by", route))

    rimmed = pl.BlockSpec((layers, SUB, columns), lambda i: (0, i, 0))
    touched = pl.BlockSpec((layers, SUB, columns), lambda i: (0, i * foot, 0))
    warm, salt = call(
        patch,
        grid=(2,),
        in_specs=[rimmed, rimmed, touched, touched],
        out_specs=[touched, touched],
        out_shape=[cube, cube],
        input_output_aliases={2: 0, 3: 1},
    )(fix_t, fix_s, warm, salt)

    basis_shape = shape_of(ITERS, strip, columns * across)
    names = ("bx", "by")
    row_shape = shape_of(across * along, 1, LANE)
    args = (*came, from_even, from_odd, main)
    basis, row = call(
        functools.partial(powers, across, along),
        grid=(1,),
        in_specs=[whole(a) for a in args],
        out_specs=[whole(basis_shape), whole(row_shape)],
        out_shape=[basis_shape, row_shape],
        scratch_shapes=[pltpu.VMEM((tall, columns * across), jnp.float32)] * 2,
    )(*args)
    gathered = lax.all_to_all(row, names, 0, 0, tiled=True)
    result = shape_of(strip, columns * across)
    pressure = call(
        combine,
        grid=(1,),
        in_specs=[whole(gathered), whole(basis)],
        out_specs=whole(result),
        out_shape=result,
    )(gathered, basis)
    return warm, salt, pressure


def solution(mesh):
    tile = P(None, "bx", "by")
    rows = P(("bx", "by"), None)
    return jax.shard_map(
        local,
        mesh=mesh,
        in_specs=(tile,) * 7 + (P("bx", "by"), rows),
        out_specs=(tile, tile, rows),
        check_vma=False,
    )
```

```python
import functools
import math

import jax
import jax.numpy as jnp
from jax import lax
from jax.experimental import pallas as pl
from jax.experimental.pallas import tpu as pltpu
from jax.sharding import PartitionSpec as P

ITERS = 3
CENTRE = 4.5
SCALE = 4.5
DEEP = ITERS + 1
SUB = 8
LANE = 128
PAIRS = ((0, 0), (0, 1), (1, 1), (1, 2), (2, 2), (2, 3))


def iota(shape, dim):
    return lax.broadcasted_iota(jnp.int32, shape, dim)


def below(x):
    return pltpu.roll(x, x.shape[0] - 1, 0)


def above(x):
    return pltpu.roll(x, 1, 0)


def left_by(x, lanes):
    return pltpu.roll(x, x.shape[1] - lanes, 1)


def pack_edges(t, s, v, y, depth, main, first_ref, even_ref, odd_ref, cubes, planes, lines, sems):
    layers, rows, columns = t.shape
    cells = 2 * layers
    wide = ITERS - 1
    head, tail = pl.ds(0, LANE), pl.ds(columns - LANE, LANE)
    moves = []
    for low in range(0, layers, layers // 2):
        some = pl.ds(low, layers // 2)
        for i, (ref, where) in enumerate(((t, tail), (s, tail), (v, tail), (y, tail), (t, head), (s, head))):
            moves.append((ref.at[some, :, where], cubes.at[i, some]))
    moves += [(depth.at[:, tail], planes.at[0]), (depth.at[:, head], planes.at[1]), (main, lines)]
    copies = [pltpu.make_async_copy(a, b, sems.at[i]) for i, (a, b) in enumerate(moves)]
    for copy in copies:
        copy.start()
    for copy in copies:
        copy.wait()
    lane = iota((rows, LANE), 1)
    first = jnp.zeros((rows, LANE), jnp.float32)
    last = jnp.zeros((rows, LANE), jnp.float32)
    edge = LANE - 1
    for k in range(layers):
        first = jnp.where(lane == k, cubes[4, k][:, 0:1], first)
        first = jnp.where(lane == layers + k, cubes[5, k][:, 0:1], first)
        last = jnp.where(lane == k, cubes[0, k][:, edge:], last)
        last = jnp.where(lane == layers + k, cubes[1, k][:, edge:], last)
        two = (lane == cells + k) | (lane == cells + layers + k)
        last = jnp.where(two, cubes[2, k][:, edge:], last)
        two = (lane == 2 * cells + k) | (lane == 2 * cells + layers + k)
        last = jnp.where(two, cubes[3, k][:, edge:], last)
    span = (lane >= 3 * cells) & (lane < 4 * cells)
    first = jnp.where(span, planes[1][:, 0:1].astype(jnp.float32), first)
    last = jnp.where(span, planes[0][:, edge:].astype(jnp.float32), last)
    first_ref[...] = first
    even = lax.axis_index("by") % 2 == 0
    even_ref[:rows, :] = jnp.where(even, last, first)
    odd_ref[:rows, :] = jnp.where(even, first, last)
    strip = lines.shape[0]
    parts = lines.shape[1] // LANE
    for r in range(wide):
        for j in range(parts):
            here = slice(j * LANE, (j + 1) * LANE)
            up = lines[r : r + 1, here]
            down = lines[strip - wide + r : strip - wide + r + 1, here]
            at = rows + r * parts + j
            even_ref[at : at + 1, :] = jnp.where(even, down, up)
            odd_ref[at : at + 1, :] = jnp.where(even, up, down)


def gather_rows(t, s, u, v, x, y, source, depth, near, near_depth, sems):
    rows = t.shape[1]
    copies = []
    at = 0
    for ref in (t, s, u, v, x, y, source):
        for i, start in enumerate((0, rows - SUB)):
            planes = near.at[pl.ds(at, ref.shape[0]), pl.ds(i * SUB, SUB)]
            copies.append((ref.at[:, pl.ds(start, SUB)], planes))
        at += ref.shape[0]
    for i, start in enumerate((0, rows - SUB)):
        copies.append((depth.at[pl.ds(start, SUB)], near_depth.at[pl.ds(i * SUB, SUB)]))
    copies = [pltpu.make_async_copy(a, b, sems.at[i]) for i, (a, b) in enumerate(copies)]
    for copy in copies:
        copy.start()
    for copy in copies:
        copy.wait()


def pack_rows(across, first_ref, from_even, from_odd, near, near_depth, main, edge_ref, even_ref, odd_ref):
    rows, half = first_ref.shape[0], LANE // 2
    layers = near.shape[0] // 6
    even = lax.axis_index("by") % 2 == 0
    lane = iota((rows, LANE), 1)
    a, b = from_even[:rows, :], from_odd[:rows, :]
    left = jnp.where(even, b, a)
    right = jnp.where(even, a, b)
    left = jnp.where(lane < half, left, pltpu.roll(first_ref[...], half, 1))
    edge_ref[:, :LANE] = left
    edge_ref[:, LANE:] = right

    base = 6 * layers
    depth = near_depth[...].astype(jnp.float32)
    edge = jnp.concatenate([edge_ref[:SUB, :], edge_ref[rows - SUB :, :]], 0)
    _, _, forcing = tile_step(
        lambda kind, k: near[kind * layers + k], [near[base], near[base + 1]], depth, edge, layers
    )
    even = lax.axis_index("bx") % 2 == 0
    group = iota((SUB, edge.shape[1]), 0) // 2

    def put(q, planes):
        out_even, out_odd = None, None
        for j, (up, down) in enumerate(planes):
            one = jnp.where(even, down, up)
            two = jnp.where(even, up, down)
            one, two = [z if j == 0 else pltpu.roll(z, 2 * j, 0) for z in (one, two)]
            out_even = one if j == 0 else jnp.where(group == j, one, out_even)
            out_odd = two if j == 0 else jnp.where(group == j, two, out_odd)
        even_ref[q] = out_even
        odd_ref[q] = out_odd

    def ends(plane):
        return plane[:SUB], pltpu.roll(plane[SUB:], 2, 0)

    for q in range(base // 4):
        put(q, [ends(near[4 * q + j]) for j in range(4)])
    put(base // 4, [ends(near[base]), ends(near[base + 1]), ends(depth), ends(edge)])
    put(base // 4 + 1, [(pltpu.roll(forcing[:SUB], SUB - 1, 0), pltpu.roll(forcing[SUB:], 3, 0))])
    count = base // 4 + 2
    wide = ITERS - 1
    strip = main.shape[0]
    width = edge.shape[1]
    for r in range(wide):
        for j in range(across):
            here = slice(j * width, (j + 1) * width)
            up = main[r : r + 1, here]
            down = main[strip - wide + r : strip - wide + r + 1, here]
            q, at = divmod(r * across + j, SUB)
            even_ref[count + q, at : at + 1, :] = jnp.where(even, down, up)
            odd_ref[count + q, at : at + 1, :] = jnp.where(even, up, down)


def tile_step(get, source, depth, edge, layers):
    rows, columns = depth.shape
    cells = 2 * layers
    lane = iota((rows, columns), 1)
    first, last = lane == 0, lane == columns - 1

    def after(x, fill):
        return jnp.where(last, fill, left_by(x, 1))

    def before(x, fill):
        return jnp.where(first, fill, pltpu.roll(x, 1, 1))

    level = (iota((rows, LANE), 1) % layers).astype(jnp.float32)
    left, right = edge[:, :LANE], edge[:, LANE:]
    wet_left = level < left_by(left, 3 * cells)
    wet_own = level < left_by(left, LANE // 2 + 3 * cells)
    wet_right = level < left_by(right, 3 * cells)
    cell_left = jnp.where(wet_left, left, 0.0)
    cell_own = jnp.where(wet_own, left_by(left, LANE // 2), 0.0)
    cell_right = jnp.where(wet_right, right, 0.0)
    slope_left = below(cell_left) - above(cell_left)
    slope_own = below(cell_own) - above(cell_own)
    slope_right = below(cell_right) - above(cell_right)
    flux_left = left_by(left, cells) * 0.5 * (cell_left + cell_own) - 0.15 * (
        cell_own - cell_left + left_by(left, 2 * cells) * 0.25 * (slope_left + slope_own)
    )
    flux_left = jnp.where(wet_left & wet_own, flux_left, 0.0)

    depth_right = right[:, 3 * cells : 3 * cells + 1]
    depth_east = jnp.minimum(depth, below(depth))
    depth_north = jnp.minimum(depth, after(depth, depth_right))
    stars = ([], [])
    for k in range(layers):
        wet = depth > k
        mask = depth_east > k
        half = 0.5 * get(2, k)
        e_here = jnp.where(mask, half + 0.15, 0.0)
        e_next = jnp.where(mask, half - 0.15, 0.0)
        e_cross = jnp.where(mask, 0.0375 * get(4, k), 0.0)
        mask = depth_north > k
        half = 0.5 * get(3, k)
        n_here = jnp.where(mask, half + 0.15, 0.0)
        n_next = jnp.where(mask, half - 0.15, 0.0)
        n_cross = jnp.where(mask, 0.0375 * get(5, k), 0.0)
        for t in range(2):
            one = slice(t * layers + k, t * layers + k + 1)
            cell = jnp.where(wet, get(t, k), 0.0)
            east, west = below(cell), above(cell)
            north = after(cell, cell_right[:, one])
            south = before(cell, cell_left[:, one])
            cross = north - south
            flux = e_here * cell + e_next * east - e_cross * (cross + below(cross))
            star = cell - (flux - above(flux))
            cross = east - west
            cross = cross + after(cross, slope_right[:, one])
            flux = n_here * cell + n_next * north - n_cross * cross
            star = star - (flux - before(flux, flux_left[:, one]))
            if k == 0:
                star = star + source[t]
            stars[t].append(jnp.where(wet, star, 0.0))
    primes, rights = [], ([], [])
    upper = None
    density = 0.8 * stars[1][0] - 0.2 * stars[0][0]
    for k in range(layers):
        if k + 1 < layers:
            deeper = 0.8 * stars[1][k + 1] - 0.2 * stars[0][k + 1]
            couple = 0.05 + 1.0 / (1.0 + 10.0 * jnp.maximum(deeper - density, 0.0))
            couple = jnp.where(depth > k + 1, couple, 0.0)
            density = deeper
        else:
            couple = None
        if k == 0:
            inverse = 1.0 / (1.0 + couple)
        elif couple is not None:
            inverse = 1.0 / (1.0 + upper + couple - upper * primes[-1])
        else:
            inverse = 1.0 / (1.0 + upper - upper * primes[-1])
        for t in range(2):
            value = stars[t][k]
            if k:
                value = value + upper * rights[t][-1]
            rights[t].append(value * inverse)
        if couple is not None:
            primes.append(couple * inverse)
        upper = couple
    fresh = ([None] * layers, [None] * layers)
    forcing = None
    solved = [rights[0][-1], rights[1][-1]]
    for k in range(layers - 1, -1, -1):
        wet = depth > k
        for t in range(2):
            if k < layers - 1:
                solved[t] = rights[t][k] + primes[k] * solved[t]
            fresh[t][k] = jnp.where(wet, solved[t], 0.0)
        part = 0.8 * fresh[1][k] - 0.2 * fresh[0][k]
        forcing = part if forcing is None else forcing + part
    return fresh[0], fresh[1], forcing * (4.0 / math.sqrt(layers))


def inner_tile(t, s, u, v, x, y, source, depth, edge, t_out, s_out, f_out):
    layers = t.shape[0]
    refs = (t, s, u, v, x, y)
    warm, salt, forcing = tile_step(
        lambda kind, k: refs[kind][k],
        [source[0], source[1]],
        depth[...].astype(jnp.float32),
        edge[...],
        layers,
    )
    for k in range(layers):
        t_out[k] = warm[k]
        s_out[k] = salt[k]
    f_out[...] = forcing


def rim_rows(across, even_out, odd_out, even_in, odd_in, f_old, *refs):
    layers = refs[0].shape[0]
    t_fix, s_fix = refs[:2]
    sends, (field, blocks) = refs[2 : 2 + across], refs[2 + across :]
    rows = f_old.shape[0]
    strip = rows // across
    even = lax.axis_index("bx") % 2 == 0
    me = lax.axis_index("by")
    shape = (SUB, f_old.shape[1])
    line = iota(shape, 0)
    planes = []
    base = 6 * layers
    for q in range(base // 4 + 1):
        sent_even, sent_odd, came_even, came_odd = even_out[q], odd_out[q], even_in[q], odd_in[q]
        parts = [jnp.where(even, came_odd, came_even), jnp.where(even, sent_odd, sent_even)]
        parts += [jnp.where(even, sent_even, sent_odd), jnp.where(even, came_even, came_odd)]
        for j in range(4):
            total = None
            for i, part in enumerate(parts):
                part = part if i == j else pltpu.roll(part, (2 * (i - j)) % SUB, 0)
                total = part if i == 0 else jnp.where(line // 2 == i, part, total)
            planes.append(total)
    warm, salt, forcing = tile_step(
        lambda kind, k: planes[kind * layers + k],
        [planes[base], planes[base + 1]],
        planes[base + 2],
        planes[base + 3],
        layers,
    )
    for fix, fresh in ((t_fix, warm), (s_fix, salt)):
        for k in range(layers):
            fix[k] = jnp.where(line == 0, pltpu.roll(fresh[k], 6, 0), pltpu.roll(fresh[k], 2, 0))
    top, bottom = pltpu.roll(forcing, 6, 0), pltpu.roll(forcing, 2, 0)
    ahead = base // 4 + 1
    over = pltpu.roll(jnp.where(even, odd_in[ahead], even_in[ahead]), 5, 0)
    under = pltpu.roll(jnp.where(even, even_in[ahead], odd_in[ahead]), 1, 0)
    last = SUB - 1
    field[:SUB, :] = jnp.where(line == last, top, over)
    field[SUB : 2 * SUB, :] = jnp.where(line == 0, top, f_old[:SUB, :])
    field[2 * SUB : rows, :] = f_old[SUB : rows - SUB, :]
    field[rows : rows + SUB, :] = jnp.where(line == last, bottom, f_old[rows - SUB :, :])
    field[SUB + rows : 2 * SUB + rows, :] = jnp.where(line == 0, bottom, under)
    extra = even_out.shape[0] - ahead - 1
    tall = blocks.shape[1] - extra * SUB
    for peer in range(across):
        start = SUB - ITERS + peer * strip
        stop = min(start + tall, field.shape[0])
        blocks[peer, : stop - start, :] = field[start:stop, :]
    use_even = even == (me == 0)
    for q in range(extra):
        relay = jnp.where(use_even, even_in[ahead + 1 + q], odd_in[ahead + 1 + q])
        for peer in range(across):
            blocks[peer, tall + q * SUB : tall + (q + 1) * SUB, :] = relay
    for hop in range(across):
        sends[hop][...] = blocks[hop_peer(me, hop, across)]


def main_rows(from_even, from_odd, main_own, out):
    strip, columns = main_own.shape
    wide = ITERS - 1
    out[...] = jnp.zeros(out.shape, jnp.float32)
    out[ITERS : ITERS + strip, :] = main_own[...]
    over, under = ITERS - wide, ITERS + strip
    even = lax.axis_index("by") % 2 == 0
    parts = columns // LANE
    begin = from_even.shape[0] - wide * parts
    for r in range(wide):
        for j in range(parts):
            here = slice(j * LANE, (j + 1) * LANE)
            at = begin + r * parts + j
            a, b = from_even[at : at + 1, :], from_odd[at : at + 1, :]
            out[over + r : over + r + 1, here] = jnp.where(even, b, a)
            out[under + r : under + r + 1, here] = jnp.where(even, a, b)


def patch(fix_t, fix_s, t_old, s_old, t_new, s_new):
    target = jnp.where(pl.program_id(0) == 0, 0, SUB - 1)
    mine = iota(t_old.shape, 1) == target
    t_new[...] = jnp.where(mine, fix_t[...], t_old[...])
    s_new[...] = jnp.where(mine, fix_s[...], s_old[...])


def hop_peer(me, hop, count):
    if count & (count - 1) == 0:
        return me ^ hop
    return (me + hop) % count


def hop_origin(me, hop, count):
    if count & (count - 1) == 0:
        return me ^ hop
    return (me + count - hop) % count


def powers(across, along, *refs):
    came = refs[:across]
    main_in, basis_ref, row_ref, field, main = refs[across:]
    tall, columns = main_in.shape
    strip = basis_ref.shape[1]
    width = columns // across
    me = lax.axis_index("by")
    for hop in range(across):
        origin = hop_origin(me, hop, across)
        field[:, pl.ds(pl.multiple_of(origin * width, LANE), width)] = came[hop][:tall, :]
    wide = ITERS - 1
    main[...] = main_in[...]

    def relayed(start, mine, sender):
        hop = [h for h in range(across) if hop_origin(mine, h, across) == sender][0]

        @pl.when(me == mine)
        def _():
            for r in range(wide):
                for j in range(across):
                    at = tall + r * across + j
                    here = slice(j * width, (j + 1) * width)
                    main[start + r : start + r + 1, here] = came[hop][at : at + 1, :]

    relayed(ITERS - wide, 0, across - 1)
    relayed(ITERS + strip, across - 1, 0)
    shape = (tall, columns)
    lane = iota(shape, 1)
    line = (lax.axis_index("bx") * across + me) * strip - ITERS + iota(shape, 0)
    inside = (line >= 0) & (line < along * across * strip)
    first, last = lane == 0, lane == columns - 1
    centre = (main[...] + (6.0 - CENTRE)) * (1.0 / SCALE)
    centre = jnp.where(inside, centre, 0.0)
    share = jnp.where(inside, -1.0 / SCALE, 0.0)
    now = field[...]
    own = [now[ITERS : ITERS + strip]]
    for _ in range(ITERS):
        beside = below(now) + above(now)
        spread = now + 0.5 * beside
        east = jnp.where(last, 0.0, left_by(spread, 1))
        west = jnp.where(first, 0.0, pltpu.roll(spread, 1, 1))
        now = centre * now + share * (beside + east + west)
        own.append(now[ITERS : ITERS + strip])
    for k in range(ITERS):
        basis_ref[k] = own[k]
    place = iota((1, LANE), 1)
    row = jnp.zeros((1, LANE), jnp.float32)
    for k, (i, j) in enumerate(PAIRS):
        part = jnp.sum(own[i] * own[j], axis=0, keepdims=True)
        row = jnp.where(place == k, jnp.sum(part, axis=1, keepdims=True), row)
    row_ref[...] = jnp.broadcast_to(row[None], row_ref.shape)


def coefficients(moments):
    def inner(a, b):
        return sum(x * y * moments[i + j] for i, x in enumerate(a) for j, y in enumerate(b))

    zero = jnp.zeros_like(moments[0])
    resid = [zero + 1.0]
    direction = [zero + 1.0]
    total = [zero] * ITERS
    norm_now = inner(resid, resid)
    for step in range(ITERS):
        image = [zero] * (len(direction) + 1)
        for i, x in enumerate(direction):
            image[i] = image[i] + CENTRE * x
            image[i + 1] = image[i + 1] + SCALE * x
        alpha = norm_now / inner(direction, image)
        for i, x in enumerate(direction):
            total[i] = total[i] + alpha * x
        if step + 1 < ITERS:
            resid = [r - alpha * q for r, q in zip(resid + [zero], image)]
            norm_next = inner(resid, resid)
            beta = norm_next / norm_now
            direction = [r + beta * p for r, p in zip(resid, direction + [zero])]
            norm_now = norm_next
    return total


def combine(rows_ref, basis_ref, out_ref):
    moments = jnp.sum(rows_ref[...], axis=0)
    total = coefficients([moments[:, k : k + 1] for k in range(len(PAIRS))])
    out_ref[...] = total[0] * basis_ref[0] + total[1] * basis_ref[1] + total[2] * basis_ref[2]


def shape_of(*dims):
    return jax.ShapeDtypeStruct(dims, jnp.float32)


def whole(x):
    return pl.BlockSpec(x.shape, lambda *_: (0,) * len(x.shape))


def block(shape, *index):
    return pl.BlockSpec(shape, lambda *_: index)


def pairs(count, start):
    both = [(i, i + 1) for i in range(start, count - 1, 2)]
    return both + [(b, a) for a, b in both]


def local(t, s, u, v, x, y, source, depth, main):
    layers, rows, columns = t.shape
    across, along = lax.axis_size("by"), lax.axis_size("bx")
    strip = rows // across
    params = pltpu.CompilerParams(vmem_limit_bytes=48 << 20)

    call = functools.partial(pl.pallas_call, compiler_params=params)

    hbm = pl.BlockSpec(memory_space=pltpu.HBM)
    wide = ITERS - 1
    pack = shape_of(rows, LANE)
    more = shape_of(rows + wide * (columns * across // LANE), LANE)
    first, even, odd = call(
        pack_edges,
        grid=(1,),
        in_specs=[hbm] * 6,
        out_specs=[whole(pack), whole(more), whole(more)],
        out_shape=[pack, more, more],
        scratch_shapes=[
            pltpu.VMEM((6, layers, rows, LANE), jnp.float32),
            pltpu.VMEM((2, rows, LANE), jnp.int32),
            pltpu.VMEM(main.shape, jnp.float32),
            pltpu.SemaphoreType.DMA((15,)),
        ],
    )(*(pltpu.with_memory_space_constraint(a, pltpu.HBM) for a in (t, s, v, y, depth, main)))
    from_even = lax.ppermute(even, "by", pairs(across, 0))
    from_odd = lax.ppermute(odd, "by", pairs(across, 1))

    fields = (t, s, u, v, x, y, source)
    foot = rows // SUB - 1
    near = shape_of(6 * layers + 2, 2 * SUB, columns)
    near_depth = jax.ShapeDtypeStruct((2 * SUB, columns), depth.dtype)
    near, near_depth = call(
        gather_rows,
        grid=(1,),
        in_specs=[hbm] * 8,
        out_specs=[whole(near), whole(near_depth)],
        out_shape=[near, near_depth],
        scratch_shapes=[pltpu.SemaphoreType.DMA((16,))],
    )(*(pltpu.with_memory_space_constraint(a, pltpu.HBM) for a in (*fields, depth)))

    extra = -(-wide * across // SUB)
    plane = shape_of(rows, columns)
    sides = shape_of(rows, 2 * LANE)
    rim = shape_of(6 * layers // 4 + 2 + extra, SUB, columns)
    args = (first, from_even, from_odd, near, near_depth, main)
    edge, even, odd = call(
        functools.partial(pack_rows, across),
        grid=(1,),
        in_specs=[whole(a) for a in args],
        out_specs=[whole(sides), whole(rim), whole(rim)],
        out_shape=[sides, rim, rim],
    )(*args)
    odd_in = lax.ppermute(odd, "bx", pairs(along, 1))
    even_in = lax.ppermute(even, "bx", pairs(along, 0))

    cube = shape_of(layers, rows, columns)
    args = (*fields, depth, edge)
    warm, salt, forcing = call(
        inner_tile,
        grid=(1,),
        in_specs=[whole(a) for a in args],
        out_specs=[whole(cube), whole(cube), whole(plane)],
        out_shape=[cube, cube, plane],
    )(*args)

    tall = -(-(strip + 2 * ITERS) // SUB) * SUB
    part = shape_of(tall + extra * SUB, columns)
    fix = shape_of(layers, SUB, columns)
    fix_t, fix_s, *sends = call(
        functools.partial(rim_rows, across),
        grid=(1,),
        in_specs=[whole(rim)] * 4 + [whole(plane)],
        out_specs=[whole(fix)] * 2 + [whole(part)] * across,
        out_shape=[fix] * 2 + [part] * across,
        scratch_shapes=[
            pltpu.VMEM((rows + 2 * SUB, columns), jnp.float32),
            pltpu.VMEM((across,) + part.shape, jnp.float32),
        ],
    )(even, odd, even_in, odd_in, forcing)

    came = [sends[0]]
    for hop in range(1, across):
        route = [(i, hop_peer(i, hop, across)) for i in range(across)]
        came.append(lax.ppermute(sends[hop], "by", route))

    touched = pl.BlockSpec((layers, SUB, columns), lambda i: (0, i * foot, 0))
    warm, salt = call(
        patch,
        grid=(2,),
        in_specs=[whole(fix), whole(fix), touched, touched],
        out_specs=[touched, touched],
        out_shape=[cube, cube],
        input_output_aliases={2: 0, 3: 1},
    )(fix_t, fix_s, warm, salt)

    basis_shape = shape_of(ITERS, strip, columns * across)
    names = ("bx", "by")
    row_shape = shape_of(across * along, 1, LANE)
    ready = shape_of(tall, columns * across)
    args = (from_even, from_odd, main)
    ready = call(
        main_rows,
        grid=(1,),
        in_specs=[whole(a) for a in args],
        out_specs=whole(ready),
        out_shape=ready,
    )(*args)
    args = (*came, ready)
    basis, row = call(
        functools.partial(powers, across, along),
        grid=(1,),
        in_specs=[whole(a) for a in args],
        out_specs=[whole(basis_shape), whole(row_shape)],
        out_shape=[basis_shape, row_shape],
        scratch_shapes=[pltpu.VMEM((tall, columns * across), jnp.float32)] * 2,
    )(*args)
    gathered = lax.all_to_all(row, names, 0, 0, tiled=True)
    result = shape_of(strip, columns * across)
    pressure = call(
        combine,
        grid=(1,),
        in_specs=[whole(gathered), whole(basis)],
        out_specs=whole(result),
        out_shape=result,
    )(gathered, basis)
    return warm, salt, pressure


def solution(mesh):
    tile = P(None, "bx", "by")
    rows = P(("bx", "by"), None)
    return jax.shard_map(
        local,
        mesh=mesh,
        in_specs=(tile,) * 7 + (P("bx", "by"), rows),
        out_specs=(tile, tile, rows),
        check_vma=False,
    )
```

```python
import functools
import math

import jax
import jax.numpy as jnp
from jax import lax
from jax.experimental import pallas as pl
from jax.experimental.pallas import tpu as pltpu
from jax.sharding import PartitionSpec as P

ITERS = 3
CENTRE = 4.5
SCALE = 4.5
DEEP = ITERS + 1
SUB = 8
LANE = 128
PAIRS = ((0, 0), (0, 1), (1, 1), (1, 2), (2, 2), (2, 3))


def iota(shape, dim):
    return lax.broadcasted_iota(jnp.int32, shape, dim)


def below(x):
    return pltpu.roll(x, x.shape[0] - 1, 0)


def above(x):
    return pltpu.roll(x, 1, 0)


def left_by(x, lanes):
    return pltpu.roll(x, x.shape[1] - lanes, 1)


def pack_edges(t, s, v, y, depth, main, first_ref, even_ref, odd_ref, cubes, planes, lines, sems):
    layers, rows, columns = t.shape
    cells = 2 * layers
    wide = ITERS - 1
    head, tail = pl.ds(0, LANE), pl.ds(columns - LANE, LANE)
    moves = []
    for low in range(0, layers, layers // 2):
        some = pl.ds(low, layers // 2)
        for i, (ref, where) in enumerate(((t, tail), (s, tail), (v, tail), (y, tail), (t, head), (s, head))):
            moves.append((ref.at[some, :, where], cubes.at[i, some]))
    moves += [(depth.at[:, tail], planes.at[0]), (depth.at[:, head], planes.at[1]), (main, lines)]
    copies = [pltpu.make_async_copy(a, b, sems.at[i]) for i, (a, b) in enumerate(moves)]
    for copy in copies:
        copy.start()
    for copy in copies:
        copy.wait()
    lane = iota((rows, LANE), 1)
    first = jnp.zeros((rows, LANE), jnp.float32)
    last = jnp.zeros((rows, LANE), jnp.float32)
    edge = LANE - 1
    for k in range(layers):
        first = jnp.where(lane == k, cubes[4, k][:, 0:1], first)
        first = jnp.where(lane == layers + k, cubes[5, k][:, 0:1], first)
        last = jnp.where(lane == k, cubes[0, k][:, edge:], last)
        last = jnp.where(lane == layers + k, cubes[1, k][:, edge:], last)
        two = (lane == cells + k) | (lane == cells + layers + k)
        last = jnp.where(two, cubes[2, k][:, edge:], last)
        two = (lane == 2 * cells + k) | (lane == 2 * cells + layers + k)
        last = jnp.where(two, cubes[3, k][:, edge:], last)
    span = (lane >= 3 * cells) & (lane < 4 * cells)
    first = jnp.where(span, planes[1][:, 0:1].astype(jnp.float32), first)
    last = jnp.where(span, planes[0][:, edge:].astype(jnp.float32), last)
    first_ref[...] = first
    even = lax.axis_index("by") % 2 == 0
    even_ref[:rows, :] = jnp.where(even, last, first)
    odd_ref[:rows, :] = jnp.where(even, first, last)
    strip = lines.shape[0]
    parts = lines.shape[1] // LANE
    for r in range(wide):
        for j in range(parts):
            here = slice(j * LANE, (j + 1) * LANE)
            up = lines[r : r + 1, here]
            down = lines[strip - wide + r : strip - wide + r + 1, here]
            at = rows + r * parts + j
            even_ref[at : at + 1, :] = jnp.where(even, down, up)
            odd_ref[at : at + 1, :] = jnp.where(even, up, down)


def gather_rows(across, *refs):
    fields, depth, main = refs[:7], refs[7], refs[8]
    near, even_ref, odd_ref, raw, raw_depth, sems = refs[9:]
    layers, rows = fields[0].shape[:2]
    copies = []
    at = 0
    for ref in fields:
        for i, start in enumerate((0, rows - SUB)):
            planes = raw.at[pl.ds(at, ref.shape[0]), pl.ds(i * SUB, SUB)]
            copies.append((ref.at[:, pl.ds(start, SUB)], planes))
        at += ref.shape[0]
    for i, start in enumerate((0, rows - SUB)):
        copies.append((depth.at[pl.ds(start, SUB)], raw_depth.at[pl.ds(i * SUB, SUB)]))
    copies = [pltpu.make_async_copy(a, b, sems.at[i]) for i, (a, b) in enumerate(copies)]
    for copy in copies:
        copy.start()
    for copy in copies:
        copy.wait()
    base = 6 * layers
    planes = [(raw[p, :SUB], raw[p, SUB:]) for p in range(base + 2)]
    levels = raw_depth[...].astype(jnp.float32)
    planes.append((levels[:SUB], levels[SUB:]))
    line = iota(planes[0][0].shape, 0)
    for p, (up, down) in enumerate(planes):
        near[p] = jnp.where(line < SUB // 2, up, down)
    even = lax.axis_index("bx") % 2 == 0

    def put(q, parts):
        out_even, out_odd = None, None
        for p, at, count in parts:
            up, down = planes[p]
            up = pltpu.roll(up, at, 0) if at else up
            down = pltpu.roll(down, (at + count) % SUB, 0)
            one, two = jnp.where(even, down, up), jnp.where(even, up, down)
            out_even = one if at == 0 else jnp.where(line >= at, one, out_even)
            out_odd = two if at == 0 else jnp.where(line >= at, two, out_odd)
        even_ref[q] = out_even
        odd_ref[q] = out_odd

    twice, once = row_planes(layers)
    for q in range(len(twice) // 4):
        put(q, [(twice[4 * q + j], 2 * j, 2) for j in range(4)])
    for q in range(len(once) // SUB):
        put(len(twice) // 4 + q, [(once[SUB * q + j], j, 1) for j in range(SUB)])
    count = len(twice) // 4 + len(once) // SUB
    put(count, [(base, 0, 1), (base + 1, 1, 1), (base + 2, 2, 2)])
    count += 1
    wide = ITERS - 1
    strip = main.shape[0]
    width = fields[0].shape[2]
    for r in range(wide):
        for j in range(across):
            here = slice(j * width, (j + 1) * width)
            up = main[r : r + 1, here]
            down = main[strip - wide + r : strip - wide + r + 1, here]
            q, at = divmod(r * across + j, SUB)
            even_ref[count + q, at : at + 1, :] = jnp.where(even, down, up)
            odd_ref[count + q, at : at + 1, :] = jnp.where(even, up, down)


def row_planes(layers):
    kinds = [[kind * layers + k for k in range(layers)] for kind in range(6)]
    return kinds[0] + kinds[1] + kinds[2] + kinds[4], kinds[3] + kinds[5]


def pack_rows(first_ref, from_even, from_odd, near, even_in, odd_in, edge_ref, even_ref, odd_ref):
    rows, half = first_ref.shape[0], LANE // 2
    base = near.shape[0] - 3
    layers = base // 6
    even = lax.axis_index("by") % 2 == 0
    lane = iota((rows, LANE), 1)
    a, b = from_even[:rows, :], from_odd[:rows, :]
    left = jnp.where(even, b, a)
    right = jnp.where(even, a, b)
    left = jnp.where(lane < half, left, pltpu.roll(first_ref[...], half, 1))
    edge_ref[:, :LANE] = left
    edge_ref[:, LANE:] = right
    head, tail = edge_ref[:SUB, :], edge_ref[rows - SUB :, :]
    line = iota(head.shape, 0)
    _, _, forcing = tile_step(
        lambda kind, k: near[kind * layers + k],
        [near[base], near[base + 1]],
        near[base + 2],
        jnp.where(line < SUB // 2, head, tail),
        layers,
    )
    up = jnp.where(line < 6, pltpu.roll(head, 4, 0), pltpu.roll(forcing, 5, 0))
    down = jnp.where(line < 6, pltpu.roll(tail, 6, 0), pltpu.roll(forcing, 1, 0))
    even = lax.axis_index("bx") % 2 == 0
    even_ref[0] = jnp.where(line < 4, even_in[0], jnp.where(even, down, up))
    odd_ref[0] = jnp.where(line < 4, odd_in[0], jnp.where(even, up, down))


def tile_step(get, source, depth, edge, layers):
    rows, columns = depth.shape
    cells = 2 * layers
    lane = iota((rows, columns), 1)
    first, last = lane == 0, lane == columns - 1

    def after(x, fill):
        return jnp.where(last, fill, left_by(x, 1))

    def before(x, fill):
        return jnp.where(first, fill, pltpu.roll(x, 1, 1))

    level = (iota((rows, LANE), 1) % layers).astype(jnp.float32)
    left, right = edge[:, :LANE], edge[:, LANE:]
    wet_left = level < left_by(left, 3 * cells)
    wet_own = level < left_by(left, LANE // 2 + 3 * cells)
    wet_right = level < left_by(right, 3 * cells)
    cell_left = jnp.where(wet_left, left, 0.0)
    cell_own = jnp.where(wet_own, left_by(left, LANE // 2), 0.0)
    cell_right = jnp.where(wet_right, right, 0.0)
    slope_left = below(cell_left) - above(cell_left)
    slope_own = below(cell_own) - above(cell_own)
    slope_right = below(cell_right) - above(cell_right)
    flux_left = left_by(left, cells) * 0.5 * (cell_left + cell_own) - 0.15 * (
        cell_own - cell_left + left_by(left, 2 * cells) * 0.25 * (slope_left + slope_own)
    )
    flux_left = jnp.where(wet_left & wet_own, flux_left, 0.0)

    depth_right = right[:, 3 * cells : 3 * cells + 1]
    depth_east = jnp.minimum(depth, below(depth))
    depth_north = jnp.minimum(depth, after(depth, depth_right))
    stars = ([], [])
    for k in range(layers):
        wet = depth > k
        mask = depth_east > k
        half = 0.5 * get(2, k)
        e_here = jnp.where(mask, half + 0.15, 0.0)
        e_next = jnp.where(mask, half - 0.15, 0.0)
        e_cross = jnp.where(mask, 0.0375 * get(4, k), 0.0)
        mask = depth_north > k
        half = 0.5 * get(3, k)
        n_here = jnp.where(mask, half + 0.15, 0.0)
        n_next = jnp.where(mask, half - 0.15, 0.0)
        n_cross = jnp.where(mask, 0.0375 * get(5, k), 0.0)
        for t in range(2):
            one = slice(t * layers + k, t * layers + k + 1)
            cell = jnp.where(wet, get(t, k), 0.0)
            east, west = below(cell), above(cell)
            north = after(cell, cell_right[:, one])
            south = before(cell, cell_left[:, one])
            cross = north - south
            flux = e_here * cell + e_next * east - e_cross * (cross + below(cross))
            star = cell - (flux - above(flux))
            cross = east - west
            cross = cross + after(cross, slope_right[:, one])
            flux = n_here * cell + n_next * north - n_cross * cross
            star = star - (flux - before(flux, flux_left[:, one]))
            if k == 0:
                star = star + source[t]
            stars[t].append(jnp.where(wet, star, 0.0))
    primes, rights = [], ([], [])
    upper = None
    density = 0.8 * stars[1][0] - 0.2 * stars[0][0]
    for k in range(layers):
        if k + 1 < layers:
            deeper = 0.8 * stars[1][k + 1] - 0.2 * stars[0][k + 1]
            couple = 0.05 + 1.0 / (1.0 + 10.0 * jnp.maximum(deeper - density, 0.0))
            couple = jnp.where(depth > k + 1, couple, 0.0)
            density = deeper
        else:
            couple = None
        if k == 0:
            inverse = 1.0 / (1.0 + couple)
        elif couple is not None:
            inverse = 1.0 / (1.0 + upper + couple - upper * primes[-1])
        else:
            inverse = 1.0 / (1.0 + upper - upper * primes[-1])
        for t in range(2):
            value = stars[t][k]
            if k:
                value = value + upper * rights[t][-1]
            rights[t].append(value * inverse)
        if couple is not None:
            primes.append(couple * inverse)
        upper = couple
    fresh = ([None] * layers, [None] * layers)
    forcing = None
    solved = [rights[0][-1], rights[1][-1]]
    for k in range(layers - 1, -1, -1):
        wet = depth > k
        for t in range(2):
            if k < layers - 1:
                solved[t] = rights[t][k] + primes[k] * solved[t]
            fresh[t][k] = jnp.where(wet, solved[t], 0.0)
        part = 0.8 * fresh[1][k] - 0.2 * fresh[0][k]
        forcing = part if forcing is None else forcing + part
    return fresh[0], fresh[1], forcing * (4.0 / math.sqrt(layers))


def inner_tile(t, s, u, v, x, y, source, depth, edge, t_out, s_out, f_out):
    layers = t.shape[0]
    refs = (t, s, u, v, x, y)
    warm, salt, forcing = tile_step(
        lambda kind, k: refs[kind][k],
        [source[0], source[1]],
        depth[...].astype(jnp.float32),
        edge[...],
        layers,
    )
    for k in range(layers):
        t_out[k] = warm[k]
        s_out[k] = salt[k]
    f_out[...] = forcing


def rim_rows(across, even_out, odd_out, even_in, odd_in, f_old, *refs):
    layers = refs[0].shape[0]
    t_fix, s_fix = refs[:2]
    sends, (field, blocks) = refs[2 : 2 + across], refs[2 + across :]
    rows = f_old.shape[0]
    strip = rows // across
    even = lax.axis_index("bx") % 2 == 0
    me = lax.axis_index("by")
    shape = (SUB, f_old.shape[1])
    line = iota(shape, 0)
    base = 6 * layers
    planes = [None] * (base + 4)

    def parts(q):
        sent_even, sent_odd, came_even, came_odd = even_out[q], odd_out[q], even_in[q], odd_in[q]
        four = [jnp.where(even, came_odd, came_even), jnp.where(even, sent_odd, sent_even)]
        return four + [jnp.where(even, sent_even, sent_odd), jnp.where(even, came_even, came_odd)]

    def take(four, starts, at):
        total = None
        for i, part in enumerate(four):
            part = part if starts[i] == at else pltpu.roll(part, (starts[i] - at) % SUB, 0)
            total = part if i == 0 else jnp.where(line >= 2 * i, part, total)
        return total

    two_rows, one_row = (0, 2, 4, 6), (1, 2, 5, 6)
    twice, once = row_planes(layers)
    for i, p in enumerate(twice):
        if i % 4 == 0:
            four = parts(i // 4)
        planes[p] = take(four, two_rows, 2 * (i % 4))
    for i, p in enumerate(once):
        if i % SUB == 0:
            four = parts(len(twice) // 4 + i // SUB)
        planes[p] = take(four, one_row, i % SUB)
    ahead = len(twice) // 4 + len(once) // SUB
    four = parts(ahead)
    planes[base] = take(four, one_row, 0)
    planes[base + 1] = take(four, one_row, 1)
    planes[base + 2] = take(four, two_rows, 2)
    planes[base + 3] = take(four, two_rows, 4)
    over, under = pltpu.roll(four[0], 7, 0), pltpu.roll(four[3], 3, 0)
    warm, salt, forcing = tile_step(
        lambda kind, k: planes[kind * layers + k],
        [planes[base], planes[base + 1]],
        planes[base + 2],
        planes[base + 3],
        layers,
    )
    for fix, fresh in ((t_fix, warm), (s_fix, salt)):
        for k in range(layers):
            fix[k] = jnp.where(line == 0, pltpu.roll(fresh[k], 6, 0), pltpu.roll(fresh[k], 2, 0))
    top, bottom = pltpu.roll(forcing, 6, 0), pltpu.roll(forcing, 2, 0)
    last = SUB - 1
    field[:SUB, :] = jnp.where(line == last, top, over)
    field[SUB : 2 * SUB, :] = jnp.where(line == 0, top, f_old[:SUB, :])
    field[2 * SUB : rows, :] = f_old[SUB : rows - SUB, :]
    field[rows : rows + SUB, :] = jnp.where(line == last, bottom, f_old[rows - SUB :, :])
    field[SUB + rows : 2 * SUB + rows, :] = jnp.where(line == 0, bottom, under)
    extra = even_out.shape[0] - ahead - 1
    tall = blocks.shape[1] - extra * SUB
    for peer in range(across):
        start = SUB - ITERS + peer * strip
        stop = min(start + tall, field.shape[0])
        blocks[peer, : stop - start, :] = field[start:stop, :]
    use_even = even == (me == 0)
    for q in range(extra):
        relay = jnp.where(use_even, even_in[ahead + 1 + q], odd_in[ahead + 1 + q])
        for peer in range(across):
            blocks[peer, tall + q * SUB : tall + (q + 1) * SUB, :] = relay
    for hop in range(across):
        sends[hop][...] = blocks[hop_peer(me, hop, across)]


def main_rows(from_even, from_odd, main_own, out):
    strip, columns = main_own.shape
    wide = ITERS - 1
    out[...] = jnp.zeros(out.shape, jnp.float32)
    out[ITERS : ITERS + strip, :] = main_own[...]
    over, under = ITERS - wide, ITERS + strip
    even = lax.axis_index("by") % 2 == 0
    parts = columns // LANE
    begin = from_even.shape[0] - wide * parts
    for r in range(wide):
        for j in range(parts):
            here = slice(j * LANE, (j + 1) * LANE)
            at = begin + r * parts + j
            a, b = from_even[at : at + 1, :], from_odd[at : at + 1, :]
            out[over + r : over + r + 1, here] = jnp.where(even, b, a)
            out[under + r : under + r + 1, here] = jnp.where(even, a, b)


def flush(fix_t, fix_s, t_mid, s_mid, t_out, s_out, ends, sems):
    layers, rows, columns = t_mid.shape
    inner = pl.ds(SUB, rows - 2 * SUB)
    copies = []

    def begin(source, target):
        copies.append(pltpu.make_async_copy(source, target, sems.at[len(copies)]))
        copies[-1].start()

    for mid, out in ((t_mid, t_out), (s_mid, s_out)):
        for low in range(0, layers, 2):
            some = pl.ds(low, 2)
            begin(mid.at[some, inner], out.at[some, inner])
    line = iota((layers, SUB, columns), 1)
    for i, (mid, fix, out) in enumerate(((t_mid, fix_t, t_out), (s_mid, fix_s, s_out))):
        for j, (start, at) in enumerate(((0, 0), (rows - SUB, SUB - 1))):
            old = mid[:, start : start + SUB, :]
            ends[2 * i + j] = jnp.where(line == at, fix[...], old)
            begin(ends.at[2 * i + j], out.at[:, pl.ds(start, SUB)])
    for copy in copies:
        copy.wait()


def hop_peer(me, hop, count):
    if count & (count - 1) == 0:
        return me ^ hop
    return (me + hop) % count


def hop_origin(me, hop, count):
    if count & (count - 1) == 0:
        return me ^ hop
    return (me + count - hop) % count


def powers(across, along, *refs):
    came = refs[:across]
    main_in, basis_ref, row_ref, field, main = refs[across:]
    tall, columns = main_in.shape
    strip = basis_ref.shape[1]
    width = columns // across
    me = lax.axis_index("by")
    for hop in range(across):
        origin = hop_origin(me, hop, across)
        field[:, pl.ds(pl.multiple_of(origin * width, LANE), width)] = came[hop][:tall, :]
    wide = ITERS - 1
    main[...] = main_in[...]

    def relayed(start, mine, sender):
        hop = [h for h in range(across) if hop_origin(mine, h, across) == sender][0]

        @pl.when(me == mine)
        def _():
            for r in range(wide):
                for j in range(across):
                    at = tall + r * across + j
                    here = slice(j * width, (j + 1) * width)
                    main[start + r : start + r + 1, here] = came[hop][at : at + 1, :]

    relayed(ITERS - wide, 0, across - 1)
    relayed(ITERS + strip, across - 1, 0)
    shape = (tall, columns)
    lane = iota(shape, 1)
    line = (lax.axis_index("bx") * across + me) * strip - ITERS + iota(shape, 0)
    inside = (line >= 0) & (line < along * across * strip)
    first, last = lane == 0, lane == columns - 1
    centre = (main[...] + (6.0 - CENTRE)) * (1.0 / SCALE)
    centre = jnp.where(inside, centre, 0.0)
    share = jnp.where(inside, -1.0 / SCALE, 0.0)
    now = field[...]
    own = [now[ITERS : ITERS + strip]]
    for _ in range(ITERS):
        beside = below(now) + above(now)
        spread = now + 0.5 * beside
        east = jnp.where(last, 0.0, left_by(spread, 1))
        west = jnp.where(first, 0.0, pltpu.roll(spread, 1, 1))
        now = centre * now + share * (beside + east + west)
        own.append(now[ITERS : ITERS + strip])
    for k in range(ITERS):
        basis_ref[k] = own[k]
    place = iota((1, LANE), 1)
    row = jnp.zeros((1, LANE), jnp.float32)
    for k, (i, j) in enumerate(PAIRS):
        part = jnp.sum(own[i] * own[j], axis=0, keepdims=True)
        row = jnp.where(place == k, jnp.sum(part, axis=1, keepdims=True), row)
    row_ref[...] = jnp.broadcast_to(row[None], row_ref.shape)


def coefficients(moments):
    def inner(a, b):
        return sum(x * y * moments[i + j] for i, x in enumerate(a) for j, y in enumerate(b))

    zero = jnp.zeros_like(moments[0])
    resid = [zero + 1.0]
    direction = [zero + 1.0]
    total = [zero] * ITERS
    norm_now = inner(resid, resid)
    for step in range(ITERS):
        image = [zero] * (len(direction) + 1)
        for i, x in enumerate(direction):
            image[i] = image[i] + CENTRE * x
            image[i + 1] = image[i + 1] + SCALE * x
        alpha = norm_now / inner(direction, image)
        for i, x in enumerate(direction):
            total[i] = total[i] + alpha * x
        if step + 1 < ITERS:
            resid = [r - alpha * q for r, q in zip(resid + [zero], image)]
            norm_next = inner(resid, resid)
            beta = norm_next / norm_now
            direction = [r + beta * p for r, p in zip(resid, direction + [zero])]
            norm_now = norm_next
    return total


def combine(rows_ref, basis_ref, out_ref):
    moments = jnp.sum(rows_ref[...], axis=0)
    total = coefficients([moments[:, k : k + 1] for k in range(len(PAIRS))])
    out_ref[...] = total[0] * basis_ref[0] + total[1] * basis_ref[1] + total[2] * basis_ref[2]


def shape_of(*dims):
    return jax.ShapeDtypeStruct(dims, jnp.float32)


def whole(x):
    return pl.BlockSpec(x.shape, lambda *_: (0,) * len(x.shape))


def block(shape, *index):
    return pl.BlockSpec(shape, lambda *_: index)


def pairs(count, start):
    both = [(i, i + 1) for i in range(start, count - 1, 2)]
    return both + [(b, a) for a, b in both]


def local(t, s, u, v, x, y, source, depth, main):
    layers, rows, columns = t.shape
    across, along = lax.axis_size("by"), lax.axis_size("bx")
    strip = rows // across
    params = pltpu.CompilerParams(vmem_limit_bytes=48 << 20)

    call = functools.partial(pl.pallas_call, compiler_params=params)

    hbm = pl.BlockSpec(memory_space=pltpu.HBM)
    wide = ITERS - 1
    pack = shape_of(rows, LANE)
    more = shape_of(rows + wide * (columns * across // LANE), LANE)
    first, even, odd = call(
        pack_edges,
        grid=(1,),
        in_specs=[hbm] * 6,
        out_specs=[whole(pack), whole(more), whole(more)],
        out_shape=[pack, more, more],
        scratch_shapes=[
            pltpu.VMEM((6, layers, rows, LANE), jnp.float32),
            pltpu.VMEM((2, rows, LANE), jnp.int32),
            pltpu.VMEM(main.shape, jnp.float32),
            pltpu.SemaphoreType.DMA((15,)),
        ],
    )(*(pltpu.with_memory_space_constraint(a, pltpu.HBM) for a in (t, s, v, y, depth, main)))
    from_even = lax.ppermute(even, "by", pairs(across, 0))
    from_odd = lax.ppermute(odd, "by", pairs(across, 1))

    fields = (t, s, u, v, x, y, source)
    extra = -(-wide * across // SUB)
    sides = shape_of(rows, 2 * LANE)
    near = shape_of(6 * layers + 3, SUB, columns)
    shared = layers + 2 * layers // SUB
    rim = shape_of(shared + 1 + extra, SUB, columns)
    near, even, odd = call(
        functools.partial(gather_rows, across),
        grid=(1,),
        in_specs=[hbm] * 8 + [whole(main)],
        out_specs=[whole(near), whole(rim), whole(rim)],
        out_shape=[near, rim, rim],
        scratch_shapes=[
            pltpu.VMEM((6 * layers + 2, 2 * SUB, columns), jnp.float32),
            pltpu.VMEM((2 * SUB, columns), depth.dtype),
            pltpu.SemaphoreType.DMA((16,)),
        ],
    )(*(pltpu.with_memory_space_constraint(a, pltpu.HBM) for a in (*fields, depth)), main)

    plane = shape_of(rows, columns)
    args = (first, from_even, from_odd, near)
    tile = block((1, SUB, columns), shared, 0, 0)
    edge, even, odd = call(
        pack_rows,
        grid=(1,),
        in_specs=[whole(a) for a in args] + [tile] * 2,
        out_specs=[whole(sides), tile, tile],
        out_shape=[sides, rim, rim],
        input_output_aliases={4: 1, 5: 2},
    )(*args, even, odd)
    odd_in = lax.ppermute(odd, "bx", pairs(along, 1))
    even_in = lax.ppermute(even, "bx", pairs(along, 0))

    cube = shape_of(layers, rows, columns)
    args = (*fields, depth, edge)
    warm, salt, forcing = call(
        inner_tile,
        grid=(1,),
        in_specs=[whole(a) for a in args],
        out_specs=[whole(cube), whole(cube), whole(plane)],
        out_shape=[cube, cube, plane],
    )(*args)

    tall = -(-(strip + 2 * ITERS) // SUB) * SUB
    part = shape_of(tall + extra * SUB, columns)
    fix = shape_of(layers, SUB, columns)
    fix_t, fix_s, *sends = call(
        functools.partial(rim_rows, across),
        grid=(1,),
        in_specs=[whole(rim)] * 4 + [whole(plane)],
        out_specs=[whole(fix)] * 2 + [whole(part)] * across,
        out_shape=[fix] * 2 + [part] * across,
        scratch_shapes=[
            pltpu.VMEM((rows + 2 * SUB, columns), jnp.float32),
            pltpu.VMEM((across,) + part.shape, jnp.float32),
        ],
    )(even, odd, even_in, odd_in, forcing)

    came = [sends[0]]
    for hop in range(1, across):
        route = [(i, hop_peer(i, hop, across)) for i in range(across)]
        came.append(lax.ppermute(sends[hop], "by", route))

    args = (fix_t, fix_s, warm, salt)
    warm, salt = call(
        flush,
        grid=(1,),
        in_specs=[whole(a) for a in args],
        out_specs=[hbm] * 2,
        out_shape=[cube] * 2,
        scratch_shapes=[
            pltpu.VMEM((4, layers, SUB, columns), jnp.float32),
            pltpu.SemaphoreType.DMA((layers + 4,)),
        ],
    )(*args)

    basis_shape = shape_of(ITERS, strip, columns * across)
    names = ("bx", "by")
    row_shape = shape_of(across * along, 1, LANE)
    ready = shape_of(tall, columns * across)
    args = (from_even, from_odd, main)
    ready = call(
        main_rows,
        grid=(1,),
        in_specs=[whole(a) for a in args],
        out_specs=whole(ready),
        out_shape=ready,
    )(*args)
    ready, warm, salt = lax.optimization_barrier((ready, warm, salt))
    args = (*came, ready)
    basis, row = call(
        functools.partial(powers, across, along),
        grid=(1,),
        in_specs=[whole(a) for a in args],
        out_specs=[whole(basis_shape), whole(row_shape)],
        out_shape=[basis_shape, row_shape],
        scratch_shapes=[pltpu.VMEM((tall, columns * across), jnp.float32)] * 2,
    )(*args)
    gathered = lax.all_to_all(row, names, 0, 0, tiled=True)
    result = shape_of(strip, columns * across)
    pressure = call(
        combine,
        grid=(1,),
        in_specs=[whole(gathered), whole(basis)],
        out_specs=whole(result),
        out_shape=result,
    )(gathered, basis)
    return warm, salt, pressure


def solution(mesh):
    tile = P(None, "bx", "by")
    rows = P(("bx", "by"), None)
    return jax.shard_map(
        local,
        mesh=mesh,
        in_specs=(tile,) * 7 + (P("bx", "by"), rows),
        out_specs=(tile, tile, rows),
        check_vma=False,
    )
```

```python
import functools
import math

import jax
import jax.numpy as jnp
from jax import lax
from jax.experimental import pallas as pl
from jax.experimental.pallas import tpu as pltpu
from jax.sharding import PartitionSpec as P

ITERS = 3
CENTRE = 4.5
SCALE = 4.5
DEEP = ITERS + 1
SUB = 8
LANE = 128
PAIRS = ((0, 0), (0, 1), (1, 1), (1, 2), (2, 2), (2, 3))


def iota(shape, dim):
    return lax.broadcasted_iota(jnp.int32, shape, dim)


def below(x):
    return pltpu.roll(x, x.shape[0] - 1, 0)


def above(x):
    return pltpu.roll(x, 1, 0)


def left_by(x, lanes):
    return pltpu.roll(x, x.shape[1] - lanes, 1)


def pack_edges(t, s, v, y, depth, main, first_ref, even_ref, odd_ref, cubes, planes, lines, sems):
    layers, rows, columns = t.shape
    cells = 2 * layers
    wide = ITERS - 1
    head, tail = pl.ds(0, LANE), pl.ds(columns - LANE, LANE)
    moves = []
    for low in range(0, layers, layers // 2):
        some = pl.ds(low, layers // 2)
        for i, (ref, where) in enumerate(((t, tail), (s, tail), (v, tail), (y, tail), (t, head), (s, head))):
            moves.append((ref.at[some, :, where], cubes.at[i, some]))
    moves += [(depth.at[:, tail], planes.at[0]), (depth.at[:, head], planes.at[1]), (main, lines)]
    copies = [pltpu.make_async_copy(a, b, sems.at[i]) for i, (a, b) in enumerate(moves)]
    for copy in copies:
        copy.start()
    for copy in copies:
        copy.wait()
    lane = iota((rows, LANE), 1)
    first = jnp.zeros((rows, LANE), jnp.float32)
    last = jnp.zeros((rows, LANE), jnp.float32)
    edge = LANE - 1
    for k in range(layers):
        first = jnp.where(lane == k, cubes[4, k][:, 0:1], first)
        first = jnp.where(lane == layers + k, cubes[5, k][:, 0:1], first)
        last = jnp.where(lane == k, cubes[0, k][:, edge:], last)
        last = jnp.where(lane == layers + k, cubes[1, k][:, edge:], last)
        two = (lane == cells + k) | (lane == cells + layers + k)
        last = jnp.where(two, cubes[2, k][:, edge:], last)
        two = (lane == 2 * cells + k) | (lane == 2 * cells + layers + k)
        last = jnp.where(two, cubes[3, k][:, edge:], last)
    span = (lane >= 3 * cells) & (lane < 4 * cells)
    first = jnp.where(span, planes[1][:, 0:1].astype(jnp.float32), first)
    last = jnp.where(span, planes[0][:, edge:].astype(jnp.float32), last)
    first_ref[...] = first
    even = lax.axis_index("by") % 2 == 0
    even_ref[:rows, :] = jnp.where(even, last, first)
    odd_ref[:rows, :] = jnp.where(even, first, last)
    strip = lines.shape[0]
    parts = lines.shape[1] // LANE
    for r in range(wide):
        for j in range(parts):
            here = slice(j * LANE, (j + 1) * LANE)
            up = lines[r : r + 1, here]
            down = lines[strip - wide + r : strip - wide + r + 1, here]
            at = rows + r * parts + j
            even_ref[at : at + 1, :] = jnp.where(even, down, up)
            odd_ref[at : at + 1, :] = jnp.where(even, up, down)


def gather_rows(across, *refs):
    fields, depth, main = refs[:7], refs[7], refs[8]
    near, even_ref, odd_ref, raw, raw_depth, sems = refs[9:]
    layers, rows = fields[0].shape[:2]
    copies = []
    at = 0
    for ref in fields:
        for i, start in enumerate((0, rows - SUB)):
            planes = raw.at[pl.ds(at, ref.shape[0]), pl.ds(i * SUB, SUB)]
            copies.append((ref.at[:, pl.ds(start, SUB)], planes))
        at += ref.shape[0]
    for i, start in enumerate((0, rows - SUB)):
        copies.append((depth.at[pl.ds(start, SUB)], raw_depth.at[pl.ds(i * SUB, SUB)]))
    copies = [pltpu.make_async_copy(a, b, sems.at[i]) for i, (a, b) in enumerate(copies)]
    for copy in copies:
        copy.start()
    for copy in copies:
        copy.wait()
    base = 6 * layers
    planes = [(raw[p, :SUB], raw[p, SUB:]) for p in range(base + 2)]
    levels = raw_depth[...].astype(jnp.float32)
    planes.append((levels[:SUB], levels[SUB:]))
    line = iota(planes[0][0].shape, 0)
    for p, (up, down) in enumerate(planes):
        near[p] = jnp.where(line < SUB // 2, up, down)
    even = lax.axis_index("bx") % 2 == 0

    def put(q, parts):
        out_even, out_odd = None, None
        for p, at, count in parts:
            up, down = planes[p]
            up = pltpu.roll(up, at, 0) if at else up
            down = pltpu.roll(down, (at + count) % SUB, 0)
            one, two = jnp.where(even, down, up), jnp.where(even, up, down)
            out_even = one if at == 0 else jnp.where(line >= at, one, out_even)
            out_odd = two if at == 0 else jnp.where(line >= at, two, out_odd)
        even_ref[q] = out_even
        odd_ref[q] = out_odd

    twice, once = row_planes(layers)
    for q in range(len(twice) // 4):
        put(q, [(twice[4 * q + j], 2 * j, 2) for j in range(4)])
    for q in range(len(once) // SUB):
        put(len(twice) // 4 + q, [(once[SUB * q + j], j, 1) for j in range(SUB)])
    count = len(twice) // 4 + len(once) // SUB
    put(count, [(base, 0, 1), (base + 1, 1, 1), (base + 2, 2, 2)])
    count += 1
    wide = ITERS - 1
    strip = main.shape[0]
    width = fields[0].shape[2]
    for r in range(wide):
        for j in range(across):
            here = slice(j * width, (j + 1) * width)
            up = main[r : r + 1, here]
            down = main[strip - wide + r : strip - wide + r + 1, here]
            q, at = divmod(r * across + j, SUB)
            even_ref[count + q, at : at + 1, :] = jnp.where(even, down, up)
            odd_ref[count + q, at : at + 1, :] = jnp.where(even, up, down)


def row_planes(layers):
    kinds = [[kind * layers + k for k in range(layers)] for kind in range(6)]
    return kinds[0] + kinds[1] + kinds[2] + kinds[4], kinds[3] + kinds[5]


def pack_rows(first_ref, from_odd, from_even, near, even_in, odd_in, edge_ref, even_ref, odd_ref):
    rows, half = first_ref.shape[0], LANE // 2
    base = near.shape[0] - 3
    layers = base // 6
    even = lax.axis_index("by") % 2 == 0
    lane = iota((rows, LANE), 1)
    a, b = from_even[:rows, :], from_odd[:rows, :]
    left, right = jnp.where(even, b, a), jnp.where(even, a, b)
    me = lax.axis_index("by")
    left = jnp.where(me == 0, 0.0, left)
    right = jnp.where(me == lax.axis_size("by") - 1, 0.0, right)
    left = jnp.where(lane < half, left, pltpu.roll(first_ref[...], half, 1))
    edge_ref[:, :LANE] = left
    edge_ref[:, LANE:] = right
    head, tail = edge_ref[:SUB, :], edge_ref[rows - SUB :, :]
    line = iota(head.shape, 0)
    _, _, forcing = tile_step(
        lambda kind, k: near[kind * layers + k],
        [near[base], near[base + 1]],
        near[base + 2],
        jnp.where(line < SUB // 2, head, tail),
        layers,
    )
    up = jnp.where(line < 6, pltpu.roll(head, 4, 0), pltpu.roll(forcing, 5, 0))
    down = jnp.where(line < 6, pltpu.roll(tail, 6, 0), pltpu.roll(forcing, 1, 0))
    even = lax.axis_index("bx") % 2 == 0
    even_ref[0] = jnp.where(line < 4, even_in[0], jnp.where(even, down, up))
    odd_ref[0] = jnp.where(line < 4, odd_in[0], jnp.where(even, up, down))


def tile_step(get, source, depth, edge, layers):
    rows, columns = depth.shape
    cells = 2 * layers
    lane = iota((rows, columns), 1)
    first, last = lane == 0, lane == columns - 1

    def after(x, fill):
        return jnp.where(last, fill, left_by(x, 1))

    def before(x, fill):
        return jnp.where(first, fill, pltpu.roll(x, 1, 1))

    level = (iota((rows, LANE), 1) % layers).astype(jnp.float32)
    left, right = edge[:, :LANE], edge[:, LANE:]
    wet_left = level < left_by(left, 3 * cells)
    wet_own = level < left_by(left, LANE // 2 + 3 * cells)
    wet_right = level < left_by(right, 3 * cells)
    cell_left = jnp.where(wet_left, left, 0.0)
    cell_own = jnp.where(wet_own, left_by(left, LANE // 2), 0.0)
    cell_right = jnp.where(wet_right, right, 0.0)
    slope_left = below(cell_left) - above(cell_left)
    slope_own = below(cell_own) - above(cell_own)
    slope_right = below(cell_right) - above(cell_right)
    flux_left = left_by(left, cells) * 0.5 * (cell_left + cell_own) - 0.15 * (
        cell_own - cell_left + left_by(left, 2 * cells) * 0.25 * (slope_left + slope_own)
    )
    flux_left = jnp.where(wet_left & wet_own, flux_left, 0.0)

    depth_right = right[:, 3 * cells : 3 * cells + 1]
    depth_east = jnp.minimum(depth, below(depth))
    depth_north = jnp.minimum(depth, after(depth, depth_right))
    stars = ([], [])
    for k in range(layers):
        wet = depth > k
        mask = depth_east > k
        half = 0.5 * get(2, k)
        e_here = jnp.where(mask, half + 0.15, 0.0)
        e_next = jnp.where(mask, half - 0.15, 0.0)
        e_cross = jnp.where(mask, 0.0375 * get(4, k), 0.0)
        mask = depth_north > k
        half = 0.5 * get(3, k)
        n_here = jnp.where(mask, half + 0.15, 0.0)
        n_next = jnp.where(mask, half - 0.15, 0.0)
        n_cross = jnp.where(mask, 0.0375 * get(5, k), 0.0)
        for t in range(2):
            one = slice(t * layers + k, t * layers + k + 1)
            cell = jnp.where(wet, get(t, k), 0.0)
            east, west = below(cell), above(cell)
            north = after(cell, cell_right[:, one])
            south = before(cell, cell_left[:, one])
            cross = north - south
            flux = e_here * cell + e_next * east - e_cross * (cross + below(cross))
            star = cell - (flux - above(flux))
            cross = east - west
            cross = cross + after(cross, slope_right[:, one])
            flux = n_here * cell + n_next * north - n_cross * cross
            star = star - (flux - before(flux, flux_left[:, one]))
            if k == 0:
                star = star + source[t]
            stars[t].append(jnp.where(wet, star, 0.0))
    primes, rights = [], ([], [])
    upper = None
    density = 0.8 * stars[1][0] - 0.2 * stars[0][0]
    for k in range(layers):
        if k + 1 < layers:
            deeper = 0.8 * stars[1][k + 1] - 0.2 * stars[0][k + 1]
            couple = 0.05 + 1.0 / (1.0 + 10.0 * jnp.maximum(deeper - density, 0.0))
            couple = jnp.where(depth > k + 1, couple, 0.0)
            density = deeper
        else:
            couple = None
        if k == 0:
            inverse = 1.0 / (1.0 + couple)
        elif couple is not None:
            inverse = 1.0 / (1.0 + upper + couple - upper * primes[-1])
        else:
            inverse = 1.0 / (1.0 + upper - upper * primes[-1])
        for t in range(2):
            value = stars[t][k]
            if k:
                value = value + upper * rights[t][-1]
            rights[t].append(value * inverse)
        if couple is not None:
            primes.append(couple * inverse)
        upper = couple
    fresh = ([None] * layers, [None] * layers)
    forcing = None
    solved = [rights[0][-1], rights[1][-1]]
    for k in range(layers - 1, -1, -1):
        wet = depth > k
        for t in range(2):
            if k < layers - 1:
                solved[t] = rights[t][k] + primes[k] * solved[t]
            fresh[t][k] = jnp.where(wet, solved[t], 0.0)
        part = 0.8 * fresh[1][k] - 0.2 * fresh[0][k]
        forcing = part if forcing is None else forcing + part
    return fresh[0], fresh[1], forcing * (4.0 / math.sqrt(layers))


def inner_tile(t, s, u, v, x, y, source, depth, edge, t_out, s_out, f_out):
    layers = t.shape[0]
    refs = (t, s, u, v, x, y)
    warm, salt, forcing = tile_step(
        lambda kind, k: refs[kind][k],
        [source[0], source[1]],
        depth[...].astype(jnp.float32),
        edge[...],
        layers,
    )
    for k in range(layers):
        t_out[k] = warm[k]
        s_out[k] = salt[k]
    f_out[...] = forcing


def rim_rows(across, even_out, odd_out, odd_in, even_in, f_old, *refs):
    layers = refs[0].shape[0]
    t_fix, s_fix = refs[:2]
    sends, (field, blocks) = refs[2 : 2 + across], refs[2 + across :]
    rows = f_old.shape[0]
    strip = rows // across
    even = lax.axis_index("bx") % 2 == 0
    me = lax.axis_index("by")
    shape = (SUB, f_old.shape[1])
    line = iota(shape, 0)
    base = 6 * layers
    planes = [None] * (base + 4)

    def parts(q):
        sent_even, sent_odd, came_even, came_odd = even_out[q], odd_out[q], even_in[q], odd_in[q]
        four = [jnp.where(even, came_odd, came_even), jnp.where(even, sent_odd, sent_even)]
        return four + [jnp.where(even, sent_even, sent_odd), jnp.where(even, came_even, came_odd)]

    def take(four, starts, at):
        total = None
        for i, part in enumerate(four):
            part = part if starts[i] == at else pltpu.roll(part, (starts[i] - at) % SUB, 0)
            total = part if i == 0 else jnp.where(line >= 2 * i, part, total)
        return total

    two_rows, one_row = (0, 2, 4, 6), (1, 2, 5, 6)
    twice, once = row_planes(layers)
    for i, p in enumerate(twice):
        if i % 4 == 0:
            four = parts(i // 4)
        planes[p] = take(four, two_rows, 2 * (i % 4))
    for i, p in enumerate(once):
        if i % SUB == 0:
            four = parts(len(twice) // 4 + i // SUB)
        planes[p] = take(four, one_row, i % SUB)
    ahead = len(twice) // 4 + len(once) // SUB
    four = parts(ahead)
    me_along = lax.axis_index("bx")
    four[0] = jnp.where(me_along == 0, 0.0, four[0])
    four[3] = jnp.where(me_along == lax.axis_size("bx") - 1, 0.0, four[3])
    planes[base] = take(four, one_row, 0)
    planes[base + 1] = take(four, one_row, 1)
    planes[base + 2] = take(four, two_rows, 2)
    planes[base + 3] = take(four, two_rows, 4)
    over, under = pltpu.roll(four[0], 7, 0), pltpu.roll(four[3], 3, 0)
    warm, salt, forcing = tile_step(
        lambda kind, k: planes[kind * layers + k],
        [planes[base], planes[base + 1]],
        planes[base + 2],
        planes[base + 3],
        layers,
    )
    for fix, fresh in ((t_fix, warm), (s_fix, salt)):
        for k in range(layers):
            fix[k] = jnp.where(line == 0, pltpu.roll(fresh[k], 6, 0), pltpu.roll(fresh[k], 2, 0))
    top, bottom = pltpu.roll(forcing, 6, 0), pltpu.roll(forcing, 2, 0)
    last = SUB - 1
    field[:SUB, :] = jnp.where(line == last, top, over)
    field[SUB : 2 * SUB, :] = jnp.where(line == 0, top, f_old[:SUB, :])
    field[2 * SUB : rows, :] = f_old[SUB : rows - SUB, :]
    field[rows : rows + SUB, :] = jnp.where(line == last, bottom, f_old[rows - SUB :, :])
    field[SUB + rows : 2 * SUB + rows, :] = jnp.where(line == 0, bottom, under)
    extra = even_out.shape[0] - ahead - 1
    tall = blocks.shape[1] - extra * SUB
    for peer in range(across):
        start = SUB - ITERS + peer * strip
        stop = min(start + tall, field.shape[0])
        blocks[peer, : stop - start, :] = field[start:stop, :]
    use_even = even == (me == 0)
    for q in range(extra):
        relay = jnp.where(use_even, even_in[ahead + 1 + q], odd_in[ahead + 1 + q])
        for peer in range(across):
            blocks[peer, tall + q * SUB : tall + (q + 1) * SUB, :] = relay
    for hop in range(across):
        sends[hop][...] = blocks[hop_peer(me, hop, across)]


def main_rows(from_even, from_odd, main_own, out):
    strip, columns = main_own.shape
    wide = ITERS - 1
    out[...] = jnp.zeros(out.shape, jnp.float32)
    out[ITERS : ITERS + strip, :] = main_own[...]
    over, under = ITERS - wide, ITERS + strip
    even = lax.axis_index("by") % 2 == 0
    parts = columns // LANE
    begin = from_even.shape[0] - wide * parts
    for r in range(wide):
        for j in range(parts):
            here = slice(j * LANE, (j + 1) * LANE)
            at = begin + r * parts + j
            a, b = from_even[at : at + 1, :], from_odd[at : at + 1, :]
            out[over + r : over + r + 1, here] = jnp.where(even, b, a)
            out[under + r : under + r + 1, here] = jnp.where(even, a, b)


def flush(fix_t, fix_s, t_mid, s_mid, t_out, s_out, ends, sems):
    layers, rows, columns = t_mid.shape
    inner = pl.ds(SUB, rows - 2 * SUB)
    copies = []

    def begin(source, target):
        copies.append(pltpu.make_async_copy(source, target, sems.at[len(copies)]))
        copies[-1].start()

    for mid, out in ((t_mid, t_out), (s_mid, s_out)):
        for low in range(0, layers, 2):
            some = pl.ds(low, 2)
            begin(mid.at[some, inner], out.at[some, inner])
    line = iota((layers, SUB, columns), 1)
    for i, (mid, fix, out) in enumerate(((t_mid, fix_t, t_out), (s_mid, fix_s, s_out))):
        for j, (start, at) in enumerate(((0, 0), (rows - SUB, SUB - 1))):
            old = mid[:, start : start + SUB, :]
            ends[2 * i + j] = jnp.where(line == at, fix[...], old)
            begin(ends.at[2 * i + j], out.at[:, pl.ds(start, SUB)])
    for copy in copies:
        copy.wait()


def hop_peer(me, hop, count):
    if count & (count - 1) == 0:
        return me ^ hop
    return (me + hop) % count


def hop_origin(me, hop, count):
    if count & (count - 1) == 0:
        return me ^ hop
    return (me + count - hop) % count


def powers(across, along, *refs):
    came = [refs[0], *refs[1:across][::-1]]
    main_in, basis_ref, row_ref, field, main = refs[across:]
    tall, columns = main_in.shape
    strip = basis_ref.shape[1]
    width = columns // across
    me = lax.axis_index("by")
    for hop in range(across):
        origin = hop_origin(me, hop, across)
        field[:, pl.ds(pl.multiple_of(origin * width, LANE), width)] = came[hop][:tall, :]
    wide = ITERS - 1
    main[...] = main_in[...]

    def relayed(start, mine, sender):
        hop = [h for h in range(across) if hop_origin(mine, h, across) == sender][0]

        @pl.when(me == mine)
        def _():
            for r in range(wide):
                for j in range(across):
                    at = tall + r * across + j
                    here = slice(j * width, (j + 1) * width)
                    main[start + r : start + r + 1, here] = came[hop][at : at + 1, :]

    relayed(ITERS - wide, 0, across - 1)
    relayed(ITERS + strip, across - 1, 0)
    shape = (tall, columns)
    lane = iota(shape, 1)
    line = (lax.axis_index("bx") * across + me) * strip - ITERS + iota(shape, 0)
    inside = (line >= 0) & (line < along * across * strip)
    first, last = lane == 0, lane == columns - 1
    centre = (main[...] + (6.0 - CENTRE)) * (1.0 / SCALE)
    centre = jnp.where(inside, centre, 0.0)
    share = jnp.where(inside, -1.0 / SCALE, 0.0)
    now = field[...]
    own = [now[ITERS : ITERS + strip]]
    for _ in range(ITERS):
        beside = below(now) + above(now)
        spread = now + 0.5 * beside
        east = jnp.where(last, 0.0, left_by(spread, 1))
        west = jnp.where(first, 0.0, pltpu.roll(spread, 1, 1))
        now = centre * now + share * (beside + east + west)
        own.append(now[ITERS : ITERS + strip])
    for k in range(ITERS):
        basis_ref[k] = own[k]
    place = iota((1, LANE), 1)
    row = jnp.zeros((1, LANE), jnp.float32)
    for k, (i, j) in enumerate(PAIRS):
        part = jnp.sum(own[i] * own[j], axis=0, keepdims=True)
        row = jnp.where(place == k, jnp.sum(part, axis=1, keepdims=True), row)
    row_ref[...] = jnp.broadcast_to(row[None], row_ref.shape)


def coefficients(moments):
    def inner(a, b):
        return sum(x * y * moments[i + j] for i, x in enumerate(a) for j, y in enumerate(b))

    zero = jnp.zeros_like(moments[0])
    resid = [zero + 1.0]
    direction = [zero + 1.0]
    total = [zero] * ITERS
    norm_now = inner(resid, resid)
    for step in range(ITERS):
        image = [zero] * (len(direction) + 1)
        for i, x in enumerate(direction):
            image[i] = image[i] + CENTRE * x
            image[i + 1] = image[i + 1] + SCALE * x
        alpha = norm_now / inner(direction, image)
        for i, x in enumerate(direction):
            total[i] = total[i] + alpha * x
        if step + 1 < ITERS:
            resid = [r - alpha * q for r, q in zip(resid + [zero], image)]
            norm_next = inner(resid, resid)
            beta = norm_next / norm_now
            direction = [r + beta * p for r, p in zip(resid, direction + [zero])]
            norm_now = norm_next
    return total


def combine(rows_ref, basis_ref, out_ref):
    moments = jnp.sum(rows_ref[...], axis=0)
    total = coefficients([moments[:, k : k + 1] for k in range(len(PAIRS))])
    out_ref[...] = total[0] * basis_ref[0] + total[1] * basis_ref[1] + total[2] * basis_ref[2]


def shape_of(*dims):
    return jax.ShapeDtypeStruct(dims, jnp.float32)


def whole(x):
    return pl.BlockSpec(x.shape, lambda *_: (0,) * len(x.shape))


def block(shape, *index):
    return pl.BlockSpec(shape, lambda *_: index)


def swaps(count, start):
    both = [(i, i + 1) for i in range(start, count - 1, 2)]
    both += [(b, a) for a, b in both]
    return both, sorted(set(range(count)) - {a for a, _ in both})


def across_route(across, start):
    both, alone = swaps(across, start)
    return both + list(zip(alone, alone[::-1]))


def along_route(along, across, start):
    both, alone = swaps(along, start)
    route = [(a * across + i, b * across + i) for a, b in both for i in range(across)]
    side = dict(across_route(across, 0))
    return route + [(a * across + i, a * across + side[i]) for a in alone for i in range(across)]


def local(t, s, u, v, x, y, source, depth, main):
    layers, rows, columns = t.shape
    across, along = lax.axis_size("by"), lax.axis_size("bx")
    strip = rows // across
    names = ("bx", "by")
    params = pltpu.CompilerParams(vmem_limit_bytes=48 << 20)

    call = functools.partial(pl.pallas_call, compiler_params=params)

    hbm = pl.BlockSpec(memory_space=pltpu.HBM)
    wide = ITERS - 1
    pack = shape_of(rows, LANE)
    more = shape_of(rows + wide * (columns * across // LANE), LANE)
    first, even, odd = call(
        pack_edges,
        grid=(1,),
        in_specs=[hbm] * 6,
        out_specs=[whole(pack), whole(more), whole(more)],
        out_shape=[pack, more, more],
        scratch_shapes=[
            pltpu.VMEM((6, layers, rows, LANE), jnp.float32),
            pltpu.VMEM((2, rows, LANE), jnp.int32),
            pltpu.VMEM(main.shape, jnp.float32),
            pltpu.SemaphoreType.DMA((15,)),
        ],
    )(*(pltpu.with_memory_space_constraint(a, pltpu.HBM) for a in (t, s, v, y, depth, main)))
    from_even = lax.ppermute(even, "by", across_route(across, 0))
    from_odd = lax.ppermute(odd, "by", across_route(across, 1))

    fields = (t, s, u, v, x, y, source)
    extra = -(-wide * across // SUB)
    sides = shape_of(rows, 2 * LANE)
    near = shape_of(6 * layers + 3, SUB, columns)
    shared = layers + 2 * layers // SUB
    rim = shape_of(shared + 1 + extra, SUB, columns)
    near, even, odd = call(
        functools.partial(gather_rows, across),
        grid=(1,),
        in_specs=[hbm] * 8 + [whole(main)],
        out_specs=[whole(near), whole(rim), whole(rim)],
        out_shape=[near, rim, rim],
        scratch_shapes=[
            pltpu.VMEM((6 * layers + 2, 2 * SUB, columns), jnp.float32),
            pltpu.VMEM((2 * SUB, columns), depth.dtype),
            pltpu.SemaphoreType.DMA((16,)),
        ],
    )(*(pltpu.with_memory_space_constraint(a, pltpu.HBM) for a in (*fields, depth)), main)

    plane = shape_of(rows, columns)
    args = (first, from_odd, from_even, near)
    tile = block((1, SUB, columns), shared, 0, 0)
    edge, even, odd = call(
        pack_rows,
        grid=(1,),
        in_specs=[whole(a) for a in args] + [tile] * 2,
        out_specs=[whole(sides), tile, tile],
        out_shape=[sides, rim, rim],
        input_output_aliases={4: 1, 5: 2},
    )(*args, even, odd)
    odd_in = lax.ppermute(odd, names, along_route(along, across, 1))
    even_in = lax.ppermute(even, names, along_route(along, across, 0))

    cube = shape_of(layers, rows, columns)
    args = (*fields, depth, edge)
    warm, salt, forcing = call(
        inner_tile,
        grid=(1,),
        in_specs=[whole(a) for a in args],
        out_specs=[whole(cube), whole(cube), whole(plane)],
        out_shape=[cube, cube, plane],
    )(*args)

    tall = -(-(strip + 2 * ITERS) // SUB) * SUB
    part = shape_of(tall + extra * SUB, columns)
    fix = shape_of(layers, SUB, columns)
    fix_t, fix_s, *sends = call(
        functools.partial(rim_rows, across),
        grid=(1,),
        in_specs=[whole(rim)] * 4 + [whole(plane)],
        out_specs=[whole(fix)] * 2 + [whole(part)] * across,
        out_shape=[fix] * 2 + [part] * across,
        scratch_shapes=[
            pltpu.VMEM((rows + 2 * SUB, columns), jnp.float32),
            pltpu.VMEM((across,) + part.shape, jnp.float32),
        ],
    )(even, odd, odd_in, even_in, forcing)

    came = [sends[0]]
    for hop in range(1, across):
        route = [(i, hop_peer(i, hop, across)) for i in range(across)]
        came.append(lax.ppermute(sends[hop], "by", route))

    args = (fix_t, fix_s, warm, salt)
    warm, salt = call(
        flush,
        grid=(1,),
        in_specs=[whole(a) for a in args],
        out_specs=[hbm] * 2,
        out_shape=[cube] * 2,
        scratch_shapes=[
            pltpu.VMEM((4, layers, SUB, columns), jnp.float32),
            pltpu.SemaphoreType.DMA((layers + 4,)),
        ],
    )(*args)

    basis_shape = shape_of(ITERS, strip, columns * across)
    row_shape = shape_of(across * along, 1, LANE)
    ready = shape_of(tall, columns * across)
    args = (from_even, from_odd, main)
    ready = call(
        main_rows,
        grid=(1,),
        in_specs=[whole(a) for a in args],
        out_specs=whole(ready),
        out_shape=ready,
    )(*args)
    ready, warm, salt = lax.optimization_barrier((ready, warm, salt))
    args = (came[0], *came[:0:-1], ready)
    basis, row = call(
        functools.partial(powers, across, along),
        grid=(1,),
        in_specs=[whole(a) for a in args],
        out_specs=[whole(basis_shape), whole(row_shape)],
        out_shape=[basis_shape, row_shape],
        scratch_shapes=[pltpu.VMEM((tall, columns * across), jnp.float32)] * 2,
    )(*args)
    gathered = lax.all_to_all(row, names, 0, 0, tiled=True)
    result = shape_of(strip, columns * across)
    pressure = call(
        combine,
        grid=(1,),
        in_specs=[whole(gathered), whole(basis)],
        out_specs=whole(result),
        out_shape=result,
    )(gathered, basis)
    return warm, salt, pressure


def solution(mesh):
    tile = P(None, "bx", "by")
    rows = P(("bx", "by"), None)
    return jax.shard_map(
        local,
        mesh=mesh,
        in_specs=(tile,) * 7 + (P("bx", "by"), rows),
        out_specs=(tile, tile, rows),
        check_vma=False,
    )
```

```python
import functools
import math

import jax
import jax.numpy as jnp
from jax import lax
from jax.experimental import pallas as pl
from jax.experimental.pallas import tpu as pltpu
from jax.sharding import PartitionSpec as P

ITERS = 3
CENTRE = 4.5
SCALE = 4.5
DEEP = ITERS + 1
SUB = 8
LANE = 128
PAIRS = ((0, 0), (0, 1), (1, 1), (1, 2), (2, 2), (2, 3))


def iota(shape, dim):
    return lax.broadcasted_iota(jnp.int32, shape, dim)


def below(x):
    return pltpu.roll(x, x.shape[0] - 1, 0)


def above(x):
    return pltpu.roll(x, 1, 0)


def left_by(x, lanes):
    return pltpu.roll(x, x.shape[1] - lanes, 1)


def pack_edges(t, s, v, y, depth, main, first_ref, even_ref, odd_ref, cubes, planes, lines, sems):
    layers, rows, columns = t.shape
    cells = 2 * layers
    wide = ITERS - 1
    head, tail = pl.ds(0, LANE), pl.ds(columns - LANE, LANE)
    moves = []
    for low in range(0, layers, layers // 2):
        some = pl.ds(low, layers // 2)
        for i, (ref, where) in enumerate(((t, tail), (s, tail), (v, tail), (y, tail), (t, head), (s, head))):
            moves.append((ref.at[some, :, where], cubes.at[i, some]))
    moves += [(depth.at[:, tail], planes.at[0]), (depth.at[:, head], planes.at[1]), (main, lines)]
    copies = [pltpu.make_async_copy(a, b, sems.at[i]) for i, (a, b) in enumerate(moves)]
    for copy in copies:
        copy.start()
    for copy in copies:
        copy.wait()
    lane = iota((rows, LANE), 1)
    first = jnp.zeros((rows, LANE), jnp.float32)
    last = jnp.zeros((rows, LANE), jnp.float32)
    edge = LANE - 1
    for k in range(layers):
        first = jnp.where(lane == k, cubes[4, k][:, 0:1], first)
        first = jnp.where(lane == layers + k, cubes[5, k][:, 0:1], first)
        last = jnp.where(lane == k, cubes[0, k][:, edge:], last)
        last = jnp.where(lane == layers + k, cubes[1, k][:, edge:], last)
        two = (lane == cells + k) | (lane == cells + layers + k)
        last = jnp.where(two, cubes[2, k][:, edge:], last)
        two = (lane == 2 * cells + k) | (lane == 2 * cells + layers + k)
        last = jnp.where(two, cubes[3, k][:, edge:], last)
    span = (lane >= 3 * cells) & (lane < 4 * cells)
    first = jnp.where(span, planes[1][:, 0:1].astype(jnp.float32), first)
    last = jnp.where(span, planes[0][:, edge:].astype(jnp.float32), last)
    first_ref[...] = first
    even = lax.axis_index("by") % 2 == 0
    even_ref[:rows, :] = jnp.where(even, last, first)
    odd_ref[:rows, :] = jnp.where(even, first, last)
    strip = lines.shape[0]
    parts = lines.shape[1] // LANE
    for r in range(wide):
        for j in range(parts):
            here = slice(j * LANE, (j + 1) * LANE)
            up = lines[r : r + 1, here]
            down = lines[strip - wide + r : strip - wide + r + 1, here]
            at = rows + r * parts + j
            even_ref[at : at + 1, :] = jnp.where(even, down, up)
            odd_ref[at : at + 1, :] = jnp.where(even, up, down)


def gather_rows(across, *refs):
    fields, depth, main = refs[:7], refs[7], refs[8]
    near, even_ref, odd_ref, raw, raw_depth, sems = refs[9:]
    layers, rows = fields[0].shape[:2]
    copies = []
    at = 0
    for ref in fields:
        for i, start in enumerate((0, rows - SUB)):
            planes = raw.at[pl.ds(at, ref.shape[0]), pl.ds(i * SUB, SUB)]
            copies.append((ref.at[:, pl.ds(start, SUB)], planes))
        at += ref.shape[0]
    for i, start in enumerate((0, rows - SUB)):
        copies.append((depth.at[pl.ds(start, SUB)], raw_depth.at[pl.ds(i * SUB, SUB)]))
    copies = [pltpu.make_async_copy(a, b, sems.at[i]) for i, (a, b) in enumerate(copies)]
    for copy in copies:
        copy.start()
    for copy in copies:
        copy.wait()
    base = 6 * layers
    planes = [(raw[p, :SUB], raw[p, SUB:]) for p in range(base + 2)]
    levels = raw_depth[...].astype(jnp.float32)
    planes.append((levels[:SUB], levels[SUB:]))
    line = iota(planes[0][0].shape, 0)
    for p, (up, down) in enumerate(planes):
        near[p] = jnp.where(line < SUB // 2, up, down)
    even = lax.axis_index("bx") % 2 == 0

    mine = row_planes(layers)
    begin = 2 * layers // SUB + 1
    for q in range(len(mine) // SUB):
        put_rows(even_ref, odd_ref, begin + q, [planes[p] for p in mine[q * SUB : (q + 1) * SUB]], even)
    count = begin + len(mine) // SUB
    wide = ITERS - 1
    strip = main.shape[0]
    width = fields[0].shape[2]
    for r in range(wide):
        for j in range(across):
            here = slice(j * width, (j + 1) * width)
            up = main[r : r + 1, here]
            down = main[strip - wide + r : strip - wide + r + 1, here]
            q, at = divmod(r * across + j, SUB)
            even_ref[count + q, at : at + 1, :] = jnp.where(even, down, up)
            odd_ref[count + q, at : at + 1, :] = jnp.where(even, up, down)


def put_rows(even_ref, odd_ref, q, planes, even):
    line = iota(planes[0][0].shape, 0)
    out_even, out_odd = None, None
    for j, (up, down) in enumerate(planes):
        up = pltpu.roll(up, j, 0) if j else up
        down = pltpu.roll(down, (j + 1) % SUB, 0) if (j + 1) % SUB else down
        one, two = jnp.where(even, down, up), jnp.where(even, up, down)
        out_even = one if j == 0 else jnp.where(line >= j, one, out_even)
        out_odd = two if j == 0 else jnp.where(line >= j, two, out_odd)
    even_ref[q] = out_even
    odd_ref[q] = out_odd


def row_planes(layers):
    return [kind * layers + k for kind in (0, 1, 5, 2, 4) for k in range(layers)]


def pack_rows(first_ref, from_odd, from_even, near, even_in, odd_in, edge_ref, even_ref, odd_ref):
    rows, half = first_ref.shape[0], LANE // 2
    base = near.shape[0] - 3
    layers = base // 6
    even = lax.axis_index("by") % 2 == 0
    lane = iota((rows, LANE), 1)
    a, b = from_even[:rows, :], from_odd[:rows, :]
    left, right = jnp.where(even, b, a), jnp.where(even, a, b)
    me = lax.axis_index("by")
    left = jnp.where(me == 0, 0.0, left)
    right = jnp.where(me == lax.axis_size("by") - 1, 0.0, right)
    left = jnp.where(lane < half, left, pltpu.roll(first_ref[...], half, 1))
    edge_ref[:, :LANE] = left
    edge_ref[:, LANE:] = right
    head, tail = edge_ref[:SUB, :], edge_ref[rows - SUB :, :]
    line = iota(head.shape, 0)
    depth = near[base + 2]
    stars = stars_of(
        lambda kind, k: near[kind * layers + k],
        [near[base], near[base + 1]],
        depth,
        jnp.where(line < SUB // 2, head, tail),
        layers,
        True,
    )
    _, _, forcing = solve_columns(stars, depth, layers)
    even = lax.axis_index("bx") % 2 == 0
    both = stars[0] + stars[1]
    for q in range(len(both) // SUB):
        put_rows(even_ref, odd_ref, q, [(p, p) for p in both[q * SUB : (q + 1) * SUB]], even)
    up = jnp.where(line < 1, depth, jnp.where(line < 2, pltpu.roll(head, 1, 0), pltpu.roll(forcing, 1, 0)))
    down = jnp.where(line < 2, pltpu.roll(tail, 2, 0), pltpu.roll(forcing, 5, 0))
    down = jnp.where(line < 1, pltpu.roll(depth, 1, 0), down)
    q = len(both) // SUB
    even_ref[q] = jnp.where(even, down, up)
    odd_ref[q] = jnp.where(even, up, down)


def edge_cells(edge, layers):
    rows = edge.shape[0]
    cells = 2 * layers
    level = (iota((rows, LANE), 1) % layers).astype(jnp.float32)
    left, right = edge[:, :LANE], edge[:, LANE:]
    wet_left = level < left_by(left, 3 * cells)
    wet_own = level < left_by(left, LANE // 2 + 3 * cells)
    wet_right = level < left_by(right, 3 * cells)
    cell_left = jnp.where(wet_left, left, 0.0)
    cell_own = jnp.where(wet_own, left_by(left, LANE // 2), 0.0)
    cell_right = jnp.where(wet_right, right, 0.0)
    return cell_left, cell_own, cell_right, wet_left & wet_own


def column_shifts(shape):
    lane = iota(shape, 1)
    first, last = lane == 0, lane == shape[1] - 1

    def after(x, fill):
        return jnp.where(last, fill, left_by(x, 1))

    def before(x, fill):
        return jnp.where(first, fill, pltpu.roll(x, 1, 1))

    return after, before


def stars_of(get, source, depth, edge, layers, open_ends):
    cells = 2 * layers
    after, before = column_shifts(depth.shape)

    def under(x):
        y = below(x)
        return jnp.where(iota(x.shape, 0) == x.shape[0] - 1, 0.0, y) if open_ends else y

    def over(x):
        y = above(x)
        return jnp.where(iota(x.shape, 0) == 0, 0.0, y) if open_ends else y

    left, right = edge[:, :LANE], edge[:, LANE:]
    cell_left, cell_own, cell_right, wet_both = edge_cells(edge, layers)
    slope_left = under(cell_left) - over(cell_left)
    slope_own = under(cell_own) - over(cell_own)
    slope_right = under(cell_right) - over(cell_right)
    flux_left = left_by(left, cells) * 0.5 * (cell_left + cell_own) - 0.15 * (
        cell_own - cell_left + left_by(left, 2 * cells) * 0.25 * (slope_left + slope_own)
    )
    flux_left = jnp.where(wet_both, flux_left, 0.0)
    depth_right = right[:, 3 * cells : 3 * cells + 1]
    depth_east = jnp.minimum(depth, under(depth))
    depth_north = jnp.minimum(depth, after(depth, depth_right))
    stars = ([], [])
    for k in range(layers):
        wet = depth > k
        mask = depth_east > k
        half = 0.5 * get(2, k)
        e_here = jnp.where(mask, half + 0.15, 0.0)
        e_next = jnp.where(mask, half - 0.15, 0.0)
        e_cross = jnp.where(mask, 0.0375 * get(4, k), 0.0)
        mask = depth_north > k
        half = 0.5 * get(3, k)
        n_here = jnp.where(mask, half + 0.15, 0.0)
        n_next = jnp.where(mask, half - 0.15, 0.0)
        n_cross = jnp.where(mask, 0.0375 * get(5, k), 0.0)
        for t in range(2):
            one = slice(t * layers + k, t * layers + k + 1)
            cell = jnp.where(wet, get(t, k), 0.0)
            east, west = under(cell), over(cell)
            north = after(cell, cell_right[:, one])
            south = before(cell, cell_left[:, one])
            cross = north - south
            flux = e_here * cell + e_next * east - e_cross * (cross + below(cross))
            star = cell - (flux - above(flux))
            cross = east - west
            cross = cross + after(cross, slope_right[:, one])
            flux = n_here * cell + n_next * north - n_cross * cross
            star = star - (flux - before(flux, flux_left[:, one]))
            if k == 0:
                star = star + source[t]
            stars[t].append(jnp.where(wet, star, 0.0))
    return stars


def joined_stars(part, cells_of, east_speed, east_slope, north_slope, depth, edge, upper, layers):
    cells = 2 * layers
    after, before = column_shifts(depth.shape)
    is_upper = upper(depth.shape)
    pack_upper = upper((depth.shape[0], LANE))

    def other(x, mine):
        return jnp.where(mine, below(x), above(x))

    left, right = edge[:, :LANE], edge[:, LANE:]
    cell_left, cell_own, cell_right, wet_both = edge_cells(edge, layers)
    cross_left = 0.0375 * left_by(left, 2 * cells)
    cross_left = cross_left * (other(cell_left, pack_upper) + other(cell_own, pack_upper))
    cross_left = jnp.where(wet_both, cross_left, 0.0)
    other_right = other(cell_right, pack_upper)
    depth_east = jnp.minimum(depth, below(depth))
    depth_north = jnp.minimum(depth, after(depth, right[:, 3 * cells : 3 * cells + 1]))
    stars = ([], [])
    for k in range(layers):
        wet = depth > k
        mask = depth_east > k
        half = 0.5 * east_speed[k]
        e_here = jnp.where(mask, half + 0.15, 0.0)
        e_next = jnp.where(mask, half - 0.15, 0.0)
        e_cross = jnp.where(mask, 0.0375 * east_slope[k], 0.0)
        n_cross = jnp.where(depth_north > k, 0.0375 * north_slope[k], 0.0)
        for t in range(2):
            one = slice(t * layers + k, t * layers + k + 1)
            cell = jnp.where(wet, cells_of[t][k], 0.0)
            east = below(cell)
            cross = after(cell, cell_right[:, one]) - before(cell, cell_left[:, one])
            flux = e_here * cell + e_next * east - e_cross * (cross + below(cross))
            beyond = jnp.where(is_upper, east, above(cell))
            cross = n_cross * (beyond + after(beyond, other_right[:, one]))
            cross = cross - before(cross, cross_left[:, one])
            gain = jnp.where(is_upper, cross - flux, above(flux) - cross)
            stars[t].append(jnp.where(wet, part[t][k] + gain, 0.0))
    return stars


def solve_columns(stars, depth, layers):
    primes, rights = [], ([], [])
    upper = None
    density = 0.8 * stars[1][0] - 0.2 * stars[0][0]
    for k in range(layers):
        if k + 1 < layers:
            deeper = 0.8 * stars[1][k + 1] - 0.2 * stars[0][k + 1]
            couple = 0.05 + 1.0 / (1.0 + 10.0 * jnp.maximum(deeper - density, 0.0))
            couple = jnp.where(depth > k + 1, couple, 0.0)
            density = deeper
        else:
            couple = None
        if k == 0:
            inverse = 1.0 / (1.0 + couple)
        elif couple is not None:
            inverse = 1.0 / (1.0 + upper + couple - upper * primes[-1])
        else:
            inverse = 1.0 / (1.0 + upper - upper * primes[-1])
        for t in range(2):
            value = stars[t][k]
            if k:
                value = value + upper * rights[t][-1]
            rights[t].append(value * inverse)
        if couple is not None:
            primes.append(couple * inverse)
        upper = couple
    fresh = ([None] * layers, [None] * layers)
    forcing = None
    solved = [rights[0][-1], rights[1][-1]]
    for k in range(layers - 1, -1, -1):
        wet = depth > k
        for t in range(2):
            if k < layers - 1:
                solved[t] = rights[t][k] + primes[k] * solved[t]
            fresh[t][k] = jnp.where(wet, solved[t], 0.0)
        part = 0.8 * fresh[1][k] - 0.2 * fresh[0][k]
        forcing = part if forcing is None else forcing + part
    return fresh[0], fresh[1], forcing * (4.0 / math.sqrt(layers))


def inner_tile(t, s, u, v, x, y, source, depth, edge, t_out, s_out, f_out):
    layers = t.shape[0]
    refs = (t, s, u, v, x, y)
    levels = depth[...].astype(jnp.float32)
    stars = stars_of(
        lambda kind, k: refs[kind][k], [source[0], source[1]], levels, edge[...], layers, False
    )
    warm, salt, forcing = solve_columns(stars, levels, layers)
    for k in range(layers):
        t_out[k] = warm[k]
        s_out[k] = salt[k]
    f_out[...] = forcing


def rim_rows(across, even_out, odd_out, odd_in, even_in, f_old, *refs):
    layers = refs[0].shape[0]
    t_fix, s_fix = refs[:2]
    sends, (field, blocks) = refs[2 : 2 + across], refs[2 + across :]
    rows = f_old.shape[0]
    strip = rows // across
    even = lax.axis_index("bx") % 2 == 0
    me = lax.axis_index("by")
    shape = (SUB, f_old.shape[1])
    line = iota(shape, 0)

    def parts(q):
        sent_even, sent_odd, came_even, came_odd = even_out[q], odd_out[q], even_in[q], odd_in[q]
        four = [jnp.where(even, came_odd, came_even), jnp.where(even, sent_odd, sent_even)]
        return four + [jnp.where(even, sent_even, sent_odd), jnp.where(even, came_even, came_odd)]

    def take(four, at):
        total = None
        for i, (part, place) in enumerate(zip(four, (1, 2, 5, 6))):
            part = part if place == at else pltpu.roll(part, (place - at) % SUB, 0)
            total = part if i == 0 else jnp.where(line >= 2 * i, part, total)
        return total

    def rows_from(q, count):
        out = []
        for i in range(count):
            if i % SUB == 0:
                four = parts(q + i // SUB)
            out.append(take(four, i % SUB))
        return out

    ahead = 2 * layers // SUB
    part = rows_from(0, 2 * layers)
    planes = rows_from(ahead + 1, 5 * layers)
    four = parts(ahead)
    me_along = lax.axis_index("bx")
    four[0] = jnp.where(me_along == 0, 0.0, four[0])
    four[3] = jnp.where(me_along == lax.axis_size("bx") - 1, 0.0, four[3])
    depth, edge = take(four, 0), take(four, 1)
    over, under = pltpu.roll(four[0], 3, 0), pltpu.roll(four[3], 7, 0)
    kinds = [planes[i * layers : (i + 1) * layers] for i in range(5)]

    def upper(shape):
        row = iota(shape, 0)
        return (row == 1) | (row == 5)

    stars = joined_stars(
        (part[:layers], part[layers:]),
        (kinds[0], kinds[1]),
        kinds[3],
        kinds[4],
        kinds[2],
        depth,
        edge,
        upper,
        layers,
    )
    warm, salt, forcing = solve_columns(stars, depth, layers)
    for fix, fresh in ((t_fix, warm), (s_fix, salt)):
        for k in range(layers):
            fix[k] = jnp.where(line == 0, pltpu.roll(fresh[k], 6, 0), pltpu.roll(fresh[k], 2, 0))
    top, bottom = pltpu.roll(forcing, 6, 0), pltpu.roll(forcing, 2, 0)
    last = SUB - 1
    field[:SUB, :] = jnp.where(line == last, top, over)
    field[SUB : 2 * SUB, :] = jnp.where(line == 0, top, f_old[:SUB, :])
    field[2 * SUB : rows, :] = f_old[SUB : rows - SUB, :]
    field[rows : rows + SUB, :] = jnp.where(line == last, bottom, f_old[rows - SUB :, :])
    field[SUB + rows : 2 * SUB + rows, :] = jnp.where(line == 0, bottom, under)
    later = ahead + 1 + 5 * layers // SUB
    extra = even_out.shape[0] - later
    tall = blocks.shape[1] - extra * SUB
    for peer in range(across):
        start = SUB - ITERS + peer * strip
        stop = min(start + tall, field.shape[0])
        blocks[peer, : stop - start, :] = field[start:stop, :]
    use_even = even == (me == 0)
    for q in range(extra):
        relay = jnp.where(use_even, even_in[later + q], odd_in[later + q])
        for peer in range(across):
            blocks[peer, tall + q * SUB : tall + (q + 1) * SUB, :] = relay
    for hop in range(across):
        sends[hop][...] = blocks[hop_peer(me, hop, across)]


def main_rows(from_even, from_odd, main_own, out):
    strip, columns = main_own.shape
    wide = ITERS - 1
    out[...] = jnp.zeros(out.shape, jnp.float32)
    out[ITERS : ITERS + strip, :] = main_own[...]
    over, under = ITERS - wide, ITERS + strip
    even = lax.axis_index("by") % 2 == 0
    parts = columns // LANE
    begin = from_even.shape[0] - wide * parts
    for r in range(wide):
        for j in range(parts):
            here = slice(j * LANE, (j + 1) * LANE)
            at = begin + r * parts + j
            a, b = from_even[at : at + 1, :], from_odd[at : at + 1, :]
            out[over + r : over + r + 1, here] = jnp.where(even, b, a)
            out[under + r : under + r + 1, here] = jnp.where(even, a, b)


def flush(fix_t, fix_s, t_mid, s_mid, t_out, s_out, ends, sems):
    layers, rows, columns = t_mid.shape
    inner = pl.ds(SUB, rows - 2 * SUB)
    copies = []

    def begin(source, target):
        copies.append(pltpu.make_async_copy(source, target, sems.at[len(copies)]))
        copies[-1].start()

    for mid, out in ((t_mid, t_out), (s_mid, s_out)):
        for low in range(0, layers, 2):
            some = pl.ds(low, 2)
            begin(mid.at[some, inner], out.at[some, inner])
    line = iota((layers, SUB, columns), 1)
    for i, (mid, fix, out) in enumerate(((t_mid, fix_t, t_out), (s_mid, fix_s, s_out))):
        for j, (start, at) in enumerate(((0, 0), (rows - SUB, SUB - 1))):
            old = mid[:, start : start + SUB, :]
            ends[2 * i + j] = jnp.where(line == at, fix[...], old)
            begin(ends.at[2 * i + j], out.at[:, pl.ds(start, SUB)])
    for copy in copies:
        copy.wait()


def hop_peer(me, hop, count):
    if count & (count - 1) == 0:
        return me ^ hop
    return (me + hop) % count


def hop_origin(me, hop, count):
    if count & (count - 1) == 0:
        return me ^ hop
    return (me + count - hop) % count


def powers(across, along, *refs):
    came = [refs[0], *refs[1:across][::-1]]
    main_in, basis_ref, row_ref, field, main = refs[across:]
    tall, columns = main_in.shape
    strip = basis_ref.shape[1]
    width = columns // across
    me = lax.axis_index("by")
    for hop in range(across):
        origin = hop_origin(me, hop, across)
        field[:, pl.ds(pl.multiple_of(origin * width, LANE), width)] = came[hop][:tall, :]
    wide = ITERS - 1
    main[...] = main_in[...]

    def relayed(start, mine, sender):
        hop = [h for h in range(across) if hop_origin(mine, h, across) == sender][0]

        @pl.when(me == mine)
        def _():
            for r in range(wide):
                for j in range(across):
                    at = tall + r * across + j
                    here = slice(j * width, (j + 1) * width)
                    main[start + r : start + r + 1, here] = came[hop][at : at + 1, :]

    relayed(ITERS - wide, 0, across - 1)
    relayed(ITERS + strip, across - 1, 0)
    shape = (tall, columns)
    lane = iota(shape, 1)
    line = (lax.axis_index("bx") * across + me) * strip - ITERS + iota(shape, 0)
    inside = (line >= 0) & (line < along * across * strip)
    first, last = lane == 0, lane == columns - 1
    centre = (main[...] + (6.0 - CENTRE)) * (1.0 / SCALE)
    centre = jnp.where(inside, centre, 0.0)
    share = jnp.where(inside, -1.0 / SCALE, 0.0)
    now = field[...]
    own = [now[ITERS : ITERS + strip]]
    for _ in range(ITERS):
        beside = below(now) + above(now)
        spread = now + 0.5 * beside
        east = jnp.where(last, 0.0, left_by(spread, 1))
        west = jnp.where(first, 0.0, pltpu.roll(spread, 1, 1))
        now = centre * now + share * (beside + east + west)
        own.append(now[ITERS : ITERS + strip])
    for k in range(ITERS):
        basis_ref[k] = own[k]
    place = iota((1, LANE), 1)
    row = jnp.zeros((1, LANE), jnp.float32)
    for k, (i, j) in enumerate(PAIRS):
        part = jnp.sum(own[i] * own[j], axis=0, keepdims=True)
        row = jnp.where(place == k, jnp.sum(part, axis=1, keepdims=True), row)
    row_ref[...] = jnp.broadcast_to(row[None], row_ref.shape)


def coefficients(moments):
    def inner(a, b):
        return sum(x * y * moments[i + j] for i, x in enumerate(a) for j, y in enumerate(b))

    zero = jnp.zeros_like(moments[0])
    resid = [zero + 1.0]
    direction = [zero + 1.0]
    total = [zero] * ITERS
    norm_now = inner(resid, resid)
    for step in range(ITERS):
        image = [zero] * (len(direction) + 1)
        for i, x in enumerate(direction):
            image[i] = image[i] + CENTRE * x
            image[i + 1] = image[i + 1] + SCALE * x
        alpha = norm_now / inner(direction, image)
        for i, x in enumerate(direction):
            total[i] = total[i] + alpha * x
        if step + 1 < ITERS:
            resid = [r - alpha * q for r, q in zip(resid + [zero], image)]
            norm_next = inner(resid, resid)
            beta = norm_next / norm_now
            direction = [r + beta * p for r, p in zip(resid, direction + [zero])]
            norm_now = norm_next
    return total


def combine(rows_ref, basis_ref, out_ref):
    moments = jnp.sum(rows_ref[...], axis=0)
    total = coefficients([moments[:, k : k + 1] for k in range(len(PAIRS))])
    out_ref[...] = total[0] * basis_ref[0] + total[1] * basis_ref[1] + total[2] * basis_ref[2]


def shape_of(*dims):
    return jax.ShapeDtypeStruct(dims, jnp.float32)


def whole(x):
    return pl.BlockSpec(x.shape, lambda *_: (0,) * len(x.shape))


def block(shape, *index):
    return pl.BlockSpec(shape, lambda *_: index)


def swaps(count, start):
    both = [(i, i + 1) for i in range(start, count - 1, 2)]
    both += [(b, a) for a, b in both]
    return both, sorted(set(range(count)) - {a for a, _ in both})


def across_route(across, start):
    both, alone = swaps(across, start)
    return both + list(zip(alone, alone[::-1]))


def along_route(along, across, start):
    both, alone = swaps(along, start)
    route = [(a * across + i, b * across + i) for a, b in both for i in range(across)]
    side = dict(across_route(across, 0))
    return route + [(a * across + i, a * across + side[i]) for a in alone for i in range(across)]


def local(t, s, u, v, x, y, source, depth, main):
    layers, rows, columns = t.shape
    across, along = lax.axis_size("by"), lax.axis_size("bx")
    strip = rows // across
    names = ("bx", "by")
    params = pltpu.CompilerParams(vmem_limit_bytes=48 << 20)

    call = functools.partial(pl.pallas_call, compiler_params=params)

    hbm = pl.BlockSpec(memory_space=pltpu.HBM)
    wide = ITERS - 1
    pack = shape_of(rows, LANE)
    more = shape_of(rows + wide * (columns * across // LANE), LANE)
    first, even, odd = call(
        pack_edges,
        grid=(1,),
        in_specs=[hbm] * 6,
        out_specs=[whole(pack), whole(more), whole(more)],
        out_shape=[pack, more, more],
        scratch_shapes=[
            pltpu.VMEM((6, layers, rows, LANE), jnp.float32),
            pltpu.VMEM((2, rows, LANE), jnp.int32),
            pltpu.VMEM(main.shape, jnp.float32),
            pltpu.SemaphoreType.DMA((15,)),
        ],
    )(*(pltpu.with_memory_space_constraint(a, pltpu.HBM) for a in (t, s, v, y, depth, main)))
    from_even = lax.ppermute(even, "by", across_route(across, 0))
    from_odd = lax.ppermute(odd, "by", across_route(across, 1))

    fields = (t, s, u, v, x, y, source)
    extra = -(-wide * across // SUB)
    sides = shape_of(rows, 2 * LANE)
    near = shape_of(6 * layers + 3, SUB, columns)
    shared = 2 * layers // SUB + 1
    rim = shape_of(shared + 5 * layers // SUB + extra, SUB, columns)
    near, even, odd = call(
        functools.partial(gather_rows, across),
        grid=(1,),
        in_specs=[hbm] * 8 + [whole(main)],
        out_specs=[whole(near), whole(rim), whole(rim)],
        out_shape=[near, rim, rim],
        scratch_shapes=[
            pltpu.VMEM((6 * layers + 2, 2 * SUB, columns), jnp.float32),
            pltpu.VMEM((2 * SUB, columns), depth.dtype),
            pltpu.SemaphoreType.DMA((16,)),
        ],
    )(*(pltpu.with_memory_space_constraint(a, pltpu.HBM) for a in (*fields, depth)), main)

    plane = shape_of(rows, columns)
    args = (first, from_odd, from_even, near)
    tile = block((shared, SUB, columns), 0, 0, 0)
    edge, even, odd = call(
        pack_rows,
        grid=(1,),
        in_specs=[whole(a) for a in args] + [tile] * 2,
        out_specs=[whole(sides), tile, tile],
        out_shape=[sides, rim, rim],
        input_output_aliases={4: 1, 5: 2},
    )(*args, even, odd)
    odd_in = lax.ppermute(odd, names, along_route(along, across, 1))
    even_in = lax.ppermute(even, names, along_route(along, across, 0))

    cube = shape_of(layers, rows, columns)
    args = (*fields, depth, edge)
    warm, salt, forcing = call(
        inner_tile,
        grid=(1,),
        in_specs=[whole(a) for a in args],
        out_specs=[whole(cube), whole(cube), whole(plane)],
        out_shape=[cube, cube, plane],
    )(*args)

    tall = -(-(strip + 2 * ITERS) // SUB) * SUB
    part = shape_of(tall + extra * SUB, columns)
    fix = shape_of(layers, SUB, columns)
    fix_t, fix_s, *sends = call(
        functools.partial(rim_rows, across),
        grid=(1,),
        in_specs=[whole(rim)] * 4 + [whole(plane)],
        out_specs=[whole(fix)] * 2 + [whole(part)] * across,
        out_shape=[fix] * 2 + [part] * across,
        scratch_shapes=[
            pltpu.VMEM((rows + 2 * SUB, columns), jnp.float32),
            pltpu.VMEM((across,) + part.shape, jnp.float32),
        ],
    )(even, odd, odd_in, even_in, forcing)

    came = [sends[0]]
    for hop in range(1, across):
        route = [(i, hop_peer(i, hop, across)) for i in range(across)]
        came.append(lax.ppermute(sends[hop], "by", route))

    args = (fix_t, fix_s, warm, salt)
    warm, salt = call(
        flush,
        grid=(1,),
        in_specs=[whole(a) for a in args],
        out_specs=[hbm] * 2,
        out_shape=[cube] * 2,
        scratch_shapes=[
            pltpu.VMEM((4, layers, SUB, columns), jnp.float32),
            pltpu.SemaphoreType.DMA((layers + 4,)),
        ],
    )(*args)

    basis_shape = shape_of(ITERS, strip, columns * across)
    row_shape = shape_of(across * along, 1, LANE)
    ready = shape_of(tall, columns * across)
    args = (from_even, from_odd, main)
    ready = call(
        main_rows,
        grid=(1,),
        in_specs=[whole(a) for a in args],
        out_specs=whole(ready),
        out_shape=ready,
    )(*args)
    ready, warm, salt = lax.optimization_barrier((ready, warm, salt))
    args = (came[0], *came[:0:-1], ready)
    basis, row = call(
        functools.partial(powers, across, along),
        grid=(1,),
        in_specs=[whole(a) for a in args],
        out_specs=[whole(basis_shape), whole(row_shape)],
        out_shape=[basis_shape, row_shape],
        scratch_shapes=[pltpu.VMEM((tall, columns * across), jnp.float32)] * 2,
    )(*args)
    gathered = lax.all_to_all(row, names, 0, 0, tiled=True)
    result = shape_of(strip, columns * across)
    pressure = call(
        combine,
        grid=(1,),
        in_specs=[whole(gathered), whole(basis)],
        out_specs=whole(result),
        out_shape=result,
    )(gathered, basis)
    return warm, salt, pressure


def solution(mesh):
    tile = P(None, "bx", "by")
    rows = P(("bx", "by"), None)
    return jax.shard_map(
        local,
        mesh=mesh,
        in_specs=(tile,) * 7 + (P("bx", "by"), rows),
        out_specs=(tile, tile, rows),
        check_vma=False,
    )
```

```python
import functools
import math

import jax
import jax.numpy as jnp
from jax import lax
from jax.experimental import pallas as pl
from jax.experimental.pallas import tpu as pltpu
from jax.sharding import PartitionSpec as P

ITERS = 3
CENTRE = 4.5
SCALE = 4.5
DEEP = ITERS + 1
SUB = 8
LANE = 128
PAIRS = ((0, 0), (0, 1), (1, 1), (1, 2), (2, 2), (2, 3))


def iota(shape, dim):
    return lax.broadcasted_iota(jnp.int32, shape, dim)


def below(x):
    return pltpu.roll(x, x.shape[0] - 1, 0)


def above(x):
    return pltpu.roll(x, 1, 0)


def left_by(x, lanes):
    return pltpu.roll(x, x.shape[1] - lanes, 1)


def pack_edges(t, s, v, y, depth, main, first_ref, even_ref, odd_ref, cubes, planes, lines, sems):
    layers, rows, columns = t.shape
    cells = 2 * layers
    wide = ITERS - 1
    head, tail = pl.ds(0, LANE), pl.ds(columns - LANE, LANE)
    moves = []
    for low in range(0, layers, layers // 2):
        some = pl.ds(low, layers // 2)
        for i, (ref, where) in enumerate(((t, tail), (s, tail), (v, tail), (y, tail), (t, head), (s, head))):
            moves.append((ref.at[some, :, where], cubes.at[i, some]))
    moves += [(depth.at[:, tail], planes.at[0]), (depth.at[:, head], planes.at[1]), (main, lines)]
    copies = [pltpu.make_async_copy(a, b, sems.at[i]) for i, (a, b) in enumerate(moves)]
    for copy in copies:
        copy.start()
    for copy in copies:
        copy.wait()
    lane = iota((rows, LANE), 1)
    first = jnp.zeros((rows, LANE), jnp.float32)
    last = jnp.zeros((rows, LANE), jnp.float32)
    edge = LANE - 1
    for k in range(layers):
        first = jnp.where(lane == k, cubes[4, k][:, 0:1], first)
        first = jnp.where(lane == layers + k, cubes[5, k][:, 0:1], first)
        last = jnp.where(lane == k, cubes[0, k][:, edge:], last)
        last = jnp.where(lane == layers + k, cubes[1, k][:, edge:], last)
        two = (lane == cells + k) | (lane == cells + layers + k)
        last = jnp.where(two, cubes[2, k][:, edge:], last)
        two = (lane == 2 * cells + k) | (lane == 2 * cells + layers + k)
        last = jnp.where(two, cubes[3, k][:, edge:], last)
    span = (lane >= 3 * cells) & (lane < 4 * cells)
    first = jnp.where(span, planes[1][:, 0:1].astype(jnp.float32), first)
    last = jnp.where(span, planes[0][:, edge:].astype(jnp.float32), last)
    first_ref[...] = first
    even = lax.axis_index("by") % 2 == 0
    even_ref[:rows, :] = jnp.where(even, last, first)
    odd_ref[:rows, :] = jnp.where(even, first, last)
    strip = lines.shape[0]
    parts = lines.shape[1] // LANE
    for j in range(parts):
        here = slice(j * LANE, (j + 1) * LANE)
        up, down = lines[:wide, here], lines[strip - wide :, here]
        at = rows + j * wide
        even_ref[at : at + wide, :] = jnp.where(even, down, up)
        odd_ref[at : at + wide, :] = jnp.where(even, up, down)


def gather_rows(across, *refs):
    fields, depth, main = refs[:7], refs[7], refs[8]
    near, even_ref, odd_ref, raw, raw_depth, sems = refs[9:]
    layers, rows = fields[0].shape[:2]
    copies = []
    at = 0
    for ref in fields:
        for i, start in enumerate((0, rows - SUB)):
            planes = raw.at[pl.ds(at, ref.shape[0]), pl.ds(i * SUB, SUB)]
            copies.append((ref.at[:, pl.ds(start, SUB)], planes))
        at += ref.shape[0]
    for i, start in enumerate((0, rows - SUB)):
        copies.append((depth.at[pl.ds(start, SUB)], raw_depth.at[pl.ds(i * SUB, SUB)]))
    copies = [pltpu.make_async_copy(a, b, sems.at[i]) for i, (a, b) in enumerate(copies)]
    for copy in copies:
        copy.start()
    for copy in copies:
        copy.wait()
    base = 6 * layers
    planes = [(raw[p, :SUB], raw[p, SUB:]) for p in range(base + 2)]
    levels = raw_depth[...].astype(jnp.float32)
    planes.append((levels[:SUB], levels[SUB:]))
    line = iota(planes[0][0].shape, 0)
    for p, (up, down) in enumerate(planes):
        near[p] = jnp.where(line < SUB // 2, up, down)
    even = lax.axis_index("bx") % 2 == 0

    mine = row_planes(layers)
    begin = 2 * layers // SUB + 1
    for q in range(len(mine) // SUB):
        put_rows(even_ref, odd_ref, begin + q, [planes[p] for p in mine[q * SUB : (q + 1) * SUB]], even)
    count = begin + len(mine) // SUB
    wide = ITERS - 1
    strip = main.shape[0]
    width = fields[0].shape[2]
    for j in range(across):
        here = slice(j * width, (j + 1) * width)
        up, down = main[:wide, here], main[strip - wide :, here]
        q, at = divmod(j * wide, SUB)
        even_ref[count + q, at : at + wide, :] = jnp.where(even, down, up)
        odd_ref[count + q, at : at + wide, :] = jnp.where(even, up, down)


def put_rows(even_ref, odd_ref, q, planes, even):
    line = iota(planes[0][0].shape, 0)
    out_even, out_odd = None, None
    for j, (up, down) in enumerate(planes):
        up = pltpu.roll(up, j, 0) if j else up
        down = pltpu.roll(down, (j + 1) % SUB, 0) if (j + 1) % SUB else down
        one, two = jnp.where(even, down, up), jnp.where(even, up, down)
        out_even = one if j == 0 else jnp.where(line >= j, one, out_even)
        out_odd = two if j == 0 else jnp.where(line >= j, two, out_odd)
    even_ref[q] = out_even
    odd_ref[q] = out_odd


def row_planes(layers):
    return [kind * layers + k for kind in (0, 1, 5, 2, 4) for k in range(layers)]


def pack_rows(first_ref, from_odd, from_even, near, even_in, odd_in, edge_ref, even_ref, odd_ref):
    rows, half = first_ref.shape[0], LANE // 2
    base = near.shape[0] - 3
    layers = base // 6
    even = lax.axis_index("by") % 2 == 0
    lane = iota((rows, LANE), 1)
    a, b = from_even[:rows, :], from_odd[:rows, :]
    left, right = jnp.where(even, b, a), jnp.where(even, a, b)
    me = lax.axis_index("by")
    left = jnp.where(me == 0, 0.0, left)
    right = jnp.where(me == lax.axis_size("by") - 1, 0.0, right)
    left = jnp.where(lane < half, left, pltpu.roll(first_ref[...], half, 1))
    edge_ref[:, :LANE] = left
    edge_ref[:, LANE:] = right
    head, tail = edge_ref[:SUB, :], edge_ref[rows - SUB :, :]
    line = iota(head.shape, 0)
    depth = near[base + 2]
    stars = stars_of(
        lambda kind, k: near[kind * layers + k],
        [near[base], near[base + 1]],
        depth,
        jnp.where(line < SUB // 2, head, tail),
        layers,
        True,
    )
    _, _, forcing = solve_columns(stars, depth, layers)
    even = lax.axis_index("bx") % 2 == 0
    both = stars[0] + stars[1]
    for q in range(len(both) // SUB):
        put_rows(even_ref, odd_ref, q, [(p, p) for p in both[q * SUB : (q + 1) * SUB]], even)
    up = jnp.where(line < 1, depth, jnp.where(line < 2, pltpu.roll(head, 1, 0), pltpu.roll(forcing, 1, 0)))
    down = jnp.where(line < 2, pltpu.roll(tail, 2, 0), pltpu.roll(forcing, 5, 0))
    down = jnp.where(line < 1, pltpu.roll(depth, 1, 0), down)
    q = len(both) // SUB
    even_ref[q] = jnp.where(even, down, up)
    odd_ref[q] = jnp.where(even, up, down)


def edge_cells(edge, layers):
    rows = edge.shape[0]
    cells = 2 * layers
    level = (iota((rows, LANE), 1) % layers).astype(jnp.float32)
    left, right = edge[:, :LANE], edge[:, LANE:]
    wet_left = level < left_by(left, 3 * cells)
    wet_own = level < left_by(left, LANE // 2 + 3 * cells)
    wet_right = level < left_by(right, 3 * cells)
    cell_left = jnp.where(wet_left, left, 0.0)
    cell_own = jnp.where(wet_own, left_by(left, LANE // 2), 0.0)
    cell_right = jnp.where(wet_right, right, 0.0)
    return cell_left, cell_own, cell_right, wet_left & wet_own


def column_shifts(shape):
    lane = iota(shape, 1)
    first, last = lane == 0, lane == shape[1] - 1

    def after(x, fill):
        return jnp.where(last, fill, left_by(x, 1))

    def before(x, fill):
        return jnp.where(first, fill, pltpu.roll(x, 1, 1))

    return after, before


def stars_of(get, source, depth, edge, layers, open_ends):
    cells = 2 * layers
    after, before = column_shifts(depth.shape)

    def under(x):
        y = below(x)
        return jnp.where(iota(x.shape, 0) == x.shape[0] - 1, 0.0, y) if open_ends else y

    def over(x):
        y = above(x)
        return jnp.where(iota(x.shape, 0) == 0, 0.0, y) if open_ends else y

    left, right = edge[:, :LANE], edge[:, LANE:]
    cell_left, cell_own, cell_right, wet_both = edge_cells(edge, layers)
    slope_left = under(cell_left) - over(cell_left)
    slope_own = under(cell_own) - over(cell_own)
    slope_right = under(cell_right) - over(cell_right)
    flux_left = left_by(left, cells) * 0.5 * (cell_left + cell_own) - 0.15 * (
        cell_own - cell_left + left_by(left, 2 * cells) * 0.25 * (slope_left + slope_own)
    )
    flux_left = jnp.where(wet_both, flux_left, 0.0)
    depth_right = right[:, 3 * cells : 3 * cells + 1]
    depth_east = jnp.minimum(depth, under(depth))
    depth_north = jnp.minimum(depth, after(depth, depth_right))
    stars = ([], [])
    for k in range(layers):
        wet = depth > k
        mask = depth_east > k
        half = 0.5 * get(2, k)
        e_here = jnp.where(mask, half + 0.15, 0.0)
        e_next = jnp.where(mask, half - 0.15, 0.0)
        e_cross = jnp.where(mask, 0.0375 * get(4, k), 0.0)
        mask = depth_north > k
        half = 0.5 * get(3, k)
        n_here = jnp.where(mask, half + 0.15, 0.0)
        n_next = jnp.where(mask, half - 0.15, 0.0)
        n_cross = jnp.where(mask, 0.0375 * get(5, k), 0.0)
        for t in range(2):
            one = slice(t * layers + k, t * layers + k + 1)
            cell = jnp.where(wet, get(t, k), 0.0)
            east, west = under(cell), over(cell)
            north = after(cell, cell_right[:, one])
            south = before(cell, cell_left[:, one])
            cross = north - south
            flux = e_here * cell + e_next * east - e_cross * (cross + below(cross))
            star = cell - (flux - above(flux))
            cross = east - west
            cross = cross + after(cross, slope_right[:, one])
            flux = n_here * cell + n_next * north - n_cross * cross
            star = star - (flux - before(flux, flux_left[:, one]))
            if k == 0:
                star = star + source[t]
            stars[t].append(jnp.where(wet, star, 0.0))
    return stars


def joined_stars(part, cells_of, east_speed, east_slope, north_slope, depth, edge, upper, layers):
    cells = 2 * layers
    after, before = column_shifts(depth.shape)
    is_upper = upper(depth.shape)
    pack_upper = upper((depth.shape[0], LANE))

    def other(x, mine):
        return jnp.where(mine, below(x), above(x))

    left, right = edge[:, :LANE], edge[:, LANE:]
    cell_left, cell_own, cell_right, wet_both = edge_cells(edge, layers)
    cross_left = 0.0375 * left_by(left, 2 * cells)
    cross_left = cross_left * (other(cell_left, pack_upper) + other(cell_own, pack_upper))
    cross_left = jnp.where(wet_both, cross_left, 0.0)
    other_right = other(cell_right, pack_upper)
    depth_east = jnp.minimum(depth, below(depth))
    depth_north = jnp.minimum(depth, after(depth, right[:, 3 * cells : 3 * cells + 1]))
    stars = ([], [])
    for k in range(layers):
        wet = depth > k
        mask = depth_east > k
        half = 0.5 * east_speed[k]
        e_here = jnp.where(mask, half + 0.15, 0.0)
        e_next = jnp.where(mask, half - 0.15, 0.0)
        e_cross = jnp.where(mask, 0.0375 * east_slope[k], 0.0)
        n_cross = jnp.where(depth_north > k, 0.0375 * north_slope[k], 0.0)
        for t in range(2):
            one = slice(t * layers + k, t * layers + k + 1)
            cell = jnp.where(wet, cells_of[t][k], 0.0)
            east = below(cell)
            cross = after(cell, cell_right[:, one]) - before(cell, cell_left[:, one])
            flux = e_here * cell + e_next * east - e_cross * (cross + below(cross))
            beyond = jnp.where(is_upper, east, above(cell))
            cross = n_cross * (beyond + after(beyond, other_right[:, one]))
            cross = cross - before(cross, cross_left[:, one])
            gain = jnp.where(is_upper, cross - flux, above(flux) - cross)
            stars[t].append(jnp.where(wet, part[t][k] + gain, 0.0))
    return stars


def solve_columns(stars, depth, layers):
    primes, rights = [], ([], [])
    upper = None
    density = 0.8 * stars[1][0] - 0.2 * stars[0][0]
    for k in range(layers):
        if k + 1 < layers:
            deeper = 0.8 * stars[1][k + 1] - 0.2 * stars[0][k + 1]
            couple = 0.05 + 1.0 / (1.0 + 10.0 * jnp.maximum(deeper - density, 0.0))
            couple = jnp.where(depth > k + 1, couple, 0.0)
            density = deeper
        else:
            couple = None
        if k == 0:
            inverse = 1.0 / (1.0 + couple)
        elif couple is not None:
            inverse = 1.0 / (1.0 + upper + couple - upper * primes[-1])
        else:
            inverse = 1.0 / (1.0 + upper - upper * primes[-1])
        for t in range(2):
            value = stars[t][k]
            if k:
                value = value + upper * rights[t][-1]
            rights[t].append(value * inverse)
        if couple is not None:
            primes.append(couple * inverse)
        upper = couple
    fresh = ([None] * layers, [None] * layers)
    forcing = None
    solved = [rights[0][-1], rights[1][-1]]
    for k in range(layers - 1, -1, -1):
        wet = depth > k
        for t in range(2):
            if k < layers - 1:
                solved[t] = rights[t][k] + primes[k] * solved[t]
            fresh[t][k] = jnp.where(wet, solved[t], 0.0)
        part = 0.8 * fresh[1][k] - 0.2 * fresh[0][k]
        forcing = part if forcing is None else forcing + part
    return fresh[0], fresh[1], forcing * (4.0 / math.sqrt(layers))


def inner_tile(t, s, u, v, x, y, source, depth, edge, t_out, s_out, f_out):
    layers = t.shape[0]
    refs = (t, s, u, v, x, y)
    levels = depth[...].astype(jnp.float32)
    stars = stars_of(
        lambda kind, k: refs[kind][k], [source[0], source[1]], levels, edge[...], layers, False
    )
    warm, salt, forcing = solve_columns(stars, levels, layers)
    for k in range(layers):
        t_out[k] = warm[k]
        s_out[k] = salt[k]
    f_out[...] = forcing


def rim_rows(across, even_out, odd_out, even_in, odd_in, f_old, *refs):
    layers = refs[0].shape[0]
    t_fix, s_fix = refs[:2]
    sends, (field, blocks) = refs[2 : 2 + across], refs[2 + across :]
    rows = f_old.shape[0]
    strip = rows // across
    even = lax.axis_index("bx") % 2 == 0
    me = lax.axis_index("by")
    shape = (SUB, f_old.shape[1])
    line = iota(shape, 0)

    def parts(q):
        sent_even, sent_odd, came_even, came_odd = even_out[q], odd_out[q], even_in[q], odd_in[q]
        four = [jnp.where(even, came_odd, came_even), jnp.where(even, sent_odd, sent_even)]
        return four + [jnp.where(even, sent_even, sent_odd), jnp.where(even, came_even, came_odd)]

    def take(four, at):
        total = None
        for i, (part, place) in enumerate(zip(four, (1, 2, 5, 6))):
            part = part if place == at else pltpu.roll(part, (place - at) % SUB, 0)
            total = part if i == 0 else jnp.where(line >= 2 * i, part, total)
        return total

    def rows_from(q, count):
        out = []
        for i in range(count):
            if i % SUB == 0:
                four = parts(q + i // SUB)
            out.append(take(four, i % SUB))
        return out

    ahead = 2 * layers // SUB
    part = rows_from(0, 2 * layers)
    planes = rows_from(ahead + 1, 5 * layers)
    four = parts(ahead)
    me_along = lax.axis_index("bx")
    four[0] = jnp.where(me_along == 0, 0.0, four[0])
    four[3] = jnp.where(me_along == lax.axis_size("bx") - 1, 0.0, four[3])
    depth, edge = take(four, 0), take(four, 1)
    over, under = pltpu.roll(four[0], 3, 0), pltpu.roll(four[3], 7, 0)
    kinds = [planes[i * layers : (i + 1) * layers] for i in range(5)]

    def upper(shape):
        row = iota(shape, 0)
        return (row == 1) | (row == 5)

    stars = joined_stars(
        (part[:layers], part[layers:]),
        (kinds[0], kinds[1]),
        kinds[3],
        kinds[4],
        kinds[2],
        depth,
        edge,
        upper,
        layers,
    )
    warm, salt, forcing = solve_columns(stars, depth, layers)
    for fix, fresh in ((t_fix, warm), (s_fix, salt)):
        for k in range(layers):
            fix[k] = jnp.where(line == 0, pltpu.roll(fresh[k], 6, 0), pltpu.roll(fresh[k], 2, 0))
    top, bottom = pltpu.roll(forcing, 6, 0), pltpu.roll(forcing, 2, 0)
    last = SUB - 1
    field[:SUB, :] = jnp.where(line == last, top, over)
    field[SUB : 2 * SUB, :] = jnp.where(line == 0, top, f_old[:SUB, :])
    field[2 * SUB : rows, :] = f_old[SUB : rows - SUB, :]
    field[rows : rows + SUB, :] = jnp.where(line == last, bottom, f_old[rows - SUB :, :])
    field[SUB + rows : 2 * SUB + rows, :] = jnp.where(line == 0, bottom, under)
    later = ahead + 1 + 5 * layers // SUB
    extra = even_out.shape[0] - later
    tall = blocks.shape[1]
    for peer in range(across):
        start = SUB - ITERS + peer * strip
        stop = min(start + tall, field.shape[0])
        blocks[peer, : stop - start, :] = field[start:stop, :]
    for hop in range(across):
        sends[hop][:tall, :] = blocks[hop_peer(me, hop, across)]
    use_even = even == (me == 0)
    for q in range(extra):
        relay = jnp.where(use_even, even_in[later + q], odd_in[later + q])
        for hop in relaying(across):
            sends[hop][tall + q * SUB : tall + (q + 1) * SUB, :] = relay


def main_rows(from_even, from_odd, main_own, out):
    strip, columns = main_own.shape
    wide = ITERS - 1
    out[...] = jnp.zeros(out.shape, jnp.float32)
    out[ITERS : ITERS + strip, :] = main_own[...]
    over, under = ITERS - wide, ITERS + strip
    even = lax.axis_index("by") % 2 == 0
    parts = columns // LANE
    begin = from_even.shape[0] - wide * parts
    for j in range(parts):
        here = slice(j * LANE, (j + 1) * LANE)
        at = begin + j * wide
        a, b = from_even[at : at + wide, :], from_odd[at : at + wide, :]
        out[over : over + wide, here] = jnp.where(even, b, a)
        out[under : under + wide, here] = jnp.where(even, a, b)


def flush(fix_t, fix_s, t_mid, s_mid, t_out, s_out, ends, sems):
    layers, rows, columns = t_mid.shape
    inner = pl.ds(SUB, rows - 2 * SUB)
    copies = []

    def begin(source, target):
        copies.append(pltpu.make_async_copy(source, target, sems.at[len(copies)]))
        copies[-1].start()

    for mid, out in ((t_mid, t_out), (s_mid, s_out)):
        for low in range(0, layers, 2):
            some = pl.ds(low, 2)
            begin(mid.at[some, inner], out.at[some, inner])
    line = iota((layers, SUB, columns), 1)
    for i, (mid, fix, out) in enumerate(((t_mid, fix_t, t_out), (s_mid, fix_s, s_out))):
        for j, (start, at) in enumerate(((0, 0), (rows - SUB, SUB - 1))):
            old = mid[:, start : start + SUB, :]
            ends[2 * i + j] = jnp.where(line == at, fix[...], old)
            begin(ends.at[2 * i + j], out.at[:, pl.ds(start, SUB)])
    for copy in copies:
        copy.wait()


def hop_peer(me, hop, count):
    if count & (count - 1) == 0:
        return me ^ hop
    return (me + hop) % count


def relaying(count):
    return [h for h in range(count) if hop_peer(0, h, count) == count - 1 or hop_peer(count - 1, h, count) == 0]


def hop_origin(me, hop, count):
    if count & (count - 1) == 0:
        return me ^ hop
    return (me + count - hop) % count


def powers(across, along, *refs):
    came = [refs[0], *refs[1:across][::-1]]
    main_in, basis_ref, row_ref, field, main = refs[across:]
    tall, columns = main_in.shape
    strip = basis_ref.shape[1]
    width = columns // across
    me = lax.axis_index("by")
    for hop in range(across):
        origin = hop_origin(me, hop, across)
        field[:, pl.ds(pl.multiple_of(origin * width, LANE), width)] = came[hop][:tall, :]
    wide = ITERS - 1
    main[...] = main_in[...]

    def relayed(start, mine, sender):
        hop = [h for h in range(across) if hop_origin(mine, h, across) == sender][0]

        @pl.when(me == mine)
        def _():
            for j in range(across):
                at = tall + j * wide
                here = slice(j * width, (j + 1) * width)
                main[start : start + wide, here] = came[hop][at : at + wide, :]

    relayed(ITERS - wide, 0, across - 1)
    relayed(ITERS + strip, across - 1, 0)
    shape = (tall, columns)
    lane = iota(shape, 1)
    line = (lax.axis_index("bx") * across + me) * strip - ITERS + iota(shape, 0)
    inside = (line >= 0) & (line < along * across * strip)
    first, last = lane == 0, lane == columns - 1
    centre = (main[...] + (6.0 - CENTRE)) * (1.0 / SCALE)
    centre = jnp.where(inside, centre, 0.0)
    share = jnp.where(inside, -1.0 / SCALE, 0.0)
    now = field[...]
    own = [now[ITERS : ITERS + strip]]
    for _ in range(ITERS):
        beside = below(now) + above(now)
        spread = now + 0.5 * beside
        east = jnp.where(last, 0.0, left_by(spread, 1))
        west = jnp.where(first, 0.0, pltpu.roll(spread, 1, 1))
        now = centre * now + share * (beside + east + west)
        own.append(now[ITERS : ITERS + strip])
    for k in range(ITERS):
        basis_ref[k] = own[k]
    place = iota((1, LANE), 1)
    row = jnp.zeros((1, LANE), jnp.float32)
    for k, (i, j) in enumerate(PAIRS):
        part = jnp.sum(own[i] * own[j], axis=0, keepdims=True)
        row = jnp.where(place == k, jnp.sum(part, axis=1, keepdims=True), row)
    row_ref[...] = jnp.broadcast_to(row[None], row_ref.shape)


def times(x, y):
    for a, b in ((x, y), (y, x)):
        if isinstance(a, float) and a in (0.0, 1.0):
            return b if a else 0.0
    return x * y


def plus(x, y):
    for a, b in ((x, y), (y, x)):
        if isinstance(a, float) and a == 0.0:
            return b
    return x + y


def coefficients(moments):
    def inner(a, b):
        total = 0.0
        for k in range(len(a) + len(b) - 1):
            part = 0.0
            for i in range(len(a)):
                if 0 <= k - i < len(b):
                    part = plus(part, times(a[i], b[k - i]))
            total = plus(total, times(part, moments[k]))
        return total

    resid, direction, total = [1.0], [1.0], [0.0] * ITERS
    norm_now = inner(resid, resid)
    for step in range(ITERS):
        image = [0.0] * (len(direction) + 1)
        for i, x in enumerate(direction):
            image[i] = plus(image[i], times(CENTRE, x))
            image[i + 1] = times(SCALE, x)
        alpha = norm_now / inner(direction, image)
        for i, x in enumerate(direction):
            total[i] = plus(total[i], times(alpha, x))
        if step + 1 < ITERS:
            resid = [plus(r, times(-alpha, q)) for r, q in zip(resid + [0.0], image)]
            norm_next = inner(resid, resid)
            beta = norm_next / norm_now
            direction = [plus(r, times(beta, p)) for r, p in zip(resid, direction + [0.0])]
            norm_now = norm_next
    return total


def combine(rows_ref, basis_ref, out_ref):
    moments = jnp.sum(rows_ref[...], axis=0)
    total = coefficients([moments[:, k : k + 1] for k in range(len(PAIRS))])
    out_ref[...] = total[0] * basis_ref[0] + total[1] * basis_ref[1] + total[2] * basis_ref[2]


def shape_of(*dims):
    return jax.ShapeDtypeStruct(dims, jnp.float32)


def whole(x):
    return pl.BlockSpec(x.shape, lambda *_: (0,) * len(x.shape))


def block(shape, *index):
    return pl.BlockSpec(shape, lambda *_: index)


def swaps(count, start):
    both = [(i, i + 1) for i in range(start, count - 1, 2)]
    both += [(b, a) for a, b in both]
    return both, sorted(set(range(count)) - {a for a, _ in both})


def across_route(across, start):
    both, alone = swaps(across, start)
    return both + list(zip(alone, alone[::-1]))


def along_route(along, across, start):
    both, alone = swaps(along, start)
    route = [(a * across + i, b * across + i) for a, b in both for i in range(across)]
    side = dict(across_route(across, 0))
    return route + [(a * across + i, a * across + side[i]) for a in alone for i in range(across)]


def local(t, s, u, v, x, y, source, depth, main):
    layers, rows, columns = t.shape
    across, along = lax.axis_size("by"), lax.axis_size("bx")
    strip = rows // across
    names = ("bx", "by")
    params = pltpu.CompilerParams(vmem_limit_bytes=48 << 20)

    call = functools.partial(pl.pallas_call, compiler_params=params)

    hbm = pl.BlockSpec(memory_space=pltpu.HBM)
    wide = ITERS - 1
    pack = shape_of(rows, LANE)
    more = shape_of(rows + wide * (columns * across // LANE), LANE)
    first, even, odd = call(
        pack_edges,
        grid=(1,),
        in_specs=[hbm] * 6,
        out_specs=[whole(pack), whole(more), whole(more)],
        out_shape=[pack, more, more],
        scratch_shapes=[
            pltpu.VMEM((6, layers, rows, LANE), jnp.float32),
            pltpu.VMEM((2, rows, LANE), jnp.int32),
            pltpu.VMEM(main.shape, jnp.float32),
            pltpu.SemaphoreType.DMA((15,)),
        ],
    )(*(pltpu.with_memory_space_constraint(a, pltpu.HBM) for a in (t, s, v, y, depth, main)))
    from_even = lax.ppermute(even, "by", across_route(across, 0))
    from_odd = lax.ppermute(odd, "by", across_route(across, 1))

    fields = (t, s, u, v, x, y, source)
    extra = -(-wide * across // SUB)
    sides = shape_of(rows, 2 * LANE)
    near = shape_of(6 * layers + 3, SUB, columns)
    shared = 2 * layers // SUB + 1
    rim = shape_of(shared + 5 * layers // SUB + extra, SUB, columns)
    near, even, odd = call(
        functools.partial(gather_rows, across),
        grid=(1,),
        in_specs=[hbm] * 8 + [whole(main)],
        out_specs=[whole(near), whole(rim), whole(rim)],
        out_shape=[near, rim, rim],
        scratch_shapes=[
            pltpu.VMEM((6 * layers + 2, 2 * SUB, columns), jnp.float32),
            pltpu.VMEM((2 * SUB, columns), depth.dtype),
            pltpu.SemaphoreType.DMA((16,)),
        ],
    )(*(pltpu.with_memory_space_constraint(a, pltpu.HBM) for a in (*fields, depth)), main)

    plane = shape_of(rows, columns)
    args = (first, from_odd, from_even, near)
    tile = block((shared, SUB, columns), 0, 0, 0)
    edge, even, odd = call(
        pack_rows,
        grid=(1,),
        in_specs=[whole(a) for a in args] + [tile] * 2,
        out_specs=[whole(sides), tile, tile],
        out_shape=[sides, rim, rim],
        input_output_aliases={4: 1, 5: 2},
    )(*args, even, odd)
    odd_in = lax.ppermute(odd, names, along_route(along, across, 1))
    even_in = lax.ppermute(even, names, along_route(along, across, 0))

    cube = shape_of(layers, rows, columns)
    args = (*fields, depth, edge)
    warm, salt, forcing = call(
        inner_tile,
        grid=(1,),
        in_specs=[whole(a) for a in args],
        out_specs=[whole(cube), whole(cube), whole(plane)],
        out_shape=[cube, cube, plane],
    )(*args)

    tall = -(-(strip + 2 * ITERS) // SUB) * SUB
    parts = [shape_of(tall + extra * SUB * (hop in relaying(across)), columns) for hop in range(across)]
    fix = shape_of(layers, SUB, columns)
    fix_t, fix_s, *sends = call(
        functools.partial(rim_rows, across),
        grid=(1,),
        in_specs=[whole(rim)] * 4 + [whole(plane)],
        out_specs=[whole(fix)] * 2 + [whole(part) for part in parts],
        out_shape=[fix] * 2 + parts,
        scratch_shapes=[
            pltpu.VMEM((rows + 2 * SUB, columns), jnp.float32),
            pltpu.VMEM((across, tall, columns), jnp.float32),
        ],
    )(even, odd, even_in, odd_in, forcing)

    came = [sends[0]]
    for hop in range(1, across):
        route = [(i, hop_peer(i, hop, across)) for i in range(across)]
        came.append(lax.ppermute(sends[hop], "by", route))

    args = (fix_t, fix_s, warm, salt)
    warm, salt = call(
        flush,
        grid=(1,),
        in_specs=[whole(a) for a in args],
        out_specs=[hbm] * 2,
        out_shape=[cube] * 2,
        scratch_shapes=[
            pltpu.VMEM((4, layers, SUB, columns), jnp.float32),
            pltpu.SemaphoreType.DMA((layers + 4,)),
        ],
    )(*args)

    basis_shape = shape_of(ITERS, strip, columns * across)
    row_shape = shape_of(across * along, 1, LANE)
    ready = shape_of(tall, columns * across)
    args = (from_even, from_odd, main)
    ready = call(
        main_rows,
        grid=(1,),
        in_specs=[whole(a) for a in args],
        out_specs=whole(ready),
        out_shape=ready,
    )(*args)
    ready, warm, salt = lax.optimization_barrier((ready, warm, salt))
    args = (came[0], *came[:0:-1], ready)
    basis, row = call(
        functools.partial(powers, across, along),
        grid=(1,),
        in_specs=[whole(a) for a in args],
        out_specs=[whole(basis_shape), whole(row_shape)],
        out_shape=[basis_shape, row_shape],
        scratch_shapes=[pltpu.VMEM((tall, columns * across), jnp.float32)] * 2,
    )(*args)
    gathered = lax.all_to_all(row, names, 0, 0, tiled=True)
    result = shape_of(strip, columns * across)
    pressure = call(
        combine,
        grid=(1,),
        in_specs=[whole(gathered), whole(basis)],
        out_specs=whole(result),
        out_shape=result,
    )(gathered, basis)
    return warm, salt, pressure


def solution(mesh):
    tile = P(None, "bx", "by")
    rows = P(("bx", "by"), None)
    return jax.shard_map(
        local,
        mesh=mesh,
        in_specs=(tile,) * 7 + (P("bx", "by"), rows),
        out_specs=(tile, tile, rows),
        check_vma=False,
    )
```

```python
import functools
import math

import jax
import jax.numpy as jnp
from jax import lax
from jax.experimental import pallas as pl
from jax.experimental.pallas import tpu as pltpu
from jax.sharding import PartitionSpec as P

ITERS = 3
CENTRE = 4.5
SCALE = 4.0
LEAST = 0.0499
TINY = 1e-30
DEEP = ITERS + 1
SUB = 8
LANE = 128
PAIRS = ((0, 0), (0, 1), (1, 1), (1, 2), (2, 2), (2, 3))


def iota(shape, dim):
    return lax.broadcasted_iota(jnp.int32, shape, dim)


def below(x):
    return pltpu.roll(x, x.shape[0] - 1, 0)


def above(x):
    return pltpu.roll(x, 1, 0)


def left_by(x, lanes):
    return pltpu.roll(x, x.shape[1] - lanes, 1)


def pack_edges(t, s, v, y, depth, main, first_ref, even_ref, odd_ref, cubes, planes, lines, sems):
    layers, rows, columns = t.shape
    cells = 2 * layers
    wide = ITERS - 1
    head, tail = pl.ds(0, LANE), pl.ds(columns - LANE, LANE)
    moves = []
    for low in range(0, layers, layers // 2):
        some = pl.ds(low, layers // 2)
        for i, (ref, where) in enumerate(((t, tail), (s, tail), (v, tail), (y, tail), (t, head), (s, head))):
            moves.append((ref.at[some, :, where], cubes.at[i, some]))
    moves += [(depth.at[:, tail], planes.at[0]), (depth.at[:, head], planes.at[1]), (main, lines)]
    copies = [pltpu.make_async_copy(a, b, sems.at[i]) for i, (a, b) in enumerate(moves)]
    for copy in copies:
        copy.start()
    for copy in copies:
        copy.wait()
    lane = iota((rows, LANE), 1)
    first = jnp.zeros((rows, LANE), jnp.float32)
    last = jnp.zeros((rows, LANE), jnp.float32)
    edge = LANE - 1
    for k in range(layers):
        first = jnp.where(lane == k, cubes[4, k][:, 0:1], first)
        first = jnp.where(lane == layers + k, cubes[5, k][:, 0:1], first)
        last = jnp.where(lane == k, cubes[0, k][:, edge:], last)
        last = jnp.where(lane == layers + k, cubes[1, k][:, edge:], last)
        two = (lane == cells + k) | (lane == cells + layers + k)
        last = jnp.where(two, cubes[2, k][:, edge:], last)
        two = (lane == 2 * cells + k) | (lane == 2 * cells + layers + k)
        last = jnp.where(two, cubes[3, k][:, edge:], last)
    span = (lane >= 3 * cells) & (lane < 4 * cells)
    first = jnp.where(span, planes[1][:, 0:1].astype(jnp.float32), first)
    last = jnp.where(span, planes[0][:, edge:].astype(jnp.float32), last)
    first_ref[...] = first
    even = lax.axis_index("by") % 2 == 0
    even_ref[:rows, :] = jnp.where(even, last, first)
    odd_ref[:rows, :] = jnp.where(even, first, last)
    strip = lines.shape[0]
    parts = lines.shape[1] // LANE
    for j in range(parts):
        here = slice(j * LANE, (j + 1) * LANE)
        up, down = lines[:wide, here], lines[strip - wide :, here]
        at = rows + j * wide
        even_ref[at : at + wide, :] = jnp.where(even, down, up)
        odd_ref[at : at + wide, :] = jnp.where(even, up, down)


def gather_rows(across, *refs):
    fields, depth, main = refs[:7], refs[7], refs[8]
    near, even_ref, odd_ref, raw, raw_depth, sems = refs[9:]
    layers, rows = fields[0].shape[:2]
    copies = []
    at = 0
    for ref in fields:
        for i, start in enumerate((0, rows - SUB)):
            planes = raw.at[pl.ds(at, ref.shape[0]), pl.ds(i * SUB, SUB)]
            copies.append((ref.at[:, pl.ds(start, SUB)], planes))
        at += ref.shape[0]
    for i, start in enumerate((0, rows - SUB)):
        copies.append((depth.at[pl.ds(start, SUB)], raw_depth.at[pl.ds(i * SUB, SUB)]))
    copies = [pltpu.make_async_copy(a, b, sems.at[i]) for i, (a, b) in enumerate(copies)]
    for copy in copies:
        copy.start()
    for copy in copies:
        copy.wait()
    base = 6 * layers
    planes = [(raw[p, :SUB], raw[p, SUB:]) for p in range(base + 2)]
    levels = raw_depth[...].astype(jnp.float32)
    planes.append((levels[:SUB], levels[SUB:]))
    line = iota(planes[0][0].shape, 0)
    for p, (up, down) in enumerate(planes):
        near[p] = jnp.where(line < SUB // 2, up, down)
    even = lax.axis_index("bx") % 2 == 0

    mine = row_planes(layers)
    begin = 2 * layers // SUB + 1
    for q in range(len(mine) // SUB):
        put_rows(even_ref, odd_ref, begin + q, [planes[p] for p in mine[q * SUB : (q + 1) * SUB]], even)
    count = begin + len(mine) // SUB
    wide = ITERS - 1
    strip = main.shape[0]
    width = fields[0].shape[2]
    for j in range(across):
        here = slice(j * width, (j + 1) * width)
        up, down = main[:wide, here], main[strip - wide :, here]
        q, at = divmod(j * wide, SUB)
        even_ref[count + q, at : at + wide, :] = jnp.where(even, down, up)
        odd_ref[count + q, at : at + wide, :] = jnp.where(even, up, down)


def put_rows(even_ref, odd_ref, q, planes, even):
    line = iota(planes[0][0].shape, 0)
    out_even, out_odd = None, None
    for j, (up, down) in enumerate(planes):
        up = pltpu.roll(up, j, 0) if j else up
        down = pltpu.roll(down, (j + 1) % SUB, 0) if (j + 1) % SUB else down
        one, two = jnp.where(even, down, up), jnp.where(even, up, down)
        out_even = one if j == 0 else jnp.where(line >= j, one, out_even)
        out_odd = two if j == 0 else jnp.where(line >= j, two, out_odd)
    even_ref[q] = out_even
    odd_ref[q] = out_odd


def row_planes(layers):
    return [kind * layers + k for kind in (0, 1, 5, 2, 4) for k in range(layers)]


def pack_rows(first_ref, from_odd, from_even, near, even_in, odd_in, edge_ref, even_ref, odd_ref):
    rows, half = first_ref.shape[0], LANE // 2
    base = near.shape[0] - 3
    layers = base // 6
    even = lax.axis_index("by") % 2 == 0
    lane = iota((rows, LANE), 1)
    a, b = from_even[:rows, :], from_odd[:rows, :]
    left, right = jnp.where(even, b, a), jnp.where(even, a, b)
    me = lax.axis_index("by")
    left = jnp.where(me == 0, 0.0, left)
    right = jnp.where(me == lax.axis_size("by") - 1, 0.0, right)
    left = jnp.where(lane < half, left, pltpu.roll(first_ref[...], half, 1))
    edge_ref[:, :LANE] = left
    edge_ref[:, LANE:] = right
    head, tail = edge_ref[:SUB, :], edge_ref[rows - SUB :, :]
    line = iota(head.shape, 0)
    depth = near[base + 2]
    stars = stars_of(
        lambda kind, k: near[kind * layers + k],
        [near[base], near[base + 1]],
        depth,
        jnp.where(line < SUB // 2, head, tail),
        layers,
        True,
    )
    _, _, forcing = solve_columns(stars, depth, layers)
    even = lax.axis_index("bx") % 2 == 0
    both = stars[0] + stars[1]
    for q in range(len(both) // SUB):
        put_rows(even_ref, odd_ref, q, [(p, p) for p in both[q * SUB : (q + 1) * SUB]], even)
    up = jnp.where(line < 1, depth, jnp.where(line < 2, pltpu.roll(head, 1, 0), pltpu.roll(forcing, 1, 0)))
    down = jnp.where(line < 2, pltpu.roll(tail, 2, 0), pltpu.roll(forcing, 5, 0))
    down = jnp.where(line < 1, pltpu.roll(depth, 1, 0), down)
    q = len(both) // SUB
    even_ref[q] = jnp.where(even, down, up)
    odd_ref[q] = jnp.where(even, up, down)


def edge_cells(edge, layers):
    rows = edge.shape[0]
    cells = 2 * layers
    level = (iota((rows, LANE), 1) % layers).astype(jnp.float32)
    left, right = edge[:, :LANE], edge[:, LANE:]
    wet_left = level < left_by(left, 3 * cells)
    wet_own = level < left_by(left, LANE // 2 + 3 * cells)
    wet_right = level < left_by(right, 3 * cells)
    cell_left = jnp.where(wet_left, left, 0.0)
    cell_own = jnp.where(wet_own, left_by(left, LANE // 2), 0.0)
    cell_right = jnp.where(wet_right, right, 0.0)
    return cell_left, cell_own, cell_right, wet_left & wet_own


def column_shifts(shape):
    lane = iota(shape, 1)
    first, last = lane == 0, lane == shape[1] - 1

    def after(x, fill):
        return jnp.where(last, fill, left_by(x, 1))

    def before(x, fill):
        return jnp.where(first, fill, pltpu.roll(x, 1, 1))

    return after, before


def stars_of(get, source, depth, edge, layers, open_ends):
    cells = 2 * layers
    after, before = column_shifts(depth.shape)

    def under(x):
        y = below(x)
        return jnp.where(iota(x.shape, 0) == x.shape[0] - 1, 0.0, y) if open_ends else y

    def over(x):
        y = above(x)
        return jnp.where(iota(x.shape, 0) == 0, 0.0, y) if open_ends else y

    left, right = edge[:, :LANE], edge[:, LANE:]
    cell_left, cell_own, cell_right, wet_both = edge_cells(edge, layers)
    slope_left = under(cell_left) - over(cell_left)
    slope_own = under(cell_own) - over(cell_own)
    slope_right = under(cell_right) - over(cell_right)
    flux_left = left_by(left, cells) * 0.5 * (cell_left + cell_own) - 0.15 * (
        cell_own - cell_left + left_by(left, 2 * cells) * 0.25 * (slope_left + slope_own)
    )
    flux_left = jnp.where(wet_both, flux_left, 0.0)
    depth_right = right[:, 3 * cells : 3 * cells + 1]
    depth_east = jnp.minimum(depth, under(depth))
    depth_north = jnp.minimum(depth, after(depth, depth_right))
    stars = ([], [])
    for k in range(layers):
        wet = depth > k
        mask = depth_east > k
        half = 0.5 * get(2, k)
        e_here = jnp.where(mask, half + 0.15, 0.0)
        e_next = jnp.where(mask, half - 0.15, 0.0)
        e_cross = jnp.where(mask, 0.0375 * get(4, k), 0.0)
        mask = depth_north > k
        half = 0.5 * get(3, k)
        n_here = jnp.where(mask, half + 0.15, 0.0)
        n_next = jnp.where(mask, half - 0.15, 0.0)
        n_cross = jnp.where(mask, 0.0375 * get(5, k), 0.0)
        for t in range(2):
            one = slice(t * layers + k, t * layers + k + 1)
            cell = jnp.where(wet, get(t, k), 0.0)
            east, west = under(cell), over(cell)
            north = after(cell, cell_right[:, one])
            south = before(cell, cell_left[:, one])
            cross = north - south
            flux = e_here * cell + e_next * east - e_cross * (cross + below(cross))
            star = cell - (flux - above(flux))
            cross = east - west
            cross = cross + after(cross, slope_right[:, one])
            flux = n_here * cell + n_next * north - n_cross * cross
            star = star - (flux - before(flux, flux_left[:, one]))
            if k == 0:
                star = star + source[t]
            stars[t].append(jnp.where(wet, star, 0.0))
    return stars


def joined_stars(part, cells_of, east_speed, east_slope, north_slope, depth, edge, upper, layers):
    cells = 2 * layers
    after, before = column_shifts(depth.shape)
    is_upper = upper(depth.shape)
    pack_upper = upper((depth.shape[0], LANE))

    def other(x, mine):
        return jnp.where(mine, below(x), above(x))

    left, right = edge[:, :LANE], edge[:, LANE:]
    cell_left, cell_own, cell_right, wet_both = edge_cells(edge, layers)
    cross_left = 0.0375 * left_by(left, 2 * cells)
    cross_left = cross_left * (other(cell_left, pack_upper) + other(cell_own, pack_upper))
    cross_left = jnp.where(wet_both, cross_left, 0.0)
    other_right = other(cell_right, pack_upper)
    depth_east = jnp.minimum(depth, below(depth))
    depth_north = jnp.minimum(depth, after(depth, right[:, 3 * cells : 3 * cells + 1]))
    stars = ([], [])
    for k in range(layers):
        wet = depth > k
        mask = depth_east > k
        half = 0.5 * east_speed[k]
        e_here = jnp.where(mask, half + 0.15, 0.0)
        e_next = jnp.where(mask, half - 0.15, 0.0)
        e_cross = jnp.where(mask, 0.0375 * east_slope[k], 0.0)
        n_cross = jnp.where(depth_north > k, 0.0375 * north_slope[k], 0.0)
        for t in range(2):
            one = slice(t * layers + k, t * layers + k + 1)
            cell = jnp.where(wet, cells_of[t][k], 0.0)
            east = below(cell)
            cross = after(cell, cell_right[:, one]) - before(cell, cell_left[:, one])
            flux = e_here * cell + e_next * east - e_cross * (cross + below(cross))
            beyond = jnp.where(is_upper, east, above(cell))
            cross = n_cross * (beyond + after(beyond, other_right[:, one]))
            cross = cross - before(cross, cross_left[:, one])
            gain = jnp.where(is_upper, cross - flux, above(flux) - cross)
            stars[t].append(jnp.where(wet, part[t][k] + gain, 0.0))
    return stars


def solve_columns(stars, depth, layers):
    primes, rights = [], ([], [])
    upper = None
    density = 0.8 * stars[1][0] - 0.2 * stars[0][0]
    for k in range(layers):
        if k + 1 < layers:
            deeper = 0.8 * stars[1][k + 1] - 0.2 * stars[0][k + 1]
            couple = 0.05 + 1.0 / (1.0 + 10.0 * jnp.maximum(deeper - density, 0.0))
            couple = jnp.where(depth > k + 1, couple, 0.0)
            density = deeper
        else:
            couple = None
        if k == 0:
            inverse = 1.0 / (1.0 + couple)
        elif couple is not None:
            inverse = 1.0 / (1.0 + upper + couple - upper * primes[-1])
        else:
            inverse = 1.0 / (1.0 + upper - upper * primes[-1])
        for t in range(2):
            value = stars[t][k]
            if k:
                value = value + upper * rights[t][-1]
            rights[t].append(value * inverse)
        if couple is not None:
            primes.append(couple * inverse)
        upper = couple
    fresh = ([None] * layers, [None] * layers)
    forcing = None
    solved = [rights[0][-1], rights[1][-1]]
    for k in range(layers - 1, -1, -1):
        wet = depth > k
        for t in range(2):
            if k < layers - 1:
                solved[t] = rights[t][k] + primes[k] * solved[t]
            fresh[t][k] = jnp.where(wet, solved[t], 0.0)
        part = 0.8 * fresh[1][k] - 0.2 * fresh[0][k]
        forcing = part if forcing is None else forcing + part
    return fresh[0], fresh[1], forcing * (4.0 / math.sqrt(layers))


def inner_tile(t, s, u, v, x, y, source, depth, edge, t_out, s_out, f_out):
    layers = t.shape[0]
    refs = (t, s, u, v, x, y)
    levels = depth[...].astype(jnp.float32)
    stars = stars_of(
        lambda kind, k: refs[kind][k], [source[0], source[1]], levels, edge[...], layers, False
    )
    warm, salt, forcing = solve_columns(stars, levels, layers)
    for k in range(layers):
        t_out[k] = warm[k]
        s_out[k] = salt[k]
    f_out[...] = forcing


def rim_rows(across, even_out, odd_out, even_in, odd_in, f_old, *refs):
    layers = refs[0].shape[0]
    t_fix, s_fix = refs[:2]
    sends, (field, blocks) = refs[2 : 2 + across], refs[2 + across :]
    rows = f_old.shape[0]
    strip = rows // across
    even = lax.axis_index("bx") % 2 == 0
    me = lax.axis_index("by")
    shape = (SUB, f_old.shape[1])
    line = iota(shape, 0)

    def parts(q):
        sent_even, sent_odd, came_even, came_odd = even_out[q], odd_out[q], even_in[q], odd_in[q]
        four = [jnp.where(even, came_odd, came_even), jnp.where(even, sent_odd, sent_even)]
        return four + [jnp.where(even, sent_even, sent_odd), jnp.where(even, came_even, came_odd)]

    def take(four, at):
        total = None
        for i, (part, place) in enumerate(zip(four, (1, 2, 5, 6))):
            part = part if place == at else pltpu.roll(part, (place - at) % SUB, 0)
            total = part if i == 0 else jnp.where(line >= 2 * i, part, total)
        return total

    def rows_from(q, count):
        out = []
        for i in range(count):
            if i % SUB == 0:
                four = parts(q + i // SUB)
            out.append(take(four, i % SUB))
        return out

    ahead = 2 * layers // SUB
    part = rows_from(0, 2 * layers)
    planes = rows_from(ahead + 1, 5 * layers)
    four = parts(ahead)
    me_along = lax.axis_index("bx")
    four[0] = jnp.where(me_along == 0, 0.0, four[0])
    four[3] = jnp.where(me_along == lax.axis_size("bx") - 1, 0.0, four[3])
    depth, edge = take(four, 0), take(four, 1)
    over, under = pltpu.roll(four[0], 3, 0), pltpu.roll(four[3], 7, 0)
    kinds = [planes[i * layers : (i + 1) * layers] for i in range(5)]

    def upper(shape):
        row = iota(shape, 0)
        return (row == 1) | (row == 5)

    stars = joined_stars(
        (part[:layers], part[layers:]),
        (kinds[0], kinds[1]),
        kinds[3],
        kinds[4],
        kinds[2],
        depth,
        edge,
        upper,
        layers,
    )
    warm, salt, forcing = solve_columns(stars, depth, layers)
    for fix, fresh in ((t_fix, warm), (s_fix, salt)):
        for k in range(layers):
            fix[k] = jnp.where(line == 0, pltpu.roll(fresh[k], 6, 0), pltpu.roll(fresh[k], 2, 0))
    top, bottom = pltpu.roll(forcing, 6, 0), pltpu.roll(forcing, 2, 0)
    last = SUB - 1
    field[:SUB, :] = jnp.where(line == last, top, over)
    field[SUB : 2 * SUB, :] = jnp.where(line == 0, top, f_old[:SUB, :])
    field[2 * SUB : rows, :] = f_old[SUB : rows - SUB, :]
    field[rows : rows + SUB, :] = jnp.where(line == last, bottom, f_old[rows - SUB :, :])
    field[SUB + rows : 2 * SUB + rows, :] = jnp.where(line == 0, bottom, under)
    later = ahead + 1 + 5 * layers // SUB
    extra = even_out.shape[0] - later
    tall = blocks.shape[1]
    for peer in range(across):
        start = SUB - ITERS + peer * strip
        stop = min(start + tall, field.shape[0])
        blocks[peer, : stop - start, :] = field[start:stop, :]
    for hop in range(across):
        sends[hop][:tall, :] = blocks[hop_peer(me, hop, across)]
    use_even = even == (me == 0)
    for q in range(extra):
        relay = jnp.where(use_even, even_in[later + q], odd_in[later + q])
        for hop in relaying(across):
            sends[hop][tall + q * SUB : tall + (q + 1) * SUB, :] = relay


def main_rows(from_even, from_odd, main_own, out):
    strip, columns = main_own.shape
    wide = ITERS - 1
    out[...] = jnp.zeros(out.shape, jnp.float32)
    out[ITERS : ITERS + strip, :] = main_own[...]
    over, under = ITERS - wide, ITERS + strip
    even = lax.axis_index("by") % 2 == 0
    parts = columns // LANE
    begin = from_even.shape[0] - wide * parts
    for j in range(parts):
        here = slice(j * LANE, (j + 1) * LANE)
        at = begin + j * wide
        a, b = from_even[at : at + wide, :], from_odd[at : at + wide, :]
        out[over : over + wide, here] = jnp.where(even, b, a)
        out[under : under + wide, here] = jnp.where(even, a, b)


def flush(fix_t, fix_s, t_mid, s_mid, t_out, s_out, ends, sems):
    layers, rows, columns = t_mid.shape
    inner = pl.ds(SUB, rows - 2 * SUB)
    copies = []

    def begin(source, target):
        copies.append(pltpu.make_async_copy(source, target, sems.at[len(copies)]))
        copies[-1].start()

    for mid, out in ((t_mid, t_out), (s_mid, s_out)):
        for low in range(0, layers, 2):
            some = pl.ds(low, 2)
            begin(mid.at[some, inner], out.at[some, inner])
    line = iota((layers, SUB, columns), 1)
    for i, (mid, fix, out) in enumerate(((t_mid, fix_t, t_out), (s_mid, fix_s, s_out))):
        for j, (start, at) in enumerate(((0, 0), (rows - SUB, SUB - 1))):
            old = mid[:, start : start + SUB, :]
            ends[2 * i + j] = jnp.where(line == at, fix[...], old)
            begin(ends.at[2 * i + j], out.at[:, pl.ds(start, SUB)])
    for copy in copies:
        copy.wait()


def hop_peer(me, hop, count):
    if count & (count - 1) == 0:
        return me ^ hop
    return (me + hop) % count


def relaying(count):
    return [h for h in range(count) if hop_peer(0, h, count) == count - 1 or hop_peer(count - 1, h, count) == 0]


def hop_origin(me, hop, count):
    if count & (count - 1) == 0:
        return me ^ hop
    return (me + count - hop) % count


def powers(across, along, *refs):
    came = [refs[0], *refs[1:across][::-1]]
    main_in, basis_ref, row_ref, field, main = refs[across:]
    tall, columns = main_in.shape
    strip = basis_ref.shape[1]
    width = columns // across
    me = lax.axis_index("by")
    for hop in range(across):
        origin = hop_origin(me, hop, across)
        field[:, pl.ds(pl.multiple_of(origin * width, LANE), width)] = came[hop][:tall, :]
    wide = ITERS - 1
    main[...] = main_in[...]

    def relayed(start, mine, sender):
        hop = [h for h in range(across) if hop_origin(mine, h, across) == sender][0]

        @pl.when(me == mine)
        def _():
            for j in range(across):
                at = tall + j * wide
                here = slice(j * width, (j + 1) * width)
                main[start : start + wide, here] = came[hop][at : at + wide, :]

    relayed(ITERS - wide, 0, across - 1)
    relayed(ITERS + strip, across - 1, 0)
    shape = (tall, columns)
    lane = iota(shape, 1)
    line = (lax.axis_index("bx") * across + me) * strip - ITERS + iota(shape, 0)
    inside = (line >= 0) & (line < along * across * strip)
    first, last = lane == 0, lane == columns - 1
    centre = (main[...] + (6.0 - CENTRE)) * (1.0 / SCALE)
    centre = jnp.where(inside, centre, 0.0)
    share = jnp.where(inside, -1.0 / SCALE, 0.0)
    now = field[...]
    own = [now[ITERS : ITERS + strip]]
    for _ in range(ITERS):
        beside = below(now) + above(now)
        spread = now + 0.5 * beside
        east = jnp.where(last, 0.0, left_by(spread, 1))
        west = jnp.where(first, 0.0, pltpu.roll(spread, 1, 1))
        now = centre * now + share * (beside + east + west)
        own.append(now[ITERS : ITERS + strip])
    for k in range(ITERS):
        basis_ref[k] = own[k]
    place = iota((1, LANE), 1)
    row = jnp.zeros((1, LANE), jnp.float32)
    for k, (i, j) in enumerate(PAIRS):
        part = jnp.sum(own[i] * own[j], axis=0, keepdims=True)
        row = jnp.where(place == k, jnp.sum(part, axis=1, keepdims=True), row)
    row_ref[...] = jnp.broadcast_to(row[None], row_ref.shape)


def times(x, y):
    for a, b in ((x, y), (y, x)):
        if isinstance(a, float) and a in (0.0, 1.0):
            return b if a else 0.0
    return x * y


def plus(x, y):
    for a, b in ((x, y), (y, x)):
        if isinstance(a, float) and a == 0.0:
            return b
    return x + y


def coefficients(moments):
    def inner(a, b):
        total = 0.0
        for k in range(len(a) + len(b) - 1):
            part = 0.0
            for i in range(len(a)):
                if 0 <= k - i < len(b):
                    part = plus(part, times(a[i], b[k - i]))
            total = plus(total, times(part, moments[k]))
        return total

    resid, direction, total = [1.0], [1.0], [0.0] * ITERS
    norm_now = inner(resid, resid)
    for step in range(ITERS):
        image = [0.0] * (len(direction) + 1)
        for i, x in enumerate(direction):
            image[i] = plus(image[i], times(CENTRE, x))
            image[i + 1] = times(SCALE, x)
        bound = jnp.maximum(LEAST * norm_now, TINY)
        alpha = norm_now / jnp.maximum(inner(direction, image), bound)
        for i, x in enumerate(direction):
            total[i] = plus(total[i], times(alpha, x))
        if step + 1 < ITERS:
            resid = [plus(r, times(-alpha, q)) for r, q in zip(resid + [0.0], image)]
            norm_next = jnp.maximum(inner(resid, resid), 0.0)
            beta = norm_next / jnp.maximum(norm_now, TINY)
            direction = [plus(r, times(beta, p)) for r, p in zip(resid, direction + [0.0])]
            norm_now = norm_next
    return total


def combine(rows_ref, basis_ref, out_ref):
    moments = jnp.sum(rows_ref[...], axis=0)
    total = coefficients([moments[:, k : k + 1] for k in range(len(PAIRS))])
    out_ref[...] = total[0] * basis_ref[0] + total[1] * basis_ref[1] + total[2] * basis_ref[2]


def shape_of(*dims):
    return jax.ShapeDtypeStruct(dims, jnp.float32)


def whole(x):
    return pl.BlockSpec(x.shape, lambda *_: (0,) * len(x.shape))


def block(shape, *index):
    return pl.BlockSpec(shape, lambda *_: index)


def swaps(count, start):
    both = [(i, i + 1) for i in range(start, count - 1, 2)]
    both += [(b, a) for a, b in both]
    return both, sorted(set(range(count)) - {a for a, _ in both})


def across_route(across, start):
    both, alone = swaps(across, start)
    return both + list(zip(alone, alone[::-1]))


def along_route(along, across, start):
    both, alone = swaps(along, start)
    route = [(a * across + i, b * across + i) for a, b in both for i in range(across)]
    side = dict(across_route(across, 0))
    return route + [(a * across + i, a * across + side[i]) for a in alone for i in range(across)]


def local(t, s, u, v, x, y, source, depth, main):
    layers, rows, columns = t.shape
    across, along = lax.axis_size("by"), lax.axis_size("bx")
    strip = rows // across
    names = ("bx", "by")
    params = pltpu.CompilerParams(vmem_limit_bytes=48 << 20)

    call = functools.partial(pl.pallas_call, compiler_params=params)

    hbm = pl.BlockSpec(memory_space=pltpu.HBM)
    wide = ITERS - 1
    pack = shape_of(rows, LANE)
    more = shape_of(rows + wide * (columns * across // LANE), LANE)
    first, even, odd = call(
        pack_edges,
        grid=(1,),
        in_specs=[hbm] * 6,
        out_specs=[whole(pack), whole(more), whole(more)],
        out_shape=[pack, more, more],
        scratch_shapes=[
            pltpu.VMEM((6, layers, rows, LANE), jnp.float32),
            pltpu.VMEM((2, rows, LANE), jnp.int32),
            pltpu.VMEM(main.shape, jnp.float32),
            pltpu.SemaphoreType.DMA((15,)),
        ],
    )(*(pltpu.with_memory_space_constraint(a, pltpu.HBM) for a in (t, s, v, y, depth, main)))
    from_even = lax.ppermute(even, "by", across_route(across, 0))
    from_odd = lax.ppermute(odd, "by", across_route(across, 1))

    fields = (t, s, u, v, x, y, source)
    extra = -(-wide * across // SUB)
    sides = shape_of(rows, 2 * LANE)
    near = shape_of(6 * layers + 3, SUB, columns)
    shared = 2 * layers // SUB + 1
    rim = shape_of(shared + 5 * layers // SUB + extra, SUB, columns)
    near, even, odd = call(
        functools.partial(gather_rows, across),
        grid=(1,),
        in_specs=[hbm] * 8 + [whole(main)],
        out_specs=[whole(near), whole(rim), whole(rim)],
        out_shape=[near, rim, rim],
        scratch_shapes=[
            pltpu.VMEM((6 * layers + 2, 2 * SUB, columns), jnp.float32),
            pltpu.VMEM((2 * SUB, columns), depth.dtype),
            pltpu.SemaphoreType.DMA((16,)),
        ],
    )(*(pltpu.with_memory_space_constraint(a, pltpu.HBM) for a in (*fields, depth)), main)

    plane = shape_of(rows, columns)
    args = (first, from_odd, from_even, near)
    tile = block((shared, SUB, columns), 0, 0, 0)
    edge, even, odd = call(
        pack_rows,
        grid=(1,),
        in_specs=[whole(a) for a in args] + [tile] * 2,
        out_specs=[whole(sides), tile, tile],
        out_shape=[sides, rim, rim],
        input_output_aliases={4: 1, 5: 2},
    )(*args, even, odd)
    odd_in = lax.ppermute(odd, names, along_route(along, across, 1))
    even_in = lax.ppermute(even, names, along_route(along, across, 0))

    cube = shape_of(layers, rows, columns)
    args = (*fields, depth, edge)
    warm, salt, forcing = call(
        inner_tile,
        grid=(1,),
        in_specs=[whole(a) for a in args],
        out_specs=[whole(cube), whole(cube), whole(plane)],
        out_shape=[cube, cube, plane],
    )(*args)

    tall = -(-(strip + 2 * ITERS) // SUB) * SUB
    parts = [shape_of(tall + extra * SUB * (hop in relaying(across)), columns) for hop in range(across)]
    fix = shape_of(layers, SUB, columns)
    fix_t, fix_s, *sends = call(
        functools.partial(rim_rows, across),
        grid=(1,),
        in_specs=[whole(rim)] * 4 + [whole(plane)],
        out_specs=[whole(fix)] * 2 + [whole(part) for part in parts],
        out_shape=[fix] * 2 + parts,
        scratch_shapes=[
            pltpu.VMEM((rows + 2 * SUB, columns), jnp.float32),
            pltpu.VMEM((across, tall, columns), jnp.float32),
        ],
    )(even, odd, even_in, odd_in, forcing)

    came = [sends[0]]
    for hop in range(1, across):
        route = [(i, hop_peer(i, hop, across)) for i in range(across)]
        came.append(lax.ppermute(sends[hop], "by", route))

    args = (fix_t, fix_s, warm, salt)
    warm, salt = call(
        flush,
        grid=(1,),
        in_specs=[whole(a) for a in args],
        out_specs=[hbm] * 2,
        out_shape=[cube] * 2,
        scratch_shapes=[
            pltpu.VMEM((4, layers, SUB, columns), jnp.float32),
            pltpu.SemaphoreType.DMA((layers + 4,)),
        ],
    )(*args)

    basis_shape = shape_of(ITERS, strip, columns * across)
    row_shape = shape_of(across * along, 1, LANE)
    ready = shape_of(tall, columns * across)
    args = (from_even, from_odd, main)
    ready = call(
        main_rows,
        grid=(1,),
        in_specs=[whole(a) for a in args],
        out_specs=whole(ready),
        out_shape=ready,
    )(*args)
    ready, warm, salt = lax.optimization_barrier((ready, warm, salt))
    args = (came[0], *came[:0:-1], ready)
    basis, row = call(
        functools.partial(powers, across, along),
        grid=(1,),
        in_specs=[whole(a) for a in args],
        out_specs=[whole(basis_shape), whole(row_shape)],
        out_shape=[basis_shape, row_shape],
        scratch_shapes=[pltpu.VMEM((tall, columns * across), jnp.float32)] * 2,
    )(*args)
    gathered = lax.all_to_all(row, names, 0, 0, tiled=True)
    result = shape_of(strip, columns * across)
    pressure = call(
        combine,
        grid=(1,),
        in_specs=[whole(gathered), whole(basis)],
        out_specs=whole(result),
        out_shape=result,
    )(gathered, basis)
    return warm, salt, pressure


def solution(mesh):
    tile = P(None, "bx", "by")
    rows = P(("bx", "by"), None)
    return jax.shard_map(
        local,
        mesh=mesh,
        in_specs=(tile,) * 7 + (P("bx", "by"), rows),
        out_specs=(tile, tile, rows),
        check_vma=False,
    )
```

```python
import functools
import math

import jax
import jax.numpy as jnp
from jax import lax
from jax.experimental import pallas as pl
from jax.experimental.pallas import tpu as pltpu
from jax.sharding import PartitionSpec as P

ITERS = 3
CENTRE = 4.5
SCALE = 4.0
LEAST = 0.0499
TINY = 1e-30
DEEP = ITERS + 1
SUB = 8
LANE = 128
PAIRS = ((0, 0), (0, 1), (1, 1), (1, 2), (2, 2), (2, 3))


def iota(shape, dim):
    return lax.broadcasted_iota(jnp.int32, shape, dim)


def below(x):
    return pltpu.roll(x, x.shape[0] - 1, 0)


def above(x):
    return pltpu.roll(x, 1, 0)


def left_by(x, lanes):
    return pltpu.roll(x, x.shape[1] - lanes, 1)


def pack_edges(t, s, v, y, depth, main, first_ref, even_ref, odd_ref, cubes, planes, lines, sems):
    layers, rows, columns = t.shape
    cells = 2 * layers
    wide = ITERS - 1
    head, tail = pl.ds(0, LANE), pl.ds(columns - LANE, LANE)
    moves = []
    for low in range(0, layers, layers // 2):
        some = pl.ds(low, layers // 2)
        for i, (ref, where) in enumerate(((t, tail), (s, tail), (v, tail), (y, tail), (t, head), (s, head))):
            moves.append((ref.at[some, :, where], cubes.at[i, some]))
    moves += [(depth.at[:, tail], planes.at[0]), (depth.at[:, head], planes.at[1]), (main, lines)]
    copies = [pltpu.make_async_copy(a, b, sems.at[i]) for i, (a, b) in enumerate(moves)]
    for copy in copies:
        copy.start()
    for copy in copies:
        copy.wait()
    lane = iota((rows, LANE), 1)
    first = jnp.zeros((rows, LANE), jnp.float32)
    last = jnp.zeros((rows, LANE), jnp.float32)
    edge = LANE - 1
    for k in range(layers):
        first = jnp.where(lane == k, cubes[4, k][:, 0:1], first)
        first = jnp.where(lane == layers + k, cubes[5, k][:, 0:1], first)
        last = jnp.where(lane == k, cubes[0, k][:, edge:], last)
        last = jnp.where(lane == layers + k, cubes[1, k][:, edge:], last)
        two = (lane == cells + k) | (lane == cells + layers + k)
        last = jnp.where(two, cubes[2, k][:, edge:], last)
        two = (lane == 2 * cells + k) | (lane == 2 * cells + layers + k)
        last = jnp.where(two, cubes[3, k][:, edge:], last)
    span = (lane >= 3 * cells) & (lane < 4 * cells)
    first = jnp.where(span, planes[1][:, 0:1].astype(jnp.float32), first)
    last = jnp.where(span, planes[0][:, edge:].astype(jnp.float32), last)
    first_ref[...] = first
    even = lax.axis_index("by") % 2 == 0
    even_ref[:rows, :] = jnp.where(even, last, first)
    odd_ref[:rows, :] = jnp.where(even, first, last)
    strip = lines.shape[0]
    parts = lines.shape[1] // LANE
    for j in range(parts):
        here = slice(j * LANE, (j + 1) * LANE)
        up, down = lines[:wide, here], lines[strip - wide :, here]
        at = rows + j * wide
        even_ref[at : at + wide, :] = jnp.where(even, down, up)
        odd_ref[at : at + wide, :] = jnp.where(even, up, down)


def gather_rows(across, *refs):
    fields, depth, main = refs[:7], refs[7], refs[8]
    near, even_ref, odd_ref, raw, raw_depth, sems = refs[9:]
    layers, rows = fields[0].shape[:2]
    copies = []
    at = 0
    for ref in fields:
        for i, start in enumerate((0, rows - SUB)):
            planes = raw.at[pl.ds(at, ref.shape[0]), pl.ds(i * SUB, SUB)]
            copies.append((ref.at[:, pl.ds(start, SUB)], planes))
        at += ref.shape[0]
    for i, start in enumerate((0, rows - SUB)):
        copies.append((depth.at[pl.ds(start, SUB)], raw_depth.at[pl.ds(i * SUB, SUB)]))
    copies = [pltpu.make_async_copy(a, b, sems.at[i]) for i, (a, b) in enumerate(copies)]
    for copy in copies:
        copy.start()
    for copy in copies:
        copy.wait()
    base = 6 * layers
    planes = [(raw[p, :SUB], raw[p, SUB:]) for p in range(base + 2)]
    levels = raw_depth[...].astype(jnp.float32)
    planes.append((levels[:SUB], levels[SUB:]))
    line = iota(planes[0][0].shape, 0)
    for p, (up, down) in enumerate(planes):
        near[p] = jnp.where(line < SUB // 2, up, down)
    even = lax.axis_index("bx") % 2 == 0

    mine = row_planes(layers)
    begin = 2 * layers // SUB + 1
    for q in range(len(mine) // SUB):
        put_rows(even_ref, odd_ref, begin + q, [planes[p] for p in mine[q * SUB : (q + 1) * SUB]], even)
    count = begin + len(mine) // SUB
    wide = ITERS - 1
    strip = main.shape[0]
    width = fields[0].shape[2]
    for j in range(across):
        here = slice(j * width, (j + 1) * width)
        up, down = main[:wide, here], main[strip - wide :, here]
        q, at = divmod(j * wide, SUB)
        even_ref[count + q, at : at + wide, :] = jnp.where(even, down, up)
        odd_ref[count + q, at : at + wide, :] = jnp.where(even, up, down)


def put_rows(even_ref, odd_ref, q, planes, even):
    line = iota(planes[0][0].shape, 0)
    out_even, out_odd = None, None
    for j, (up, down) in enumerate(planes):
        up = pltpu.roll(up, j, 0) if j else up
        down = pltpu.roll(down, (j + 1) % SUB, 0) if (j + 1) % SUB else down
        one, two = jnp.where(even, down, up), jnp.where(even, up, down)
        out_even = one if j == 0 else jnp.where(line >= j, one, out_even)
        out_odd = two if j == 0 else jnp.where(line >= j, two, out_odd)
    even_ref[q] = out_even
    odd_ref[q] = out_odd


def row_planes(layers):
    return [kind * layers + k for kind in (0, 1, 5, 2, 4) for k in range(layers)]


def pack_rows(first_ref, from_odd, from_even, near, even_in, odd_in, edge_ref, even_ref, odd_ref):
    rows, half = first_ref.shape[0], LANE // 2
    base = near.shape[0] - 3
    layers = base // 6
    even = lax.axis_index("by") % 2 == 0
    lane = iota((rows, LANE), 1)
    a, b = from_even[:rows, :], from_odd[:rows, :]
    left, right = jnp.where(even, b, a), jnp.where(even, a, b)
    me = lax.axis_index("by")
    left = jnp.where(me == 0, 0.0, left)
    right = jnp.where(me == lax.axis_size("by") - 1, 0.0, right)
    left = jnp.where(lane < half, left, pltpu.roll(first_ref[...], half, 1))
    edge_ref[:, :LANE] = left
    edge_ref[:, LANE:] = right
    head, tail = edge_ref[:SUB, :], edge_ref[rows - SUB :, :]
    line = iota(head.shape, 0)
    depth = near[base + 2]
    stars = stars_of(
        lambda kind, k: near[kind * layers + k],
        [near[base], near[base + 1]],
        depth,
        jnp.where(line < SUB // 2, head, tail),
        layers,
        True,
    )
    _, _, forcing = solve_columns(stars, depth, layers)
    even = lax.axis_index("bx") % 2 == 0
    both = stars[0] + stars[1]
    for q in range(len(both) // SUB):
        put_rows(even_ref, odd_ref, q, [(p, p) for p in both[q * SUB : (q + 1) * SUB]], even)
    up = jnp.where(line < 1, depth, jnp.where(line < 2, pltpu.roll(head, 1, 0), pltpu.roll(forcing, 1, 0)))
    down = jnp.where(line < 2, pltpu.roll(tail, 2, 0), pltpu.roll(forcing, 5, 0))
    down = jnp.where(line < 1, pltpu.roll(depth, 1, 0), down)
    q = len(both) // SUB
    even_ref[q] = jnp.where(even, down, up)
    odd_ref[q] = jnp.where(even, up, down)


def edge_cells(edge, layers):
    rows = edge.shape[0]
    cells = 2 * layers
    level = (iota((rows, LANE), 1) % layers).astype(jnp.float32)
    left, right = edge[:, :LANE], edge[:, LANE:]
    wet_left = level < left_by(left, 3 * cells)
    wet_own = level < left_by(left, LANE // 2 + 3 * cells)
    wet_right = level < left_by(right, 3 * cells)
    cell_left = jnp.where(wet_left, left, 0.0)
    cell_own = jnp.where(wet_own, left_by(left, LANE // 2), 0.0)
    cell_right = jnp.where(wet_right, right, 0.0)
    return cell_left, cell_own, cell_right, wet_left & wet_own


def column_shifts(shape):
    lane = iota(shape, 1)
    first, last = lane == 0, lane == shape[1] - 1

    def after(x, fill):
        return jnp.where(last, fill, left_by(x, 1))

    def before(x, fill):
        return jnp.where(first, fill, pltpu.roll(x, 1, 1))

    return after, before


def stars_of(get, source, depth, edge, layers, open_ends):
    cells = 2 * layers
    after, before = column_shifts(depth.shape)

    def under(x):
        y = below(x)
        return jnp.where(iota(x.shape, 0) == x.shape[0] - 1, 0.0, y) if open_ends else y

    def over(x):
        y = above(x)
        return jnp.where(iota(x.shape, 0) == 0, 0.0, y) if open_ends else y

    left, right = edge[:, :LANE], edge[:, LANE:]
    cell_left, cell_own, cell_right, wet_both = edge_cells(edge, layers)
    slope_left = under(cell_left) - over(cell_left)
    slope_own = under(cell_own) - over(cell_own)
    slope_right = under(cell_right) - over(cell_right)
    flux_left = left_by(left, cells) * 0.5 * (cell_left + cell_own) - 0.15 * (
        cell_own - cell_left + left_by(left, 2 * cells) * 0.25 * (slope_left + slope_own)
    )
    flux_left = jnp.where(wet_both, flux_left, 0.0)
    depth_right = right[:, 3 * cells : 3 * cells + 1]
    depth_east = jnp.minimum(depth, under(depth))
    depth_north = jnp.minimum(depth, after(depth, depth_right))
    stars = ([], [])
    for k in range(layers):
        wet = depth > k
        mask = depth_east > k
        half = 0.5 * get(2, k)
        e_here = jnp.where(mask, half + 0.15, 0.0)
        e_next = jnp.where(mask, half - 0.15, 0.0)
        e_cross = jnp.where(mask, 0.0375 * get(4, k), 0.0)
        mask = depth_north > k
        half = 0.5 * get(3, k)
        n_here = jnp.where(mask, half + 0.15, 0.0)
        n_next = jnp.where(mask, half - 0.15, 0.0)
        n_cross = jnp.where(mask, 0.0375 * get(5, k), 0.0)
        for t in range(2):
            one = slice(t * layers + k, t * layers + k + 1)
            cell = jnp.where(wet, get(t, k), 0.0)
            east, west = under(cell), over(cell)
            north = after(cell, cell_right[:, one])
            south = before(cell, cell_left[:, one])
            cross = north - south
            flux = e_here * cell + e_next * east - e_cross * (cross + below(cross))
            star = cell - (flux - above(flux))
            cross = east - west
            cross = cross + after(cross, slope_right[:, one])
            flux = n_here * cell + n_next * north - n_cross * cross
            star = star - (flux - before(flux, flux_left[:, one]))
            if k == 0:
                star = star + source[t]
            stars[t].append(jnp.where(wet, star, 0.0))
    return stars


def joined_stars(part, cells_of, east_speed, east_slope, north_slope, depth, edge, upper, layers):
    cells = 2 * layers
    after, before = column_shifts(depth.shape)
    is_upper = upper(depth.shape)
    pack_upper = upper((depth.shape[0], LANE))

    def other(x, mine):
        return jnp.where(mine, below(x), above(x))

    left, right = edge[:, :LANE], edge[:, LANE:]
    cell_left, cell_own, cell_right, wet_both = edge_cells(edge, layers)
    cross_left = 0.0375 * left_by(left, 2 * cells)
    cross_left = cross_left * (other(cell_left, pack_upper) + other(cell_own, pack_upper))
    cross_left = jnp.where(wet_both, cross_left, 0.0)
    other_right = other(cell_right, pack_upper)
    depth_east = jnp.minimum(depth, below(depth))
    depth_north = jnp.minimum(depth, after(depth, right[:, 3 * cells : 3 * cells + 1]))
    stars = ([], [])
    for k in range(layers):
        wet = depth > k
        mask = depth_east > k
        half = 0.5 * east_speed[k]
        e_here = jnp.where(mask, half + 0.15, 0.0)
        e_next = jnp.where(mask, half - 0.15, 0.0)
        e_cross = jnp.where(mask, 0.0375 * east_slope[k], 0.0)
        n_cross = jnp.where(depth_north > k, 0.0375 * north_slope[k], 0.0)
        for t in range(2):
            one = slice(t * layers + k, t * layers + k + 1)
            cell = jnp.where(wet, cells_of[t][k], 0.0)
            east = below(cell)
            cross = after(cell, cell_right[:, one]) - before(cell, cell_left[:, one])
            flux = e_here * cell + e_next * east - e_cross * (cross + below(cross))
            beyond = jnp.where(is_upper, east, above(cell))
            cross = n_cross * (beyond + after(beyond, other_right[:, one]))
            cross = cross - before(cross, cross_left[:, one])
            gain = jnp.where(is_upper, cross - flux, above(flux) - cross)
            stars[t].append(jnp.where(wet, part[t][k] + gain, 0.0))
    return stars


def solve_columns(stars, depth, layers):
    primes, rights = [], ([], [])
    upper = None
    density = 0.8 * stars[1][0] - 0.2 * stars[0][0]
    for k in range(layers):
        if k + 1 < layers:
            deeper = 0.8 * stars[1][k + 1] - 0.2 * stars[0][k + 1]
            couple = 0.05 + 1.0 / (1.0 + 10.0 * jnp.maximum(deeper - density, 0.0))
            couple = jnp.where(depth > k + 1, couple, 0.0)
            density = deeper
        else:
            couple = None
        if k == 0:
            inverse = 1.0 / (1.0 + couple)
        elif couple is not None:
            inverse = 1.0 / (1.0 + upper + couple - upper * primes[-1])
        else:
            inverse = 1.0 / (1.0 + upper - upper * primes[-1])
        for t in range(2):
            value = stars[t][k]
            if k:
                value = value + upper * rights[t][-1]
            rights[t].append(value * inverse)
        if couple is not None:
            primes.append(couple * inverse)
        upper = couple
    fresh = ([None] * layers, [None] * layers)
    forcing = None
    solved = [rights[0][-1], rights[1][-1]]
    for k in range(layers - 1, -1, -1):
        wet = depth > k
        for t in range(2):
            if k < layers - 1:
                solved[t] = rights[t][k] + primes[k] * solved[t]
            fresh[t][k] = jnp.where(wet, solved[t], 0.0)
        part = 0.8 * fresh[1][k] - 0.2 * fresh[0][k]
        forcing = part if forcing is None else forcing + part
    return fresh[0], fresh[1], forcing * (4.0 / math.sqrt(layers))


def inner_tile(t, s, u, v, x, y, source, depth, edge, t_out, s_out, f_out):
    layers = t.shape[0]
    refs = (t, s, u, v, x, y)
    levels = depth[...].astype(jnp.float32)
    stars = stars_of(
        lambda kind, k: refs[kind][k], [source[0], source[1]], levels, edge[...], layers, False
    )
    warm, salt, forcing = solve_columns(stars, levels, layers)
    for k in range(layers):
        t_out[k] = warm[k]
        s_out[k] = salt[k]
    f_out[...] = forcing


def rim_rows(across, even_out, odd_out, even_in, odd_in, f_old, *refs):
    layers = refs[0].shape[0]
    t_fix, s_fix = refs[:2]
    sends, (field, blocks) = refs[2 : 2 + across], refs[2 + across :]
    rows = f_old.shape[0]
    strip = rows // across
    even = lax.axis_index("bx") % 2 == 0
    me = lax.axis_index("by")
    shape = (SUB, f_old.shape[1])
    line = iota(shape, 0)

    def parts(q):
        sent_even, sent_odd, came_even, came_odd = even_out[q], odd_out[q], even_in[q], odd_in[q]
        four = [jnp.where(even, came_odd, came_even), jnp.where(even, sent_odd, sent_even)]
        return four + [jnp.where(even, sent_even, sent_odd), jnp.where(even, came_even, came_odd)]

    def take(four, at):
        total = None
        for i, (part, place) in enumerate(zip(four, (1, 2, 5, 6))):
            part = part if place == at else pltpu.roll(part, (place - at) % SUB, 0)
            total = part if i == 0 else jnp.where(line >= 2 * i, part, total)
        return total

    def rows_from(q, count):
        out = []
        for i in range(count):
            if i % SUB == 0:
                four = parts(q + i // SUB)
            out.append(take(four, i % SUB))
        return out

    ahead = 2 * layers // SUB
    part = rows_from(0, 2 * layers)
    planes = rows_from(ahead + 1, 5 * layers)
    four = parts(ahead)
    me_along = lax.axis_index("bx")
    four[0] = jnp.where(me_along == 0, 0.0, four[0])
    four[3] = jnp.where(me_along == lax.axis_size("bx") - 1, 0.0, four[3])
    depth, edge = take(four, 0), take(four, 1)
    over, under = pltpu.roll(four[0], 3, 0), pltpu.roll(four[3], 7, 0)
    kinds = [planes[i * layers : (i + 1) * layers] for i in range(5)]

    def upper(shape):
        row = iota(shape, 0)
        return (row == 1) | (row == 5)

    stars = joined_stars(
        (part[:layers], part[layers:]),
        (kinds[0], kinds[1]),
        kinds[3],
        kinds[4],
        kinds[2],
        depth,
        edge,
        upper,
        layers,
    )
    warm, salt, forcing = solve_columns(stars, depth, layers)
    for fix, fresh in ((t_fix, warm), (s_fix, salt)):
        for k in range(layers):
            fix[k] = jnp.where(line == 0, pltpu.roll(fresh[k], 6, 0), pltpu.roll(fresh[k], 2, 0))
    top, bottom = pltpu.roll(forcing, 6, 0), pltpu.roll(forcing, 2, 0)
    last = SUB - 1
    field[:SUB, :] = jnp.where(line == last, top, over)
    field[SUB : 2 * SUB, :] = jnp.where(line == 0, top, f_old[:SUB, :])
    field[2 * SUB : rows, :] = f_old[SUB : rows - SUB, :]
    field[rows : rows + SUB, :] = jnp.where(line == last, bottom, f_old[rows - SUB :, :])
    field[SUB + rows : 2 * SUB + rows, :] = jnp.where(line == 0, bottom, under)
    later = ahead + 1 + 5 * layers // SUB
    extra = even_out.shape[0] - later
    tall = blocks.shape[1]
    for peer in range(across):
        start = SUB - ITERS + peer * strip
        stop = min(start + tall, field.shape[0])
        blocks[peer, : stop - start, :] = field[start:stop, :]
    for hop in range(across):
        sends[hop][:tall, :] = blocks[hop_peer(me, hop, across)]
    use_even = even == (me == 0)
    for q in range(extra):
        relay = jnp.where(use_even, even_in[later + q], odd_in[later + q])
        for hop in relaying(across):
            sends[hop][tall + q * SUB : tall + (q + 1) * SUB, :] = relay


def main_rows(from_even, from_odd, main_own, out):
    strip, columns = main_own.shape
    wide = ITERS - 1
    out[...] = jnp.zeros(out.shape, jnp.float32)
    out[ITERS : ITERS + strip, :] = main_own[...]
    over, under = ITERS - wide, ITERS + strip
    even = lax.axis_index("by") % 2 == 0
    parts = columns // LANE
    begin = from_even.shape[0] - wide * parts
    for j in range(parts):
        here = slice(j * LANE, (j + 1) * LANE)
        at = begin + j * wide
        a, b = from_even[at : at + wide, :], from_odd[at : at + wide, :]
        out[over : over + wide, here] = jnp.where(even, b, a)
        out[under : under + wide, here] = jnp.where(even, a, b)


def flush(fix_t, fix_s, t_mid, s_mid, t_out, s_out, ends, sems):
    layers, rows, columns = t_mid.shape
    inner = pl.ds(SUB, rows - 2 * SUB)
    copies = []

    def begin(source, target):
        copies.append(pltpu.make_async_copy(source, target, sems.at[len(copies)]))
        copies[-1].start()

    for mid, out in ((t_mid, t_out), (s_mid, s_out)):
        for low in range(0, layers, 2):
            some = pl.ds(low, 2)
            begin(mid.at[some, inner], out.at[some, inner])
    line = iota((layers, SUB, columns), 1)
    for i, (mid, fix, out) in enumerate(((t_mid, fix_t, t_out), (s_mid, fix_s, s_out))):
        for j, (start, at) in enumerate(((0, 0), (rows - SUB, SUB - 1))):
            old = mid[:, start : start + SUB, :]
            ends[2 * i + j] = jnp.where(line == at, fix[...], old)
            begin(ends.at[2 * i + j], out.at[:, pl.ds(start, SUB)])
    for copy in copies:
        copy.wait()


def hop_peer(me, hop, count):
    if count & (count - 1) == 0:
        return me ^ hop
    return (me + hop) % count


def relaying(count):
    return [h for h in range(count) if hop_peer(0, h, count) == count - 1 or hop_peer(count - 1, h, count) == 0]


def hop_origin(me, hop, count):
    if count & (count - 1) == 0:
        return me ^ hop
    return (me + count - hop) % count


def powers(across, along, *refs):
    came = [refs[0], *refs[1:across][::-1]]
    main_in, basis_ref, row_ref, field, main = refs[across:]
    tall, columns = main_in.shape
    strip = basis_ref.shape[1]
    width = columns // across
    me = lax.axis_index("by")
    for hop in range(across):
        origin = hop_origin(me, hop, across)
        field[:, pl.ds(pl.multiple_of(origin * width, LANE), width)] = came[hop][:tall, :]
    wide = ITERS - 1
    main[...] = main_in[...]

    def relayed(start, mine, sender):
        hop = [h for h in range(across) if hop_origin(mine, h, across) == sender][0]

        @pl.when(me == mine)
        def _():
            for j in range(across):
                at = tall + j * wide
                here = slice(j * width, (j + 1) * width)
                main[start : start + wide, here] = came[hop][at : at + wide, :]

    relayed(ITERS - wide, 0, across - 1)
    relayed(ITERS + strip, across - 1, 0)
    shape = (tall, columns)
    lane = iota(shape, 1)
    line = (lax.axis_index("bx") * across + me) * strip - ITERS + iota(shape, 0)
    inside = (line >= 0) & (line < along * across * strip)
    first, last = lane == 0, lane == columns - 1
    centre = (main[...] + (6.0 - CENTRE)) * (1.0 / SCALE)
    centre = jnp.where(inside, centre, 0.0)
    share = jnp.where(inside, -1.0 / SCALE, 0.0)
    now = field[...]
    own = [now[ITERS : ITERS + strip]]
    for _ in range(ITERS):
        beside = below(now) + above(now)
        spread = now + 0.5 * beside
        east = jnp.where(last, 0.0, left_by(spread, 1))
        west = jnp.where(first, 0.0, pltpu.roll(spread, 1, 1))
        now = centre * now + share * (beside + east + west)
        own.append(now[ITERS : ITERS + strip])
    for k in range(ITERS):
        basis_ref[k] = own[k]
    place = iota((1, LANE), 1)
    row = jnp.zeros((1, LANE), jnp.float32)
    for k, (i, j) in enumerate(PAIRS):
        part = own[i] * own[j]
        part = sum(part[:, c : c + LANE] for c in range(0, columns, LANE))
        part = jnp.sum(jnp.sum(part, axis=1, keepdims=True), axis=0, keepdims=True)
        row = jnp.where(place == k, part, row)
    row_ref[...] = jnp.broadcast_to(row[None], row_ref.shape)


def times(x, y):
    for a, b in ((x, y), (y, x)):
        if isinstance(a, float) and a in (0.0, 1.0):
            return b if a else 0.0
    return x * y


def plus(x, y):
    for a, b in ((x, y), (y, x)):
        if isinstance(a, float) and a == 0.0:
            return b
    return x + y


def coefficients(moments):
    def inner(a, b):
        total = 0.0
        for k in range(len(a) + len(b) - 1):
            part = 0.0
            for i in range(len(a)):
                if 0 <= k - i < len(b):
                    part = plus(part, times(a[i], b[k - i]))
            total = plus(total, times(part, moments[k]))
        return total

    resid, direction, total = [1.0], [1.0], [0.0] * ITERS
    norm_now = inner(resid, resid)
    for step in range(ITERS):
        image = [0.0] * (len(direction) + 1)
        for i, x in enumerate(direction):
            image[i] = plus(image[i], times(CENTRE, x))
            image[i + 1] = times(SCALE, x)
        bound = jnp.maximum(LEAST * norm_now, TINY)
        alpha = norm_now / jnp.maximum(inner(direction, image), bound)
        for i, x in enumerate(direction):
            total[i] = plus(total[i], times(alpha, x))
        if step + 1 < ITERS:
            resid = [plus(r, times(-alpha, q)) for r, q in zip(resid + [0.0], image)]
            norm_next = jnp.maximum(inner(resid, resid), 0.0)
            beta = norm_next / jnp.maximum(norm_now, TINY)
            direction = [plus(r, times(beta, p)) for r, p in zip(resid, direction + [0.0])]
            norm_now = norm_next
    return total


def combine(rows_ref, basis_ref, out_ref):
    moments = jnp.sum(rows_ref[...], axis=0)
    total = coefficients([moments[:, k : k + 1] for k in range(len(PAIRS))])
    out_ref[...] = total[0] * basis_ref[0] + total[1] * basis_ref[1] + total[2] * basis_ref[2]


def shape_of(*dims):
    return jax.ShapeDtypeStruct(dims, jnp.float32)


def whole(x):
    return pl.BlockSpec(x.shape, lambda *_: (0,) * len(x.shape))


def block(shape, *index):
    return pl.BlockSpec(shape, lambda *_: index)


def swaps(count, start):
    both = [(i, i + 1) for i in range(start, count - 1, 2)]
    both += [(b, a) for a, b in both]
    return both, sorted(set(range(count)) - {a for a, _ in both})


def across_route(across, start):
    both, alone = swaps(across, start)
    return both + list(zip(alone, alone[::-1]))


def along_route(along, across, start):
    both, alone = swaps(along, start)
    route = [(a * across + i, b * across + i) for a, b in both for i in range(across)]
    side = dict(across_route(across, 0))
    return route + [(a * across + i, a * across + side[i]) for a in alone for i in range(across)]


def local(t, s, u, v, x, y, source, depth, main):
    layers, rows, columns = t.shape
    across, along = lax.axis_size("by"), lax.axis_size("bx")
    strip = rows // across
    names = ("bx", "by")
    params = pltpu.CompilerParams(vmem_limit_bytes=48 << 20)

    call = functools.partial(pl.pallas_call, compiler_params=params)

    hbm = pl.BlockSpec(memory_space=pltpu.HBM)
    wide = ITERS - 1
    pack = shape_of(rows, LANE)
    more = shape_of(rows + wide * (columns * across // LANE), LANE)
    first, even, odd = call(
        pack_edges,
        grid=(1,),
        in_specs=[hbm] * 6,
        out_specs=[whole(pack), whole(more), whole(more)],
        out_shape=[pack, more, more],
        scratch_shapes=[
            pltpu.VMEM((6, layers, rows, LANE), jnp.float32),
            pltpu.VMEM((2, rows, LANE), jnp.int32),
            pltpu.VMEM(main.shape, jnp.float32),
            pltpu.SemaphoreType.DMA((15,)),
        ],
    )(*(pltpu.with_memory_space_constraint(a, pltpu.HBM) for a in (t, s, v, y, depth, main)))
    from_even = lax.ppermute(even, "by", across_route(across, 0))
    from_odd = lax.ppermute(odd, "by", across_route(across, 1))

    fields = (t, s, u, v, x, y, source)
    extra = -(-wide * across // SUB)
    sides = shape_of(rows, 2 * LANE)
    near = shape_of(6 * layers + 3, SUB, columns)
    shared = 2 * layers // SUB + 1
    rim = shape_of(shared + 5 * layers // SUB + extra, SUB, columns)
    near, even, odd = call(
        functools.partial(gather_rows, across),
        grid=(1,),
        in_specs=[hbm] * 8 + [whole(main)],
        out_specs=[whole(near), whole(rim), whole(rim)],
        out_shape=[near, rim, rim],
        scratch_shapes=[
            pltpu.VMEM((6 * layers + 2, 2 * SUB, columns), jnp.float32),
            pltpu.VMEM((2 * SUB, columns), depth.dtype),
            pltpu.SemaphoreType.DMA((16,)),
        ],
    )(*(pltpu.with_memory_space_constraint(a, pltpu.HBM) for a in (*fields, depth)), main)

    plane = shape_of(rows, columns)
    args = (first, from_odd, from_even, near)
    tile = block((shared, SUB, columns), 0, 0, 0)
    edge, even, odd = call(
        pack_rows,
        grid=(1,),
        in_specs=[whole(a) for a in args] + [tile] * 2,
        out_specs=[whole(sides), tile, tile],
        out_shape=[sides, rim, rim],
        input_output_aliases={4: 1, 5: 2},
    )(*args, even, odd)
    odd_in = lax.ppermute(odd, names, along_route(along, across, 1))
    even_in = lax.ppermute(even, names, along_route(along, across, 0))

    cube = shape_of(layers, rows, columns)
    args = (*fields, depth, edge)
    warm, salt, forcing = call(
        inner_tile,
        grid=(1,),
        in_specs=[whole(a) for a in args],
        out_specs=[whole(cube), whole(cube), whole(plane)],
        out_shape=[cube, cube, plane],
    )(*args)

    tall = -(-(strip + 2 * ITERS) // SUB) * SUB
    parts = [shape_of(tall + extra * SUB * (hop in relaying(across)), columns) for hop in range(across)]
    fix = shape_of(layers, SUB, columns)
    fix_t, fix_s, *sends = call(
        functools.partial(rim_rows, across),
        grid=(1,),
        in_specs=[whole(rim)] * 4 + [whole(plane)],
        out_specs=[whole(fix)] * 2 + [whole(part) for part in parts],
        out_shape=[fix] * 2 + parts,
        scratch_shapes=[
            pltpu.VMEM((rows + 2 * SUB, columns), jnp.float32),
            pltpu.VMEM((across, tall, columns), jnp.float32),
        ],
    )(even, odd, even_in, odd_in, forcing)

    came = [sends[0]]
    for hop in range(1, across):
        route = [(i, hop_peer(i, hop, across)) for i in range(across)]
        came.append(lax.ppermute(sends[hop], "by", route))

    args = (fix_t, fix_s, warm, salt)
    warm, salt = call(
        flush,
        grid=(1,),
        in_specs=[whole(a) for a in args],
        out_specs=[hbm] * 2,
        out_shape=[cube] * 2,
        scratch_shapes=[
            pltpu.VMEM((4, layers, SUB, columns), jnp.float32),
            pltpu.SemaphoreType.DMA((layers + 4,)),
        ],
    )(*args)

    basis_shape = shape_of(ITERS, strip, columns * across)
    row_shape = shape_of(across * along, 1, LANE)
    ready = shape_of(tall, columns * across)
    args = (from_even, from_odd, main)
    ready = call(
        main_rows,
        grid=(1,),
        in_specs=[whole(a) for a in args],
        out_specs=whole(ready),
        out_shape=ready,
    )(*args)
    ready, warm, salt = lax.optimization_barrier((ready, warm, salt))
    args = (came[0], *came[:0:-1], ready)
    basis, row = call(
        functools.partial(powers, across, along),
        grid=(1,),
        in_specs=[whole(a) for a in args],
        out_specs=[whole(basis_shape), whole(row_shape)],
        out_shape=[basis_shape, row_shape],
        scratch_shapes=[pltpu.VMEM((tall, columns * across), jnp.float32)] * 2,
    )(*args)
    gathered = lax.all_to_all(row, names, 0, 0, tiled=True)
    result = shape_of(strip, columns * across)
    pressure = call(
        combine,
        grid=(1,),
        in_specs=[whole(gathered), whole(basis)],
        out_specs=whole(result),
        out_shape=result,
    )(gathered, basis)
    return warm, salt, pressure


def solution(mesh):
    tile = P(None, "bx", "by")
    rows = P(("bx", "by"), None)
    return jax.shard_map(
        local,
        mesh=mesh,
        in_specs=(tile,) * 7 + (P("bx", "by"), rows),
        out_specs=(tile, tile, rows),
        check_vma=False,
    )
```
